32 devices in a mesh: dp: 8 (over y, x, core), mp: 4 (over z).
Axes of the slice: x: 2, y: 2, z: 4, core: 2. Of those that a mesh axis runs over, the one named last changes fastest.
Arguments:
- hidden_in: bfloat16 [4096, 2048], P(('dp', 'mp')), may hold values from -6 to 6
- doc_lengths: int32 [16], replicated, may hold values from 1 to 2048, 4096 in all
- attn_norm: float32 [2048], replicated, may hold values from 0.5 to 1.5
- query_weight: bfloat16 [2048, 2048], P('dp', 'mp'), may hold values from -0.125 to 0.125
- key_weight: bfloat16 [2048, 1024], P('dp', 'mp'), may hold values from -0.125 to 0.125
- value_weight: bfloat16 [2048, 1024], P('dp', 'mp'), may hold values from -0.125 to 0.125
- query_gain: float32 [128], replicated, may hold values from 0.1 to 1.9
- key_gain: float32 [128], replicated, may hold values from 0.1 to 1.9
- output_weight: bfloat16 [2048, 2048], P('mp', 'dp'), may hold values from -0.375 to 0.375
- ffn_norm: float32 [2048], replicated, may hold values from 0.5 to 1.5
- gate_weight: bfloat16 [2048, 6144], P('dp', 'mp'), may hold values from -0.125 to 0.125
- up_weight: bfloat16 [2048, 6144], P('dp', 'mp'), may hold values from -0.125 to 0.125
- down_weight: bfloat16 [6144, 2048], P('mp', 'dp'), may hold values from -0.078125 to 0.078125
- grad_out: bfloat16 [4096, 2048], P(('dp', 'mp')), may hold values from -6 to 6
Outputs:
- result: bfloat16 [4096, 2048], P(('dp', 'mp'))
- grad_hidden: float32 [4096, 2048], P(('dp', 'mp'))
- grad_attn_norm: float32 [2048], replicated
- grad_query: float32 [2048, 2048], P('dp', 'mp')
- grad_key: float32 [2048, 1024], P('dp', 'mp')
- grad_value: float32 [2048, 1024], P('dp', 'mp')
- grad_query_gain: float32 [128], replicated
- grad_key_gain: float32 [128], replicated
- grad_output_weight: float32 [2048, 2048], P('mp', 'dp')
- grad_ffn_norm: float32 [2048], replicated
- grad_gate: float32 [2048, 6144], P('dp', 'mp')
- grad_up: float32 [2048, 6144], P('dp', 'mp')
- grad_down: float32 [6144, 2048], P('mp', 'dp')
The draws below stay inside these ranges and needn't reach their ends.
Inputs may be any that keep to these rules, and one draw needn't show every extreme that they name: `doc_lengths`: the lengths sum to 4096 and one document is exactly 2048 tokens long.
All inputs are finite; a program needn't handle non-finite values.
Results may differ from the reference program's by a relative error of at most 0.022.
Values may be sent and summed in bfloat16 or wider, within the bound.
No kernel may reach another device: no remote copies, remote signals or barrier semaphores. Data moves between devices by JAX's collectives and lax.ppermute only.
A program may use at most 192 MiB of HBM per device.

```python
import math
import jax
import jax.numpy as jnp
import numpy as np
from jax import lax

D = 2048
HEADS = 16
KV_HEADS = 8
HEAD_DIM = 128
FF = 6144
TOKENS = 4096
MOST = 2048
DOCS = 16


def block_levels(stream_key, shape, pieces, least, largest):
    gain, own = 1.0, jax.random.fold_in(stream_key, 6)
    for dim, shards_of in pieces:
        steps = jnp.exp(jax.random.uniform(jax.random.fold_in(own, dim), (shards_of,), jnp.float32, least / len(pieces), largest / len(pieces)))
        gain = gain * jnp.repeat(steps, shape[dim] // shards_of).reshape([-1 if axis == dim else 1 for axis in range(len(shape))])
    return gain


def split_up(amount, total, limit, slope):
    weights = [(1 << 20) // math.isqrt(rank ** slope) + 1 for rank in range(2, amount + 1)]
    rest, given = total - limit - (amount - 1), [1] * (amount - 1)
    while rest > 0:
        free = [i for i in range(amount - 1) if given[i] < limit]
        whole, left = sum([weights[i] for i in free]), rest
        for i in free:
            more = min(limit - given[i], max(1, left * weights[i] // whole), rest)
            given[i] = given[i] + more
            rest = rest - more
    return np.array([limit] + given)


def ragged(key, amount, total, limit, slope):
    if amount == 2:
        one = jax.random.randint(key, (), max(1, total - limit), min(limit, total - 1) + 1)
        return jnp.stack([one, total - one])
    tallies = jnp.asarray(split_up(amount, total, limit, slope), jnp.int32)
    couples = (amount - 1) // 2
    giver, taker = tallies[1:1 + 2 * couples:2], tallies[2:2 + 2 * couples:2]
    room = jnp.minimum(giver - 1, limit - taker)
    passed = jax.random.randint(jax.random.fold_in(key, 1), (couples,), 0, 1 << 20) % (room + 1)
    tallies = tallies.at[1:1 + 2 * couples:2].set(giver - passed).at[2:2 + 2 * couples:2].set(taker + passed)
    return tallies[jax.random.permutation(jax.random.fold_in(key, 2), amount)]


def centred(stream_key, extent, scale, bound, cuts=(), kind=jnp.bfloat16):
    values = scale * jax.random.normal(stream_key, extent, jnp.float32)
    if cuts:
        values = values * block_levels(stream_key, extent, cuts, -0.22, 0.18)
    return jnp.clip(values, -bound, bound).astype(kind)


def setup_inputs(seed: int = 0) -> dict:
    seeds = jax.random.split(jax.random.key(seed), 15)
    return {
        "hidden_in": centred(seeds[0], (TOKENS, D), 1.0, 6.0, ((0, 32),)),
        "doc_lengths": ragged(seeds[1], DOCS, TOKENS, MOST, 2).astype(jnp.int32),
        "attn_norm": jnp.clip(1.0 + 0.1 * jax.random.normal(seeds[2], (D,), jnp.float32), 0.5, 1.5),
        "query_weight": centred(seeds[3], (D, HEADS * HEAD_DIM), D ** -0.5, 0.125, ((0, 8), (1, 4))),
        "key_weight": centred(seeds[4], (D, KV_HEADS * HEAD_DIM), D ** -0.5, 0.125, ((0, 8), (1, 4))),
        "value_weight": centred(seeds[5], (D, KV_HEADS * HEAD_DIM), D ** -0.5, 0.125, ((0, 8), (1, 4))),
        "query_gain": jnp.clip(1.0 + 0.18 * jax.random.normal(seeds[6], (HEAD_DIM,), jnp.float32), 0.1, 1.9),
        "key_gain": jnp.clip(1.0 + 0.18 * jax.random.normal(seeds[7], (HEAD_DIM,), jnp.float32), 0.1, 1.9),
        "output_weight": centred(seeds[8], (HEADS * HEAD_DIM, D), (HEADS * HEAD_DIM // 8) ** -0.5, 0.375, ((0, 4), (1, 8))),
        "ffn_norm": jnp.clip(1.0 + 0.1 * jax.random.normal(seeds[9], (D,), jnp.float32), 0.5, 1.5),
        "gate_weight": centred(seeds[10], (D, FF), D ** -0.5, 0.125, ((0, 8), (1, 4))),
        "up_weight": centred(seeds[11], (D, FF), D ** -0.5, 0.125, ((0, 8), (1, 4))),
        "down_weight": centred(seeds[12], (FF, D), FF ** -0.5, 0.078125, ((0, 4), (1, 8))),
        "grad_out": centred(seeds[13], (TOKENS, D), 1.0, 6.0, ((0, 32),)),
    }


eps_norm = 1e-06
rope_base = 1000000.0
masked_value = -1e+30

@jax.custom_vjp
def low(v):
    return lax.optimization_barrier(v.astype(jnp.bfloat16)).astype(jnp.float32)

@jax.custom_vjp
def low_back(v):
    return v

def low_keep(v):
    return (low(v), None)

def low_pass(kept, grad):
    return (grad,)

def back_keep(v):
    return (v, None)

def back_low(kept, grad):
    return (low(grad),)
low.defvjp(low_keep, low_pass)
low_back.defvjp(back_keep, back_low)

def rms_scale(values):
    return lax.rsqrt(lax.optimization_barrier(jnp.mean(values * values, axis=-1, keepdims=True)) + eps_norm)

def rotate(values, cos_table, sin_table):
    half_dim = values.shape[-1] // 2
    first_half = values[..., :half_dim]
    second_half = values[..., half_dim:]
    return jnp.concatenate([first_half * cos_table - second_half * sin_table, second_half * cos_table + first_half * sin_table], axis=-1)

def matmul(left, right):
    return jnp.dot(left, right, precision=lax.Precision.HIGHEST, preferred_element_type=jnp.float32)

def reference(hidden_in, doc_lengths, attn_norm, query_weight, key_weight, value_weight, query_gain, key_gain, output_weight, ffn_norm, gate_weight, up_weight, down_weight, grad_out):
    doc_ends = jnp.cumsum(doc_lengths).astype(jnp.int32)
    token_index = jnp.arange(TOKENS, dtype=jnp.int32)
    before = doc_ends[None, :] <= token_index[:, None]
    doc_index = lax.optimization_barrier(jnp.sum(before.astype(jnp.int32), axis=1)).astype(jnp.int32)
    position = token_index - lax.optimization_barrier(jnp.sum(jnp.where(before, doc_lengths[None, :], 0), axis=1)).astype(jnp.int32)
    half_dim = HEAD_DIM // 2
    inverse = rope_base ** (-(2.0 * jnp.arange(half_dim, dtype=jnp.float32)) / HEAD_DIM)
    angles = position.astype(jnp.float32)[:, None] * inverse[None, :]
    cos_table = jnp.cos(angles)[:, None, :]
    sin_table = jnp.sin(angles)[:, None, :]
    repeat = HEADS // KV_HEADS
    score_scale = HEAD_DIM ** (-0.5)
    block_rows = min(512, TOKENS)
    pad_rows = MOST

    def attention(query_rot, key_rot, value_low):
        key_pad = jnp.concatenate([jnp.zeros((pad_rows, KV_HEADS, HEAD_DIM), jnp.float32), key_rot], axis=0)
        value_pad = jnp.concatenate([jnp.zeros((pad_rows, KV_HEADS, HEAD_DIM), jnp.float32), value_low], axis=0)
        doc_pad = jnp.concatenate([jnp.full((pad_rows,), -1, jnp.int32), doc_index], axis=0)

        def one_block(start):
            qblock = lax.dynamic_slice_in_dim(query_rot, start, block_rows, 0).reshape(block_rows, KV_HEADS, repeat, HEAD_DIM)
            kblock = lax.dynamic_slice_in_dim(key_pad, start, block_rows + pad_rows, 0)
            vblock = lax.dynamic_slice_in_dim(value_pad, start, block_rows + pad_rows, 0)
            query_docs = lax.dynamic_slice_in_dim(doc_index, start, block_rows, 0)
            key_docs = lax.dynamic_slice_in_dim(doc_pad, start, block_rows + pad_rows, 0)
            query_places = start + jnp.arange(block_rows, dtype=jnp.int32)
            key_places = start - pad_rows + jnp.arange(block_rows + pad_rows, dtype=jnp.int32)
            allowed = ((query_docs[:, None] == key_docs[None, :]) & (key_places[None, :] <= query_places[:, None]))[None, None]
            raw_scores = jnp.einsum('qkrd,skd->krqs', qblock, kblock, precision=lax.Precision.HIGHEST)
            scores = jnp.where(allowed, low_back(raw_scores) * score_scale, masked_value)
            highest = lax.optimization_barrier(jnp.max(scores, axis=-1, keepdims=True))
            exp_scores = jnp.exp(scores - highest)
            attn_probs = low(exp_scores / lax.optimization_barrier(jnp.sum(exp_scores, axis=-1, keepdims=True)))
            attended = jnp.einsum('krqs,skd->qkrd', attn_probs, vblock, precision=lax.Precision.HIGHEST)
            return attended.reshape(block_rows, HEADS * HEAD_DIM)
        starts = jnp.arange(TOKENS // block_rows, dtype=jnp.int32) * block_rows
        return lax.map(jax.checkpoint(one_block), starts).reshape(TOKENS, HEADS * HEAD_DIM)

    def forward(hidden, attn_gain, query_mat, key_mat, value_mat, query_gain_f, key_gain_f, out_mat, ffn_gain, gate_mat, up_mat, down_mat):
        normed_one = hidden * rms_scale(hidden)
        attn_input = low(normed_one * attn_gain)
        query_raw = low_back(matmul(attn_input, query_mat)).reshape(TOKENS, HEADS, HEAD_DIM)
        key_raw = low_back(matmul(attn_input, key_mat)).reshape(TOKENS, KV_HEADS, HEAD_DIM)
        value_low = low(low_back(matmul(attn_input, value_mat))).reshape(TOKENS, KV_HEADS, HEAD_DIM)
        query_rot = low(rotate(query_raw * rms_scale(query_raw) * query_gain_f, cos_table, sin_table))
        key_rot = low(rotate(key_raw * rms_scale(key_raw) * key_gain_f, cos_table, sin_table))
        attended = low(low_back(attention(query_rot, key_rot, value_low)))
        mixed_rows = hidden + low_back(matmul(attended, out_mat))
        normed_two = mixed_rows * rms_scale(mixed_rows)
        ffn_input = low(normed_two * ffn_gain)
        gate_pre = low_back(matmul(ffn_input, gate_mat))
        up_value = low_back(matmul(ffn_input, up_mat))
        hidden_act = low(gate_pre * jax.nn.sigmoid(gate_pre) * up_value)
        return mixed_rows + low_back(matmul(hidden_act, down_mat))
    result, pullback = jax.vjp(forward, hidden_in.astype(jnp.float32), attn_norm.astype(jnp.float32), query_weight.astype(jnp.float32), key_weight.astype(jnp.float32), value_weight.astype(jnp.float32), query_gain.astype(jnp.float32), key_gain.astype(jnp.float32), output_weight.astype(jnp.float32), ffn_norm.astype(jnp.float32), gate_weight.astype(jnp.float32), up_weight.astype(jnp.float32), down_weight.astype(jnp.float32))
    gradients = pullback(grad_out.astype(jnp.float32))
    return (result.astype(jnp.bfloat16), gradients[0], gradients[1], gradients[2], gradients[3], gradients[4], gradients[5], gradients[6], gradients[7], gradients[8], gradients[9], gradients[10], gradients[11])
```

```python
import functools

import jax
import jax.numpy as jnp
from jax import lax
from jax.experimental import pallas as pl
from jax.experimental.pallas import tpu as pltpu
from jax.sharding import PartitionSpec as P

eps_norm = 1e-06
rope_base = 1000000.0
log2_e = 1.4426950408889634
bf16 = jnp.bfloat16
f32 = jnp.float32


def rms_scale(values):
    return lax.rsqrt(jnp.mean(values * values, axis=-1, keepdims=True) + eps_norm)


def norm_back(grad_hat, normed, scale_rows):
    return scale_rows * (grad_hat - normed * jnp.mean(grad_hat * normed, axis=-1, keepdims=True))


def rotate(values, cos_table, sin_table):
    half_dim = values.shape[-1] // 2
    first_half = values[..., :half_dim]
    second_half = values[..., half_dim:]
    return jnp.concatenate(
        [
            first_half * cos_table - second_half * sin_table,
            second_half * cos_table + first_half * sin_table,
        ],
        axis=-1,
    )


def unrotate(gradient, cos_table, sin_table):
    half_dim = gradient.shape[-1] // 2
    first_half = gradient[..., :half_dim]
    second_half = gradient[..., half_dim:]
    return jnp.concatenate(
        [
            first_half * cos_table + second_half * sin_table,
            second_half * cos_table - first_half * sin_table,
        ],
        axis=-1,
    )


def mm(left, right):
    return jnp.dot(left, right, preferred_element_type=f32)


def mm_nt(left, right):
    return lax.dot_general(left, right, (((1,), (1,)), ((), ())), preferred_element_type=f32)


def mm_tn(left, right):
    return lax.dot_general(left, right, (((0,), (0,)), ((), ())), preferred_element_type=f32)


def pair_mask(kb, places_ref, base_ref, block, slot, tok, sub):
    start = places_ref[slot, 0:1, :]
    place = places_ref[slot, 1:2, :]
    pieces = []
    for piece in range(sub):
        base = base_ref[block * sub + piece]
        rows = lax.broadcasted_iota(jnp.int32, (tok, start.shape[1]), 0)
        pieces.append((rows >= start - base) & (rows <= place - base))
    return jnp.concatenate(pieces, axis=0)


def attn_fwd_kernel(flags_ref, base_ref, places_ref, q_ref, k_ref, v_ref, o_ref, lse_ref, acc_ref, sum_ref, *, tok, sub, slots, blocks, repeat):
    head_dim = k_ref.shape[1]
    kb = tok * sub
    acc_ref[...] = jnp.zeros_like(acc_ref)
    sum_ref[...] = jnp.zeros_like(sum_ref)

    def step(block, slot, vt, masked):
        rows = pl.ds(pl.multiple_of(slot * tok, tok), tok)
        q = jnp.concatenate([q_ref[rows, i * head_dim:(i + 1) * head_dim] for i in range(repeat)], axis=0)
        k = k_ref[pl.ds(pl.multiple_of(block * kb, kb), kb), :]
        p = jnp.exp2(mm_nt(k, q))
        if masked:
            p = jnp.where(pair_mask(kb, places_ref, base_ref, block, slot, tok, sub), p, 0.0)
        sum_ref[slot] += jnp.sum(p, axis=0, keepdims=True)
        acc_ref[slot] += mm(vt, p.astype(bf16))

    @pl.loop(0, blocks)
    def _(block):
        any_flag = flags_ref[0, block]
        for slot in range(1, slots):
            any_flag = any_flag + flags_ref[slot, block]

        @pl.when(any_flag > 0)
        def _():
            vt = v_ref[pl.ds(pl.multiple_of(block * kb, kb), kb), :].T

            @pl.loop(0, slots)
            def _(slot):
                flag = flags_ref[slot, block]

                @pl.when(flag == 1)
                def _():
                    step(block, slot, vt, True)

                @pl.when(flag == 2)
                def _():
                    step(block, slot, vt, False)

    @pl.loop(0, slots)
    def _(slot):
        total = sum_ref[slot]
        out = (acc_ref[slot] * (1.0 / total)).T
        rows = pl.ds(pl.multiple_of(slot * tok, tok), tok)
        for i in range(repeat):
            o_ref[rows, i * head_dim:(i + 1) * head_dim] = out[i * tok:(i + 1) * tok].astype(bf16)
        lse_ref[slot] = jnp.log2(total)


def attn_bwd_kernel(flags_ref, base_ref, places_ref, q_ref, k_ref, v_ref, lse_ref, o_ref, do_ref, dq_ref, dk_ref, dv_ref, dqt_ref, delta_ref, dka_ref, dva_ref, *, tok, sub, slots, blocks, repeat, dq_scale, dk_scale):
    head_dim = k_ref.shape[1]
    kb = tok * sub
    dqt_ref[...] = jnp.zeros_like(dqt_ref)

    def rows_of(ref, slot):
        rows = pl.ds(pl.multiple_of(slot * tok, tok), tok)
        return jnp.concatenate([ref[rows, i * head_dim:(i + 1) * head_dim] for i in range(repeat)], axis=0)

    @pl.loop(0, slots)
    def _(slot):
        prod = rows_of(do_ref, slot).astype(f32) * rows_of(o_ref, slot).astype(f32)
        delta_ref[slot] = jnp.sum(prod.T, axis=0, keepdims=True)

    def step(block, slot, k, v, kt, masked):
        q = rows_of(q_ref, slot)
        do = rows_of(do_ref, slot)
        p = jnp.exp2(mm_nt(k, q) - lse_ref[slot])
        if masked:
            p = jnp.where(pair_mask(kb, places_ref, base_ref, block, slot, tok, sub), p, 0.0)
        ds = (p * (mm_nt(v, do) - delta_ref[slot])).astype(bf16)
        dva_ref[...] += mm(p.astype(bf16), do)
        dka_ref[...] += mm(ds, q)
        dqt_ref[slot] += mm(kt, ds)

    @pl.loop(0, blocks)
    def _(block):
        any_flag = flags_ref[0, block]
        for slot in range(1, slots):
            any_flag = any_flag + flags_ref[slot, block]
        dka_ref[...] = jnp.zeros_like(dka_ref)
        dva_ref[...] = jnp.zeros_like(dva_ref)
        keys = pl.ds(pl.multiple_of(block * kb, kb), kb)

        @pl.when(any_flag > 0)
        def _():
            k = k_ref[keys, :]
            v = v_ref[keys, :]
            kt = k.T

            @pl.loop(0, slots)
            def _(slot):
                flag = flags_ref[slot, block]

                @pl.when(flag == 1)
                def _():
                    step(block, slot, k, v, kt, True)

                @pl.when(flag == 2)
                def _():
                    step(block, slot, k, v, kt, False)

        dk_ref[keys, :] = (dka_ref[...] * dk_scale).astype(bf16)
        dv_ref[keys, :] = dva_ref[...].astype(bf16)

    @pl.loop(0, slots)
    def _(slot):
        out = (dqt_ref[slot] * dq_scale).T
        rows = pl.ds(pl.multiple_of(slot * tok, tok), tok)
        for i in range(repeat):
            dq_ref[rows, i * head_dim:(i + 1) * head_dim] = out[i * tok:(i + 1) * tok]


def body(
    hidden_in,
    doc_lengths,
    attn_norm,
    query_weight,
    key_weight,
    value_weight,
    query_gain,
    key_gain,
    output_weight,
    ffn_norm,
    gate_weight,
    up_weight,
    down_weight,
    grad_out,
):
    dp_count = lax.axis_size("dp")
    mp_count = lax.axis_size("mp")
    slots = mp_count
    tok, width = hidden_in.shape
    group_rows = tok * mp_count
    head_dim = query_gain.shape[0]
    half_dim = head_dim // 2
    q_cols = query_weight.shape[1]
    k_cols = key_weight.shape[1]
    kv_local = k_cols // head_dim
    repeat = q_cols // k_cols
    ff = gate_weight.shape[1]
    group = lax.axis_index("dp")
    my_z = lax.axis_index("mp")
    score_scale = head_dim ** (-0.5)

    ring = [(i, (i + 1) % mp_count) for i in range(mp_count)]

    def shift(values):
        return lax.ppermute(values, "mp", ring)

    def swap(values, mask):
        return lax.ppermute(values, "dp", [(i, i ^ mask) for i in range(dp_count)])

    def ring_gather(values):
        held = [values]
        for _ in range(mp_count - 1):
            held.append(shift(held[-1]))
        return held

    def ring_scatter(parts):
        acc = parts[1].astype(bf16)
        for slot in range(2, mp_count):
            acc = (shift(acc).astype(f32) + parts[slot]).astype(bf16)
        return shift(acc).astype(f32) + parts[0]

    def split_slots(values):
        return [values[i * tok:(i + 1) * tok] for i in range(slots)]

    w_qkv = lax.all_gather(
        jnp.concatenate([query_weight, key_weight, value_weight], axis=1), "dp", axis=0, tiled=True
    )
    w_out = lax.all_gather(output_weight, "dp", axis=1, tiled=True)
    w_gu = lax.all_gather(
        jnp.concatenate([gate_weight, up_weight], axis=1), "dp", axis=0, tiled=True
    )
    w_down = lax.all_gather(down_weight, "dp", axis=1, tiled=True)

    doc_ends = jnp.cumsum(doc_lengths)
    slot_offset = ((my_z - jnp.arange(slots, dtype=jnp.int32)) % mp_count) * tok
    places = (
        group * group_rows
        + slot_offset[:, None]
        + jnp.arange(tok, dtype=jnp.int32)[None, :]
    )
    before = doc_ends[None, None, :] <= places[:, :, None]
    starts = jnp.sum(jnp.where(before, doc_lengths[None, None, :], 0), axis=-1)
    position = (places - starts).reshape(group_rows)
    inverse = rope_base ** (-(2.0 * jnp.arange(half_dim, dtype=f32)) / head_dim)
    angles = position.astype(f32)[:, None] * inverse[None, :]
    cos_table = jnp.cos(angles)[:, None, :]
    sin_table = jnp.sin(angles)[:, None, :]

    masks = list(range(0, dp_count, 2)) + list(range(1, dp_count, 2))
    sub = min(4, slots)
    key_base = (
        (group ^ jnp.array(masks, jnp.int32))[:, None] * group_rows + slot_offset[None, :]
    )
    blocks = dp_count * slots // sub
    key_base = key_base.reshape(blocks, sub)
    q_first, q_last = places[:, 0], places[:, -1]
    s_first, s_last = starts[:, 0], starts[:, -1]
    piece_lo, piece_hi = key_base[None], key_base[None] + tok - 1
    some = (piece_lo <= q_last[:, None, None]) & (s_first[:, None, None] <= piece_hi)
    every = (piece_hi <= q_first[:, None, None]) & (s_last[:, None, None] <= piece_lo)
    flags = jnp.where(jnp.all(every, -1), 2, jnp.any(some, -1).astype(jnp.int32)).astype(jnp.int32)
    key_base = key_base.reshape(-1)
    lane_places = jnp.tile(jnp.stack([starts, places], axis=1), (1, 1, repeat))

    hidden_slots = ring_gather(hidden_in)
    grad_slots = ring_gather(grad_out)
    normed_slots, attn_slots = [], []
    for values in hidden_slots:
        values = values.astype(f32)
        normed = values * rms_scale(values)
        normed_slots.append(normed)
        attn_slots.append((normed * attn_norm).astype(bf16))
    resid_in = hidden_in.astype(f32)
    scale_one = rms_scale(resid_in)
    normed_one = normed_slots[0]
    attn_input = jnp.concatenate(attn_slots, axis=0)
    kv_raw = mm(attn_input, w_qkv[:, q_cols:])
    key_raw = kv_raw[:, :k_cols].reshape(group_rows, kv_local, head_dim)
    value_low = kv_raw[:, k_cols:].astype(bf16)
    key_norm_scale = rms_scale(key_raw)
    key_hat = key_raw * key_norm_scale
    key_rot = rotate(key_hat * key_gain, cos_table, sin_table).astype(bf16).reshape(group_rows, k_cols)
    kv_own = jnp.concatenate([key_rot, value_low], axis=1)
    kv_even = [kv_own] + [swap(kv_own, mask) for mask in range(2, dp_count, 2)]
    kv_even = jnp.concatenate(kv_even, axis=0)
    kv_all = jnp.concatenate([kv_even, swap(kv_even, 1)], axis=0)

    query_raw = mm(attn_input, w_qkv[:, :q_cols]).reshape(group_rows, -1, head_dim)
    query_norm_scale = rms_scale(query_raw)
    query_hat = query_raw * query_norm_scale
    query_rot = (
        rotate(query_hat * query_gain, cos_table, sin_table) * (score_scale * log2_e)
    ).astype(bf16).reshape(group_rows, q_cols)

    keys_total = dp_count * group_rows
    head_rows = repeat * tok
    smem = pl.BlockSpec(memory_space=pltpu.SMEM)
    whole_places = pl.BlockSpec((slots, 2, head_rows), lambda h: (0, 0, 0))
    q_spec = pl.BlockSpec((group_rows, repeat * head_dim), lambda h: (0, h))
    k_spec = pl.BlockSpec((keys_total, head_dim), lambda h: (0, h))
    v_spec = pl.BlockSpec((keys_total, head_dim), lambda h: (0, kv_local + h))
    lse_spec = pl.BlockSpec((None, slots, 1, head_rows), lambda h: (h, 0, 0, 0))
    dims = dict(tok=tok, sub=sub, slots=slots, blocks=blocks, repeat=repeat)
    pair_flops = 2 * group_rows * (2048 + group_rows) * q_cols
    attended_low, lse = pl.pallas_call(
        functools.partial(attn_fwd_kernel, **dims),
        grid=(kv_local,),
        in_specs=[smem, smem, whole_places, q_spec, k_spec, v_spec],
        out_specs=[q_spec, lse_spec],
        out_shape=[
            jax.ShapeDtypeStruct((group_rows, q_cols), bf16),
            jax.ShapeDtypeStruct((kv_local, slots, 1, head_rows), f32),
        ],
        scratch_shapes=[
            pltpu.VMEM((slots, head_dim, head_rows), f32),
            pltpu.VMEM((slots, 1, head_rows), f32),
        ],
        cost_estimate=pl.CostEstimate(flops=2 * pair_flops, bytes_accessed=6 << 20, transcendentals=5 << 20),
        name="attn_fwd",
    )(flags, key_base, lane_places, query_rot, kv_all, kv_all)

    attn_parts = split_slots(mm(attended_low, w_out))
    mixed_rows = resid_in + ring_scatter(attn_parts)
    scale_two = rms_scale(mixed_rows)
    normed_two = mixed_rows * scale_two
    ffn_slots = ring_gather((normed_two * ffn_norm).astype(bf16))

    act_chunks, dgu_chunks, back_parts = [], [], []
    for first in range(0, slots, 2):
        ffn_input = jnp.concatenate(ffn_slots[first:first + 2], axis=0)
        grad_rows = jnp.concatenate(grad_slots[first:first + 2], axis=0)
        gu = mm(ffn_input, w_gu)
        gate_pre, up_value = gu[:, :ff], gu[:, ff:]
        sigmoid_gate = jax.nn.sigmoid(gate_pre)
        act_chunks.append((gate_pre * sigmoid_gate * up_value).astype(bf16))
        grad_act = mm_nt(grad_rows, w_down)
        grad_gate_pre = (
            grad_act * up_value * sigmoid_gate * (1.0 + gate_pre * (1.0 - sigmoid_gate))
        ).astype(bf16)
        grad_up_value = (grad_act * gate_pre * sigmoid_gate).astype(bf16)
        dgu = jnp.concatenate([grad_gate_pre, grad_up_value], axis=1)
        dgu_chunks.append(dgu)
        back_parts += [mm_nt(dgu, w_gu)[i * tok:(i + 1) * tok] for i in range(2)]
    grad_ffn_input = ring_scatter(back_parts)
    grad_ffn_norm = jnp.sum(grad_ffn_input * normed_two, axis=0)
    grad_mixed = grad_out.astype(f32) + norm_back(
        grad_ffn_input * ffn_norm, normed_two, scale_two
    )
    mid_slots = ring_gather(grad_mixed.astype(bf16))

    hidden_act = jnp.concatenate(act_chunks, axis=0)
    dgu_all = jnp.concatenate(dgu_chunks, axis=0)
    ffn_all = jnp.concatenate(ffn_slots, axis=0)
    grad_all = jnp.concatenate(grad_slots, axis=0)
    ffn_out = ring_scatter(split_slots(mm(hidden_act, w_down)))
    result = (mixed_rows + ffn_out).astype(bf16)
    grad_gu = lax.psum_scatter(
        mm_tn(ffn_all, dgu_all).astype(bf16), "dp", scatter_dimension=0, tiled=True
    )
    grad_down = lax.psum_scatter(
        mm_tn(hidden_act, grad_all).astype(bf16), "dp", scatter_dimension=1, tiled=True
    )

    grad_mid = jnp.concatenate(mid_slots, axis=0)
    grad_attended = mm_nt(grad_mid, w_out).astype(bf16)
    grad_output_weight = lax.psum_scatter(
        mm_tn(attended_low, grad_mid).astype(bf16), "dp", scatter_dimension=1, tiled=True
    )
    dq_rot, dk_all, dv_all = pl.pallas_call(
        functools.partial(
            attn_bwd_kernel, **dims, dq_scale=score_scale, dk_scale=1.0 / log2_e
        ),
        grid=(kv_local,),
        in_specs=[smem, smem, whole_places, q_spec, k_spec, v_spec, lse_spec, q_spec, q_spec],
        out_specs=[q_spec, k_spec, k_spec],
        out_shape=[
            jax.ShapeDtypeStruct((group_rows, q_cols), f32),
            jax.ShapeDtypeStruct((keys_total, k_cols), bf16),
            jax.ShapeDtypeStruct((keys_total, k_cols), bf16),
        ],
        scratch_shapes=[
            pltpu.VMEM((slots, head_dim, head_rows), f32),
            pltpu.VMEM((slots, 1, head_rows), f32),
            pltpu.VMEM((tok * sub, head_dim), f32),
            pltpu.VMEM((tok * sub, head_dim), f32),
        ],
        cost_estimate=pl.CostEstimate(flops=5 * pair_flops, bytes_accessed=12 << 20, transcendentals=5 << 20),
        name="attn_bwd",
    )(flags, key_base, lane_places, query_rot, kv_all, kv_all, lse, attended_low, grad_attended)

    half_rows = keys_total // 2

    def return_home(grads):
        column = (
            grads[:half_rows].astype(f32) + swap(grads[half_rows:], 1).astype(f32)
        ).astype(bf16)
        total = column[:group_rows].astype(f32)
        for mask in range(2, dp_count, 2):
            first = mask // 2 * group_rows
            total = total + swap(column[first:first + group_rows], mask).astype(f32)
        return total

    key_grad_rot = return_home(dk_all)
    value_grad = return_home(dv_all)
    key_grad_norm = unrotate(
        key_grad_rot.reshape(group_rows, kv_local, head_dim), cos_table, sin_table
    )
    key_gain_part = jnp.sum(key_grad_norm * key_hat, axis=(0, 1))
    grad_key_raw = norm_back(key_grad_norm * key_gain, key_hat, key_norm_scale)
    query_grad_norm = unrotate(
        dq_rot.reshape(group_rows, -1, head_dim), cos_table, sin_table
    )
    query_gain_part = jnp.sum(query_grad_norm * query_hat, axis=(0, 1))
    grad_query_raw = norm_back(query_grad_norm * query_gain, query_hat, query_norm_scale)
    dqkv = jnp.concatenate(
        [
            grad_query_raw.reshape(group_rows, -1).astype(bf16),
            grad_key_raw.reshape(group_rows, -1).astype(bf16),
            value_grad.astype(bf16),
        ],
        axis=1,
    )
    attn_back = split_slots(mm_nt(dqkv, w_qkv))
    attn_gain_part = sum(
        jnp.sum(part * normed, axis=0) for part, normed in zip(attn_back, normed_slots)
    )
    grad_attn_input = ring_scatter(attn_back)
    grad_hidden = grad_mixed + norm_back(grad_attn_input * attn_norm, normed_one, scale_one)
    grad_qkv = lax.psum_scatter(
        mm_tn(attn_input, dqkv).astype(bf16), "dp", scatter_dimension=0, tiled=True
    )

    small = jnp.concatenate([attn_gain_part, grad_ffn_norm, query_gain_part, key_gain_part])
    small = small.reshape(-1, head_dim)
    mask = 1
    while mask < dp_count:
        small = small + swap(small, mask)
        mask *= 2
    mask = 1
    while mask < mp_count:
        small = small + lax.ppermute(small, "mp", [(i, i ^ mask) for i in range(mp_count)])
        mask *= 2
    small = small.reshape(-1)
    grad_attn_norm = small[:width]
    grad_ffn_gain = small[width:2 * width]
    grad_query_gain = small[2 * width:2 * width + head_dim]
    grad_key_gain = small[2 * width + head_dim:]
    return (
        result,
        grad_hidden,
        grad_attn_norm,
        grad_qkv[:, :q_cols].astype(f32),
        grad_qkv[:, q_cols:q_cols + k_cols].astype(f32),
        grad_qkv[:, q_cols + k_cols:].astype(f32),
        grad_query_gain,
        grad_key_gain,
        grad_output_weight.astype(f32),
        grad_ffn_gain,
        grad_gu[:, :ff].astype(f32),
        grad_gu[:, ff:].astype(f32),
        grad_down.astype(f32),
    )


def solution(mesh):
    rows = P(("dp", "mp"), None)
    placed = (
        rows,
        P(),
        P(),
        P("dp", "mp"),
        P("dp", "mp"),
        P("dp", "mp"),
        P(),
        P(),
        P("mp", "dp"),
        P(),
        P("dp", "mp"),
        P("dp", "mp"),
        P("mp", "dp"),
        rows,
    )
    return jax.shard_map(
        body,
        mesh=mesh,
        in_specs=placed,
        out_specs=(
            rows,
            rows,
            P(),
            P("dp", "mp"),
            P("dp", "mp"),
            P("dp", "mp"),
            P(),
            P(),
            P("mp", "dp"),
            P(),
            P("dp", "mp"),
            P("dp", "mp"),
            P("mp", "dp"),
        ),
        check_vma=False,
    )
```

```python
import functools

import jax
import jax.numpy as jnp
from jax import lax
from jax.experimental import pallas as pl
from jax.experimental.pallas import tpu as pltpu
from jax.sharding import PartitionSpec as P

eps_norm = 1e-06
rope_base = 1000000.0
log2_e = 1.4426950408889634
bf16 = jnp.bfloat16
f32 = jnp.float32
longest = 2048
light_cost = pl.CostEstimate(flops=1 << 20, bytes_accessed=1 << 16, transcendentals=0)


def rms_scale(values):
    return lax.rsqrt(jnp.mean(values * values, axis=-1, keepdims=True) + eps_norm)


def norm_back(grad_hat, normed, scale_rows):
    return scale_rows * (grad_hat - normed * jnp.mean(grad_hat * normed, axis=-1, keepdims=True))


def mm(left, right):
    return jnp.dot(left, right, preferred_element_type=f32)


def mm_nt(left, right):
    return lax.dot_general(left, right, (((1,), (1,)), ((), ())), preferred_element_type=f32)


def mm_tn(left, right):
    return lax.dot_general(left, right, (((0,), (0,)), ((), ())), preferred_element_type=f32)


def pair_mask(kb, places_ref, base_ref, block, slot, tok, sub):
    start = places_ref[slot, 0:1, :]
    place = places_ref[slot, 1:2, :]
    pieces = []
    for piece in range(sub):
        base = base_ref[block * sub + piece]
        rows = lax.broadcasted_iota(jnp.int32, (tok, start.shape[1]), 0)
        pieces.append((rows >= start - base) & (rows <= place - base))
    return jnp.concatenate(pieces, axis=0)


def load_pieces(refs, held_ref, sem_ref):
    rows = refs[0].shape[0]
    copies = [
        pltpu.make_async_copy(ref, held_ref.at[pl.ds(i * rows, rows), :], sem_ref.at[i])
        for i, ref in enumerate(refs)
    ]
    for copy in copies:
        copy.start()
    for copy in copies:
        copy.wait()


def attn_fwd_kernel(flags_ref, base_ref, places_ref, q_ref, *refs, tok, sub, slots, blocks, pieces, repeat, head_dim):
    kv_refs, (o_ref, lse_ref, kv_ref, acc_ref, sum_ref, sem_ref) = refs[:pieces], refs[pieces:]
    kb = tok * sub
    head = pl.program_id(0)
    k_lanes = pl.ds(pl.multiple_of(head * head_dim, head_dim), head_dim)
    v_lanes = pl.ds(pl.multiple_of((pl.num_programs(0) + head) * head_dim, head_dim), head_dim)

    @pl.when(head == 0)
    def _():
        load_pieces(kv_refs, kv_ref, sem_ref)

    acc_ref[...] = jnp.zeros_like(acc_ref)
    sum_ref[...] = jnp.zeros_like(sum_ref)

    def step(keys, block, pair, vt, masked):
        k = kv_ref[keys, k_lanes]
        for slot in [pair * 2, pair * 2 + 1]:
            rows = pl.ds(pl.multiple_of(slot * tok, tok), tok)
            q = jnp.concatenate([q_ref[rows, i * head_dim:(i + 1) * head_dim] for i in range(repeat)], axis=0)
            p = jnp.exp2(mm_nt(k, q))
            if masked:
                p = jnp.where(pair_mask(kb, places_ref, base_ref, block, slot, tok, sub), p, 0.0)
            sum_ref[slot] += jnp.sum(p, axis=0, keepdims=True)
            acc_ref[slot] += mm(vt, p.astype(bf16))

    @pl.loop(0, blocks)
    def _(block):
        any_flag = flags_ref[0, block]
        for pair in range(1, slots // 2):
            any_flag = any_flag + flags_ref[pair, block]
        keys = pl.ds(pl.multiple_of(block * kb, kb), kb)

        @pl.when(any_flag > 0)
        def _():
            vt = kv_ref[keys, v_lanes].T

            @pl.loop(0, slots // 2)
            def _(slot):
                flag = flags_ref[slot, block]

                @pl.when(flag == 1)
                def _():
                    step(keys, block, slot, vt, True)

                @pl.when(flag == 2)
                def _():
                    step(keys, block, slot, vt, False)

    @pl.loop(0, slots)
    def _(slot):
        total = sum_ref[slot]
        out = (acc_ref[slot] * (1.0 / total)).T
        rows = pl.ds(pl.multiple_of(slot * tok, tok), tok)
        for i in range(repeat):
            o_ref[rows, i * head_dim:(i + 1) * head_dim] = out[i * tok:(i + 1) * tok].astype(bf16)
        lse_ref[slot] = jnp.log2(total)


def attn_bwd_kernel(flags_ref, base_ref, places_ref, q_ref, lse_ref, o_ref, do_ref, *refs, tok, sub, slots, blocks, pieces, repeat, head_dim, dq_scale, dk_scale):
    kv_refs = refs[:pieces]
    dq_ref, near_ref, far_ref, kv_ref, dqt_ref, delta_ref, dka_ref, dva_ref, sem_ref = refs[pieces:]
    kb = tok * sub
    head = pl.program_id(0)
    k_lanes = pl.ds(pl.multiple_of(head * head_dim, head_dim), head_dim)
    v_lanes = pl.ds(pl.multiple_of((pl.num_programs(0) + head) * head_dim, head_dim), head_dim)

    @pl.when(head == 0)
    def _():
        load_pieces(kv_refs, kv_ref, sem_ref)

    dqt_ref[...] = jnp.zeros_like(dqt_ref)

    def rows_of(ref, slot):
        rows = pl.ds(pl.multiple_of(slot * tok, tok), tok)
        return jnp.concatenate([ref[rows, i * head_dim:(i + 1) * head_dim] for i in range(repeat)], axis=0)

    @pl.loop(0, slots)
    def _(slot):
        prod = rows_of(do_ref, slot).astype(f32) * rows_of(o_ref, slot).astype(f32)
        delta_ref[slot] = jnp.sum(prod.T, axis=0, keepdims=True)

    def step(block, pair, k, v, kt, masked):
        for slot in [pair * 2, pair * 2 + 1]:
            q = rows_of(q_ref, slot)
            do = rows_of(do_ref, slot)
            p = jnp.exp2(mm_nt(k, q) - lse_ref[slot])
            if masked:
                p = jnp.where(pair_mask(kb, places_ref, base_ref, block, slot, tok, sub), p, 0.0)
            ds = (p * (mm_nt(v, do) - delta_ref[slot])).astype(bf16)
            dva_ref[...] += mm(p.astype(bf16), do)
            dka_ref[...] += mm(ds, q)
            dqt_ref[slot] += mm(kt, ds)

    @pl.loop(0, blocks)
    def _(block):
        any_flag = flags_ref[0, block]
        for pair in range(1, slots // 2):
            any_flag = any_flag + flags_ref[pair, block]
        dka_ref[...] = jnp.zeros_like(dka_ref)
        dva_ref[...] = jnp.zeros_like(dva_ref)
        keys = pl.ds(pl.multiple_of(block * kb, kb), kb)

        @pl.when(any_flag > 0)
        def _():
            k = kv_ref[keys, k_lanes]
            v = kv_ref[keys, v_lanes]
            kt = k.T

            @pl.loop(0, slots // 2)
            def _(slot):
                flag = flags_ref[slot, block]

                @pl.when(flag == 1)
                def _():
                    step(block, slot, k, v, kt, True)

                @pl.when(flag == 2)
                def _():
                    step(block, slot, k, v, kt, False)

        @pl.when(block < blocks // 2)
        def _():
            near_ref[keys, k_lanes] = (dka_ref[...] * dk_scale).astype(bf16)
            near_ref[keys, v_lanes] = dva_ref[...].astype(bf16)

        @pl.when(block >= blocks // 2)
        def _():
            far = pl.ds(pl.multiple_of(block * kb - blocks // 2 * kb, kb), kb)
            far_ref[far, k_lanes] = (dka_ref[...] * dk_scale).astype(bf16)
            far_ref[far, v_lanes] = dva_ref[...].astype(bf16)

    @pl.loop(0, slots)
    def _(slot):
        out = (dqt_ref[slot] * dq_scale).T
        rows = pl.ds(pl.multiple_of(slot * tok, tok), tok)
        for i in range(repeat):
            dq_ref[rows, i * head_dim:(i + 1) * head_dim] = out[i * tok:(i + 1) * tok]


def turn(values):
    half = values.shape[-1] // 2
    return jnp.concatenate([values[:, half:], values[:, :half]], axis=1)


def project_kernel(x_ref, near_ref, far_ref, cos_ref, sin_ref, gain_ref, raw_ref, out_ref, *, head_dim, roped, scale):
    half = x_ref.shape[1] // 2
    raw = mm(x_ref[:, :half], near_ref[...]) + mm(x_ref[:, half:], far_ref[...])

    def rotated():
        raw_ref[...] = raw
        for first in range(0, raw.shape[1], head_dim):
            lanes = slice(first, first + head_dim)
            hat = raw[:, lanes] * rms_scale(raw[:, lanes])
            hat = hat * gain_ref[...]
            out_ref[:, lanes] = ((hat * cos_ref[...] + turn(hat) * sin_ref[...]) * scale).astype(bf16)

    if roped is None:
        rotated()
    else:
        pl.when(pl.program_id(0) < roped)(rotated)

        @pl.when(pl.program_id(0) >= roped)
        def _():
            out_ref[...] = raw.astype(bf16)


def project(x, w_near, w_far, cos_table, sin_table, gain, first, count, roped, tile, scale, name):
    tokens, width = x.shape
    head_dim = gain.shape[1]
    tables = pl.BlockSpec((tokens, head_dim), lambda j: (0, 0))
    weights = pl.BlockSpec((width // 2, tile), lambda j: (0, j + first))
    return pl.pallas_call(
        functools.partial(
            project_kernel, head_dim=head_dim, roped=None if roped == count else roped, scale=scale
        ),
        grid=(count,),
        in_specs=[
            pl.BlockSpec((tokens, width), lambda j: (0, 0)),
            weights,
            weights,
            tables,
            tables,
            pl.BlockSpec((1, head_dim), lambda j: (0, 0)),
        ],
        out_specs=[
            pl.BlockSpec((tokens, tile), lambda j: (0, jnp.minimum(j, roped - 1))),
            pl.BlockSpec((tokens, tile), lambda j: (0, j)),
        ],
        out_shape=[
            jax.ShapeDtypeStruct((tokens, roped * tile), f32),
            jax.ShapeDtypeStruct((tokens, count * tile), bf16),
        ],
        cost_estimate=light_cost,
        name=name,
    )(x, w_near, w_far, cos_table, sin_table, gain)


def unproject_kernel(raw_ref, cos_ref, sin_ref, gain_ref, *refs, head_dim, sums):
    grad_refs, (out_ref, part_ref) = refs[:sums], refs[sums:]
    part = jnp.zeros((1, head_dim), f32)
    for first in range(0, out_ref.shape[1], head_dim):
        lanes = slice(first, first + head_dim)
        grad = grad_refs[0][:, lanes].astype(f32)
        for grad_ref in grad_refs[1:]:
            grad = grad + grad_ref[:, lanes].astype(f32)
        if first < raw_ref.shape[1]:
            raw = raw_ref[:, lanes]
            scale = rms_scale(raw)
            hat = raw * scale
            grad = grad * cos_ref[...] - turn(grad) * sin_ref[...]
            part = part + jnp.sum(grad * hat, axis=0, keepdims=True)
            grad = norm_back(grad * gain_ref[...], hat, scale)
        out_ref[:, lanes] = grad.astype(bf16)
    part_ref[...] = part


def unproject(raw, cos_table, sin_table, gain, grads, name):
    tokens, cols = raw.shape[0], grads[0].shape[1]
    head_dim = gain.shape[1]

    def first_rows(width):
        return pl.BlockSpec((tokens, width), lambda j: (0, 0))

    gain_spec = pl.BlockSpec((1, head_dim), lambda j: (0, 0))
    return pl.pallas_call(
        functools.partial(unproject_kernel, head_dim=head_dim, sums=len(grads)),
        grid=(1,),
        in_specs=[first_rows(raw.shape[1]), first_rows(head_dim), first_rows(head_dim), gain_spec]
        + [first_rows(cols)] * len(grads),
        out_specs=[first_rows(cols), gain_spec],
        out_shape=[
            jax.ShapeDtypeStruct((tokens, cols), bf16),
            jax.ShapeDtypeStruct(gain.shape, f32),
        ],
        cost_estimate=light_cost,
        name=name,
    )(raw, cos_table, sin_table, gain, *grads)


def ffn_kernel(x0_ref, x1_ref, g0_ref, g1_ref, gate_ref, up_ref, down_ref, *refs, held):
    act_ref, grad_ref, x_ref, go_ref, back_ref = refs[held:]
    tile = pl.program_id(0)
    tok, size = x0_ref.shape[0], gate_ref.shape[1]
    ff = act_ref.shape[1]

    @pl.when(tile == 0)
    def _():
        x_ref[:tok] = x0_ref[...]
        x_ref[tok:] = x1_ref[...]
        go_ref[:tok] = g0_ref[...]
        go_ref[tok:] = g1_ref[...]
        back_ref[...] = jnp.zeros_like(back_ref)

    x = x_ref[...]
    gate_pre = mm(x, gate_ref[...])
    up_value = mm(x, up_ref[...])
    grad_act = mm_nt(go_ref[...], down_ref[...])
    sigmoid_gate = jax.nn.sigmoid(gate_pre)
    gated = gate_pre * sigmoid_gate
    grad_gate_pre = (
        grad_act * up_value * sigmoid_gate * (1.0 + gate_pre * (1.0 - sigmoid_gate))
    ).astype(bf16)
    grad_up_value = (grad_act * gated).astype(bf16)
    lanes = pl.ds(pl.multiple_of(tile * size, size), size)
    act_ref[:, lanes] = (gated * up_value).astype(bf16)
    grad_ref[:, lanes] = grad_gate_pre
    grad_ref[:, pl.ds(pl.multiple_of(ff + tile * size, size), size)] = grad_up_value
    back_ref[...] += mm_nt(grad_gate_pre, gate_ref[...]) + mm_nt(grad_up_value, up_ref[...])


def feed_forward(slot_pair, grad_pair, w_gu, w_down, held, chunk, chunks):
    tok, width = slot_pair[0].shape
    ff = w_down.shape[0]
    size = next(s for s in (512, 384, 256, 128) if ff % s == 0)
    tiles = ff // size
    slot_spec = pl.BlockSpec((tok, width), lambda t: (0, 0))

    def rows_spec(cols):
        return pl.BlockSpec((2 * tok, cols), lambda t: (chunk, 0))

    rows = 2 * tok * chunks
    return pl.pallas_call(
        functools.partial(ffn_kernel, held=len(held)),
        grid=(tiles,),
        in_specs=[slot_spec] * 4
        + [
            pl.BlockSpec((width, size), lambda t: (0, t)),
            pl.BlockSpec((width, size), lambda t: (0, tiles + t)),
            pl.BlockSpec((size, width), lambda t: (t, 0)),
        ]
        + [pl.BlockSpec(memory_space=pl.ANY)] * len(held),
        out_specs=[
            rows_spec(ff),
            rows_spec(2 * ff),
            rows_spec(width),
            rows_spec(width),
            pl.BlockSpec((2 * tok, width), lambda t: (0, 0)),
        ],
        out_shape=[
            jax.ShapeDtypeStruct((rows, ff), bf16),
            jax.ShapeDtypeStruct((rows, 2 * ff), bf16),
            jax.ShapeDtypeStruct((rows, width), bf16),
            jax.ShapeDtypeStruct((rows, width), bf16),
            jax.ShapeDtypeStruct((2 * tok, width), f32),
        ],
        input_output_aliases={7 + i: i for i in range(len(held))},
        cost_estimate=light_cost,
        name="feed_forward",
    )(*slot_pair, *grad_pair, w_gu, w_gu, w_down, *held)


def fold_kernel(near_ref, got_ref, *out_refs):
    rows = out_refs[0].shape[0]
    for i, out_ref in enumerate(out_refs):
        lines = slice((i + 1) * rows, (i + 2) * rows)
        out_ref[...] = (near_ref[lines].astype(f32) + got_ref[lines].astype(f32)).astype(bf16)


def fold_blocks(near, got, count):
    vmem = pl.BlockSpec(memory_space=pltpu.VMEM)
    shape = jax.ShapeDtypeStruct((near.shape[0] // count, near.shape[1]), bf16)
    return pl.pallas_call(
        fold_kernel,
        in_specs=[vmem, vmem],
        out_specs=[vmem] * (count - 1),
        out_shape=[shape] * (count - 1),
        cost_estimate=light_cost,
        name="fold_blocks",
    )(near, got)


def moved_kernel(table_ref, x_ref, o_ref, *, count):
    cols = x_ref.shape[1] // count
    for j in range(count):
        lanes = pl.ds(pl.multiple_of(table_ref[j] * cols, cols), cols)
        o_ref[:, j * cols:(j + 1) * cols] = x_ref[:, lanes]


def move_columns(values, table):
    vmem = pl.BlockSpec(memory_space=pltpu.VMEM)
    return pl.pallas_call(
        functools.partial(moved_kernel, count=table.shape[0]),
        in_specs=[pl.BlockSpec(memory_space=pltpu.SMEM), vmem],
        out_specs=vmem,
        out_shape=jax.ShapeDtypeStruct(values.shape, values.dtype),
        cost_estimate=light_cost,
        name="move_columns",
    )(table, values)


def weight_grad_kernel(table_ref, left_ref, right_ref, *refs, by_rows, adds, kind, piece):
    add_refs, out_refs, turned_ref = refs[:adds], refs[adds:-1], refs[-1]
    j = pl.program_id(0)
    if by_rows:
        turned_ref[...] = left_ref[...].T
    else:
        @pl.when(j == 0)
        def _():
            turned_ref[...] = left_ref[...].T

    def store(out_ref, done):
        if by_rows:
            for first in range(0, out_ref.shape[-1], piece):
                lanes = slice(done + first, done + first + piece)
                total = mm(turned_ref[...], right_ref[:, lanes])
                for add_ref in add_refs:
                    total = total + add_ref[:, lanes].astype(f32)
                out_ref[:, first:first + piece] = total.astype(out_ref.dtype)
        else:
            total = mm(turned_ref[...], right_ref[...])
            for add_ref in add_refs:
                total = total + add_ref[...].astype(f32)
            out_ref[...] = total.astype(out_ref.dtype)

    if kind == "apart":
        for k, out_ref in enumerate(out_refs):
            @pl.when(j == k)
            def _(out_ref=out_ref):
                store(out_ref, 0)
    else:
        done = 0
        for out_ref in out_refs:
            store(out_ref, done)
            done += out_ref.shape[-1]


def weight_grad(by_rows, parts, left, right, table, adds, kind, name, splits=None):
    tokens, count = left.shape[0], table.shape[0]
    rows = left.shape[1] // parts if by_rows else left.shape[1]
    cols = right.shape[1] if by_rows else right.shape[1] // parts
    splits = splits or (cols,)
    piece = min([512] + list(splits))
    if by_rows:
        left_spec = pl.BlockSpec((tokens, rows), lambda j, ids: (0, ids[j]))
        right_spec = pl.BlockSpec((tokens, cols), lambda j, ids: (0, 0))
    else:
        left_spec = pl.BlockSpec((tokens, rows), lambda j, ids: (0, 0))
        right_spec = pl.BlockSpec((tokens, cols), lambda j, ids: (0, ids[j]))
    add_arrays, add_specs = [], []
    for add in adds:
        if isinstance(add, tuple):
            array, first = add
            add_specs.append(pl.BlockSpec((None, rows, cols), lambda j, ids, first=first: (j + first, 0, 0)))
        else:
            array = add
            add_specs.append(pl.BlockSpec((rows, cols), lambda j, ids: (0, 0)))
        add_arrays.append(array)
    if kind == "stack":
        out_specs = [pl.BlockSpec((None, rows, cols), lambda j, ids: (j, 0, 0))]
        out_shape = [jax.ShapeDtypeStruct((count, rows, cols), bf16)]
    elif kind == "apart":
        out_specs = [pl.BlockSpec((rows, cols), lambda j, ids: (0, 0))] * count
        out_shape = [jax.ShapeDtypeStruct((rows, cols), bf16)] * count
    else:
        out_specs = [pl.BlockSpec((rows, part), lambda j, ids: (0, 0)) for part in splits]
        out_shape = [jax.ShapeDtypeStruct((rows, part), f32) for part in splits]
    return pl.pallas_call(
        functools.partial(weight_grad_kernel, by_rows=by_rows, adds=len(adds), kind=kind, piece=piece),
        grid_spec=pltpu.PrefetchScalarGridSpec(
            num_scalar_prefetch=1,
            grid=(count,),
            in_specs=[left_spec, right_spec] + add_specs,
            out_specs=out_specs,
            scratch_shapes=[pltpu.VMEM((rows, tokens), bf16)],
        ),
        out_shape=out_shape,
        cost_estimate=light_cost,
        name=name,
    )(table, left, right, *add_arrays)


def body(
    hidden_in,
    doc_lengths,
    attn_norm,
    query_weight,
    key_weight,
    value_weight,
    query_gain,
    key_gain,
    output_weight,
    ffn_norm,
    gate_weight,
    up_weight,
    down_weight,
    grad_out,
):
    dp_count = lax.axis_size("dp")
    mp_count = lax.axis_size("mp")
    slots = mp_count
    tok, width = hidden_in.shape
    group_rows = tok * mp_count
    head_dim = query_gain.shape[0]
    half_dim = head_dim // 2
    q_cols = query_weight.shape[1]
    k_cols = key_weight.shape[1]
    kv_local = k_cols // head_dim
    repeat = q_cols // k_cols
    ff = gate_weight.shape[1]
    group = lax.axis_index("dp")
    my_z = lax.axis_index("mp")
    score_scale = head_dim ** (-0.5)
    ring = [(i, (i + 1) % mp_count) for i in range(mp_count)]
    near_masks = list(range(0, dp_count, 2))
    masks = near_masks + [mask + 1 for mask in near_masks]
    far_masks = near_masks[1:]

    def tie(value, *others):
        return lax.optimization_barrier((value,) + others)[0]

    def shift(values):
        return lax.ppermute(values, "mp", ring)

    def swap(values, mask):
        return lax.ppermute(values, "dp", [(i, i ^ mask) for i in range(dp_count)])

    reach = (min(longest, group_rows * dp_count) - 2) // group_rows + 1

    def needs(reader, owner):
        first = reader // 2 * 2
        return owner <= first + 1 and owner >= first - reach

    def swap_forward(values, mask):
        pairs = [(i, i ^ mask) for i in range(dp_count) if needs(i ^ mask, i)]
        return lax.ppermute(values, "dp", pairs)

    def swap_back(values, mask):
        pairs = [(i, i ^ mask) for i in range(dp_count) if needs(i, i ^ mask)]
        return lax.ppermute(values, "dp", pairs)

    def ring_gather(values):
        held = [values]
        for _ in range(mp_count - 1):
            held.append(shift(held[-1]))
        return held

    def ring_scatter(parts):
        acc = parts[1].astype(bf16)
        for slot in range(2, mp_count):
            acc = (shift(acc).astype(f32) + parts[slot]).astype(bf16)
        return shift(acc).astype(f32) + parts[0]

    def split_slots(values):
        return [values[i * tok:(i + 1) * tok] for i in range(slots)]

    w_gu = lax.all_gather(
        jnp.concatenate([gate_weight, up_weight], axis=1), "dp", axis=0, tiled=True
    )
    w_down = lax.all_gather(down_weight, "dp", axis=1, tiled=True)

    w_own = jnp.concatenate([query_weight, key_weight, value_weight], axis=1)
    w_came = [swap(w_own, mask) for mask in far_masks]
    out_came_w = [swap(output_weight, mask) for mask in far_masks]
    ids = jnp.array(masks, jnp.int32)
    mask_blocks = group ^ ids
    true_ids = group ^ jnp.arange(dp_count, dtype=jnp.int32)
    true_blocks = true_ids // 2 + (true_ids % 2) * (dp_count // 2)

    doc_ends = jnp.cumsum(doc_lengths)
    slot_offset = ((my_z - jnp.arange(slots, dtype=jnp.int32)) % mp_count) * tok
    places = (
        group * group_rows
        + slot_offset[:, None]
        + jnp.arange(tok, dtype=jnp.int32)[None, :]
    )
    before = doc_ends[None, None, :] <= places[:, :, None]
    starts = jnp.sum(jnp.where(before, doc_lengths[None, None, :], 0), axis=-1)
    position = (places - starts).reshape(group_rows)
    inverse = rope_base ** (-(2.0 * jnp.arange(half_dim, dtype=f32)) / head_dim)
    angles = position.astype(f32)[:, None] * inverse[None, :]
    cos_table, sin_table = jnp.cos(angles), jnp.sin(angles)
    cos_table = jnp.concatenate([cos_table, cos_table], axis=1)
    sin_table = jnp.concatenate([-sin_table, sin_table], axis=1)

    sub = min(4, slots)
    key_base = mask_blocks[:, None] * group_rows + slot_offset[None, :]
    blocks = dp_count * slots // sub
    key_base = key_base.reshape(blocks, sub)
    q_first, q_last = places[:, 0], places[:, -1]
    s_first, s_last = starts[:, 0], starts[:, -1]
    piece_lo, piece_hi = key_base[None], key_base[None] + tok - 1
    some = (piece_lo <= q_last[:, None, None]) & (s_first[:, None, None] <= piece_hi)
    every = (piece_hi <= q_first[:, None, None]) & (s_last[:, None, None] <= piece_lo)
    flags = jnp.where(jnp.all(every, -1), 2, jnp.any(some, -1).astype(jnp.int32)).astype(jnp.int32)
    by_pair = flags.reshape(slots // 2, 2, blocks)
    flags = jnp.where(jnp.all(by_pair == 2, axis=1), 2, jnp.any(by_pair > 0, axis=1).astype(jnp.int32))
    key_base = key_base.reshape(-1)
    lane_places = jnp.tile(jnp.stack([starts, places], axis=1), (1, 1, repeat))

    hidden_slots = ring_gather(move_columns(hidden_in, mask_blocks))
    attn_gain = move_columns(jnp.broadcast_to(attn_norm, (8, width)), mask_blocks)[:1]
    w_near = jnp.concatenate([w_own] + [tie(came, hidden_slots[-1]) for came in w_came], axis=0)
    w_far = swap(w_near, 1)
    normed_slots, attn_slots = [], []
    for values in hidden_slots:
        values = values.astype(f32)
        normed = values * rms_scale(values)
        normed_slots.append(normed)
        attn_slots.append((normed * attn_gain).astype(bf16))
    resid_in = hidden_in.astype(f32)
    scale_one = rms_scale(resid_in)
    normed_one = resid_in * scale_one
    attn_input = jnp.concatenate(attn_slots, axis=0)
    q_gain, k_gain = query_gain.reshape(1, head_dim), key_gain.reshape(1, head_dim)
    key_raw, kv_own = project(
        attn_input, w_near, w_far, cos_table, sin_table, k_gain, repeat, 2, 1, k_cols, 1.0, "project_kv"
    )
    grad_slots = [grad_out]
    kv_came = [swap_forward(kv_own, mask) for mask in far_masks]
    query_raw, query_rot = project(
        tie(attn_input, kv_own), w_near, w_far, cos_table, sin_table, q_gain, 0, repeat, repeat, k_cols,
        score_scale * log2_e, "project_q",
    )
    w_out = jnp.concatenate([output_weight] + [tie(came, query_rot) for came in out_came_w], axis=1)
    w_out = jnp.concatenate([w_out, swap(w_out, 1)], axis=1)
    kv_near = [kv_own] + [tie(came, query_rot) for came in kv_came]
    kv_pieces = kv_near + [swap(piece, 1) for piece in kv_near]
    grad_slots = ring_gather(tie(grad_out, kv_own))

    keys_total = dp_count * group_rows
    head_rows = repeat * tok
    smem = pl.BlockSpec(memory_space=pltpu.SMEM)
    any_spec = pl.BlockSpec(memory_space=pl.ANY)
    whole_places = pl.BlockSpec((slots, 2, head_rows), lambda h: (0, 0, 0))
    q_spec = pl.BlockSpec((group_rows, repeat * head_dim), lambda h: (0, h))
    lse_spec = pl.BlockSpec((None, slots, 1, head_rows), lambda h: (h, 0, 0, 0))
    dims = dict(
        tok=tok, sub=sub, slots=slots, blocks=blocks, pieces=dp_count, repeat=repeat, head_dim=head_dim
    )
    kv_scratch = pltpu.VMEM((keys_total, 2 * k_cols), bf16)
    attended_low, lse = pl.pallas_call(
        functools.partial(attn_fwd_kernel, **dims),
        grid=(kv_local,),
        in_specs=[smem, smem, whole_places, q_spec] + [any_spec] * dp_count,
        out_specs=[q_spec, lse_spec],
        out_shape=[
            jax.ShapeDtypeStruct((group_rows, q_cols), bf16),
            jax.ShapeDtypeStruct((kv_local, slots, 1, head_rows), f32),
        ],
        scratch_shapes=[
            kv_scratch,
            pltpu.VMEM((slots, head_dim, head_rows), f32),
            pltpu.VMEM((slots, 1, head_rows), f32),
            pltpu.SemaphoreType.DMA((dp_count,)),
        ],
        cost_estimate=light_cost,
        name="attn_fwd",
    )(flags, key_base, lane_places, query_rot, *kv_pieces)

    attn_parts = split_slots(mm(attended_low, w_out))
    attn_parts[1] = tie(attn_parts[1], grad_slots[-1])
    mixed_rows = resid_in + move_columns(ring_scatter(attn_parts), true_blocks)
    scale_two = rms_scale(mixed_rows)
    normed_two = mixed_rows * scale_two
    ffn_slots = [(normed_two * ffn_norm).astype(bf16)]
    ffn_slots.append(shift(ffn_slots[0]))
    held, back_parts = [], []
    for first in range(0, slots, 2):
        *held, back = feed_forward(
            ffn_slots[first:first + 2], grad_slots[first:first + 2], w_gu, w_down, held, first // 2, slots // 2
        )
        back_parts += [back[:tok], back[tok:]]
        if first + 2 < slots:
            ffn_slots.append(tie(shift(ffn_slots[-1]), back))
            ffn_slots.append(shift(ffn_slots[-1]))
    hidden_act, dgu_all, ffn_all, grad_all = held
    half = dp_count // 2
    blocks_far, blocks_sent, blocks_own = mask_blocks[half:], mask_blocks[1:half], mask_blocks[:1]

    came = shift(tie(back_parts[1].astype(bf16), ffn_slots[-1]))
    gu_part = mm_tn(ffn_all, tie(dgu_all, came)).astype(bf16)
    for slot in range(2, mp_count):
        acc = (came.astype(f32) + back_parts[slot]).astype(bf16)
        came = shift(acc)
        if slot == 2:
            came = tie(came, gu_part)
            down_part = mm_tn(tie(hidden_act, came), grad_all).astype(bf16)
        if slot == 3:
            came = tie(came, down_part)
    grad_ffn_input = came.astype(f32) + back_parts[0]
    grad_gu = lax.psum_scatter(gu_part, "dp", scatter_dimension=0, tiled=True)
    grad_down = lax.psum_scatter(down_part, "dp", scatter_dimension=1, tiled=True)
    grad_ffn_norm = jnp.sum(grad_ffn_input * normed_two, axis=0)
    grad_mixed = grad_out.astype(f32) + norm_back(
        grad_ffn_input * ffn_norm, normed_two, scale_two
    )
    ffn_parts = mm(tie(hidden_act, grad_mixed), w_down)
    mid_slots = [move_columns(grad_mixed.astype(bf16), mask_blocks)]
    for slot in range(1, mp_count):
        came = shift(mid_slots[-1])
        if slot == 1:
            came = tie(came, ffn_parts)
        mid_slots.append(came)

    grad_mid = jnp.concatenate(mid_slots, axis=0)
    grad_attended = mm_nt(grad_mid, w_out).astype(bf16)
    ffn_parts = split_slots(ffn_parts)
    result_first = tie(ffn_parts[1].astype(bf16), mid_slots[-1])
    result_came = [shift(result_first)]
    near_spec = pl.BlockSpec((keys_total // 2, 2 * k_cols), lambda h: (0, 0))
    near_shape = jax.ShapeDtypeStruct((keys_total // 2, 2 * k_cols), bf16)
    dq_rot, dkv_near, dkv_far = pl.pallas_call(
        functools.partial(
            attn_bwd_kernel, **dims, dq_scale=score_scale, dk_scale=1.0 / log2_e
        ),
        grid=(kv_local,),
        in_specs=[smem, smem, whole_places, q_spec, lse_spec, q_spec, q_spec] + [any_spec] * dp_count,
        out_specs=[q_spec, near_spec, near_spec],
        out_shape=[jax.ShapeDtypeStruct((group_rows, q_cols), f32), near_shape, near_shape],
        scratch_shapes=[
            kv_scratch,
            pltpu.VMEM((slots, head_dim, head_rows), f32),
            pltpu.VMEM((slots, 1, head_rows), f32),
            pltpu.VMEM((tok * sub, head_dim), f32),
            pltpu.VMEM((tok * sub, head_dim), f32),
            pltpu.SemaphoreType.DMA((dp_count,)),
        ],
        cost_estimate=light_cost,
        name="attn_bwd",
    )(flags, key_base, lane_places, query_rot, lse, attended_low, tie(grad_attended, result_first), *kv_pieces)

    dkv_got = swap(tie(dkv_far, result_came[0]), 1)
    result_next = (result_came[0].astype(f32) + ffn_parts[2]).astype(bf16)
    result_came.append(shift(result_next))
    dkv_sent = fold_blocks(dkv_near, dkv_got, half)
    dkv_came = [swap_back(sent, mask) for sent, mask in zip(dkv_sent, far_masks)]
    dq_raw, query_gain_part = unproject(
        query_raw, cos_table, sin_table, q_gain, [tie(dq_rot, *dkv_sent)], "unproject_q"
    )
    back_q = mm_nt(dq_raw, jnp.concatenate([w_near[:, :q_cols], w_far[:, :q_cols]], axis=0))
    out_job = (False, dp_count, attended_low, tie(grad_mid, back_q))
    order = jnp.arange(dp_count, dtype=jnp.int32)
    (out_far,) = weight_grad(*out_job, order[half:], [], "stack", "out_far")
    out_got = swap(out_far, 1)
    out_sent = weight_grad(*out_job, order[1:half], [(out_got, 1)], "apart", "out_sent")
    result_came[-1] = tie(result_came[-1], *out_sent)
    dkv_came = [tie(came, result_came[-1]) for came in dkv_came]
    for slot in range(3, mp_count):
        result_came.append(shift((result_came[-1].astype(f32) + ffn_parts[slot]).astype(bf16)))
    dkv_raw, key_gain_part = unproject(
        key_raw, cos_table, sin_table, k_gain,
        [dkv_near, dkv_got] + dkv_came, "unproject_kv",
    )
    back_kv = mm_nt(dkv_raw, jnp.concatenate([w_near[:, q_cols:], w_far[:, q_cols:]], axis=0))
    attn_back = split_slots(back_q + back_kv)
    dqkv = jnp.concatenate([dq_raw, dkv_raw], axis=1)

    first = attn_back[1].astype(bf16)
    qkv_job = (True, dp_count, attn_input, tie(dqkv, first))
    (qkv_far,) = weight_grad(*qkv_job, order[half:], [], "stack", "qkv_far")
    qkv_got = swap(qkv_far, 1)
    attn_gain_part = sum(
        jnp.sum(part * normed, axis=0) for part, normed in zip(attn_back, normed_slots)
    )
    result_came[-1] = tie(result_came[-1], first)
    result = (mixed_rows + (result_came[-1].astype(f32) + ffn_parts[0])).astype(bf16)
    out_came = [swap(sent, mask) for sent, mask in zip(out_sent, far_masks)]
    came = tie(shift(first), qkv_got, attn_gain_part, result, *out_came)
    qkv_job = (True, dp_count, attn_input, tie(dqkv, came))
    qkv_sent = weight_grad(*qkv_job, order[1:half], [(qkv_got, 1)], "apart", "qkv_sent")
    qkv_came = [swap(sent, mask) for sent, mask in zip(qkv_sent, far_masks)]
    attn_gain_part = move_columns(
        jnp.broadcast_to(tie(attn_gain_part, *qkv_sent), (8, width)), true_blocks
    )[0]
    small = jnp.concatenate(
        [attn_gain_part, grad_ffn_norm, query_gain_part.reshape(-1), key_gain_part.reshape(-1)]
    ).reshape(-1, head_dim)
    mask = 1
    while mask < dp_count:
        small = small + swap(small, mask)
        mask *= 2
    for slot in range(2, mp_count):
        acc = (came.astype(f32) + attn_back[slot]).astype(bf16)
        came = shift(acc)
        if slot == 2:
            came = tie(came, small)
            small = tie(small, came)
            mask = 1
            while mask < mp_count:
                small = small + lax.ppermute(small, "mp", [(i, i ^ mask) for i in range(mp_count)])
                mask *= 2
            out_job = (False, dp_count, attended_low, tie(grad_mid, came))
            (grad_output_weight,) = weight_grad(
                *out_job, order[:1], [(out_got, 0)] + out_came, "last", "out_own"
            )
            grad_gu, grad_down = lax.optimization_barrier((grad_gu, grad_down, came))[:2]
            grad_gate, grad_up = grad_gu[:, :ff].astype(f32), grad_gu[:, ff:].astype(f32)
            grad_down = grad_down.astype(f32)
    came = tie(came, small, grad_gate, grad_up, grad_down, grad_output_weight)
    qkv_came = [tie(piece, came) for piece in qkv_came]
    grad_attn_input = move_columns(came.astype(f32) + attn_back[0], true_blocks)
    grad_hidden = grad_mixed + norm_back(grad_attn_input * attn_norm, normed_one, scale_one)
    grad_query, grad_key, grad_value = weight_grad(
        *qkv_job, order[:1], [(qkv_got, 0)] + qkv_came, "last", "qkv_own", (q_cols, k_cols, k_cols)
    )

    small = small.reshape(-1)
    grad_attn_norm = small[:width]
    grad_ffn_gain = small[width:2 * width]
    grad_query_gain = small[2 * width:2 * width + head_dim]
    grad_key_gain = small[2 * width + head_dim:]
    return (
        result,
        grad_hidden,
        grad_attn_norm,
        grad_query,
        grad_key,
        grad_value,
        grad_query_gain,
        grad_key_gain,
        grad_output_weight,
        grad_ffn_gain,
        grad_gate,
        grad_up,
        grad_down,
    )


def solution(mesh):
    rows = P(("dp", "mp"), None)
    placed = (
        rows,
        P(),
        P(),
        P("dp", "mp"),
        P("dp", "mp"),
        P("dp", "mp"),
        P(),
        P(),
        P("mp", "dp"),
        P(),
        P("dp", "mp"),
        P("dp", "mp"),
        P("mp", "dp"),
        rows,
    )
    return jax.shard_map(
        body,
        mesh=mesh,
        in_specs=placed,
        out_specs=(
            rows,
            rows,
            P(),
            P("dp", "mp"),
            P("dp", "mp"),
            P("dp", "mp"),
            P(),
            P(),
            P("mp", "dp"),
            P(),
            P("dp", "mp"),
            P("dp", "mp"),
            P("mp", "dp"),
        ),
        check_vma=False,
    )
```

```python
import functools

import jax
import jax.numpy as jnp
from jax import lax
from jax.experimental import pallas as pl
from jax.experimental.pallas import tpu as pltpu
from jax.sharding import PartitionSpec as P

eps_norm = 1e-06
rope_base = 1000000.0
log2_e = 1.4426950408889634
bf16 = jnp.bfloat16
f32 = jnp.float32
longest = 2048
light_cost = pl.CostEstimate(flops=1 << 20, bytes_accessed=1 << 16, transcendentals=0)


def rms_scale(values):
    return lax.rsqrt(jnp.mean(values * values, axis=-1, keepdims=True) + eps_norm)


def norm_back(grad_hat, normed, scale_rows):
    return scale_rows * (grad_hat - normed * jnp.mean(grad_hat * normed, axis=-1, keepdims=True))


def mm(left, right):
    return jnp.dot(left, right, preferred_element_type=f32)


def mm_nt(left, right):
    return lax.dot_general(left, right, (((1,), (1,)), ((), ())), preferred_element_type=f32)


def mm_tn(left, right):
    return lax.dot_general(left, right, (((0,), (0,)), ((), ())), preferred_element_type=f32)


def pair_mask(kb, places_ref, base_ref, block, slot, tok, sub):
    start = places_ref[slot, 0:1, :]
    place = places_ref[slot, 1:2, :]
    pieces = []
    for piece in range(sub):
        base = base_ref[block * sub + piece]
        rows = lax.broadcasted_iota(jnp.int32, (tok, start.shape[1]), 0)
        pieces.append((rows >= start - base) & (rows <= place - base))
    return jnp.concatenate(pieces, axis=0)


def load_pieces(refs, held_ref, sem_ref):
    rows = refs[0].shape[0]
    copies = [
        pltpu.make_async_copy(ref, held_ref.at[pl.ds(i * rows, rows), :], sem_ref.at[i])
        for i, ref in enumerate(refs)
    ]
    for copy in copies:
        copy.start()
    for copy in copies:
        copy.wait()


def attn_fwd_kernel(flags_ref, base_ref, places_ref, q_ref, *refs, tok, sub, slots, blocks, pieces, repeat, head_dim):
    kv_refs, (o_ref, lse_ref, kv_ref, acc_ref, sum_ref, sem_ref) = refs[:pieces], refs[pieces:]
    kb = tok * sub
    head = pl.program_id(0)
    k_lanes = pl.ds(pl.multiple_of(head * head_dim, head_dim), head_dim)
    v_lanes = pl.ds(pl.multiple_of((pl.num_programs(0) + head) * head_dim, head_dim), head_dim)

    @pl.when(head == 0)
    def _():
        load_pieces(kv_refs, kv_ref, sem_ref)

    acc_ref[...] = jnp.zeros_like(acc_ref)
    sum_ref[...] = jnp.zeros_like(sum_ref)

    def step(keys, block, pair, vt, masked):
        k = kv_ref[keys, k_lanes]
        for slot in [pair * 2, pair * 2 + 1]:
            rows = pl.ds(pl.multiple_of(slot * tok, tok), tok)
            q = jnp.concatenate([q_ref[rows, i * head_dim:(i + 1) * head_dim] for i in range(repeat)], axis=0)
            p = jnp.exp2(mm_nt(k, q))
            if masked:
                p = jnp.where(pair_mask(kb, places_ref, base_ref, block, slot, tok, sub), p, 0.0)
            sum_ref[slot] += jnp.sum(p, axis=0, keepdims=True)
            acc_ref[slot] += mm(vt, p.astype(bf16))

    @pl.loop(0, blocks)
    def _(block):
        any_flag = flags_ref[0, block]
        for pair in range(1, slots // 2):
            any_flag = any_flag + flags_ref[pair, block]
        keys = pl.ds(pl.multiple_of(block * kb, kb), kb)

        @pl.when(any_flag > 0)
        def _():
            vt = kv_ref[keys, v_lanes].T

            @pl.loop(0, slots // 2)
            def _(slot):
                flag = flags_ref[slot, block]

                @pl.when(flag == 1)
                def _():
                    step(keys, block, slot, vt, True)

                @pl.when(flag == 2)
                def _():
                    step(keys, block, slot, vt, False)

    @pl.loop(0, slots)
    def _(slot):
        total = sum_ref[slot]
        out = (acc_ref[slot] * (1.0 / total)).T
        rows = pl.ds(pl.multiple_of(slot * tok, tok), tok)
        for i in range(repeat):
            o_ref[rows, i * head_dim:(i + 1) * head_dim] = out[i * tok:(i + 1) * tok].astype(bf16)
        lse_ref[slot] = jnp.log2(total)


def attn_bwd_kernel(flags_ref, base_ref, places_ref, q_ref, lse_ref, o_ref, do_ref, *refs, tok, sub, slots, blocks, pieces, repeat, head_dim, dq_scale, dk_scale):
    kv_refs = refs[:pieces]
    dq_ref, near_ref, far_ref, kv_ref, dqt_ref, delta_ref, dka_ref, dva_ref, sem_ref = refs[pieces:]
    kb = tok * sub
    head = pl.program_id(0)
    k_lanes = pl.ds(pl.multiple_of(head * head_dim, head_dim), head_dim)
    v_lanes = pl.ds(pl.multiple_of((pl.num_programs(0) + head) * head_dim, head_dim), head_dim)

    @pl.when(head == 0)
    def _():
        load_pieces(kv_refs, kv_ref, sem_ref)

    dqt_ref[...] = jnp.zeros_like(dqt_ref)

    def rows_of(ref, slot):
        rows = pl.ds(pl.multiple_of(slot * tok, tok), tok)
        return jnp.concatenate([ref[rows, i * head_dim:(i + 1) * head_dim] for i in range(repeat)], axis=0)

    @pl.loop(0, slots)
    def _(slot):
        prod = rows_of(do_ref, slot).astype(f32) * rows_of(o_ref, slot).astype(f32)
        delta_ref[slot] = jnp.sum(prod.T, axis=0, keepdims=True)

    def step(block, pair, k, v, kt, masked):
        for slot in [pair * 2, pair * 2 + 1]:
            q = rows_of(q_ref, slot)
            do = rows_of(do_ref, slot)
            p = jnp.exp2(mm_nt(k, q) - lse_ref[slot])
            if masked:
                p = jnp.where(pair_mask(kb, places_ref, base_ref, block, slot, tok, sub), p, 0.0)
            ds = (p * (mm_nt(v, do) - delta_ref[slot])).astype(bf16)
            dva_ref[...] += mm(p.astype(bf16), do)
            dka_ref[...] += mm(ds, q)
            dqt_ref[slot] += mm(kt, ds)

    @pl.loop(0, blocks)
    def _(block):
        any_flag = flags_ref[0, block]
        for pair in range(1, slots // 2):
            any_flag = any_flag + flags_ref[pair, block]
        dka_ref[...] = jnp.zeros_like(dka_ref)
        dva_ref[...] = jnp.zeros_like(dva_ref)
        keys = pl.ds(pl.multiple_of(block * kb, kb), kb)

        @pl.when(any_flag > 0)
        def _():
            k = kv_ref[keys, k_lanes]
            v = kv_ref[keys, v_lanes]
            kt = k.T

            @pl.loop(0, slots // 2)
            def _(slot):
                flag = flags_ref[slot, block]

                @pl.when(flag == 1)
                def _():
                    step(block, slot, k, v, kt, True)

                @pl.when(flag == 2)
                def _():
                    step(block, slot, k, v, kt, False)

        @pl.when(block < blocks // 2)
        def _():
            near_ref[keys, k_lanes] = (dka_ref[...] * dk_scale).astype(bf16)
            near_ref[keys, v_lanes] = dva_ref[...].astype(bf16)

        @pl.when(block >= blocks // 2)
        def _():
            far = pl.ds(pl.multiple_of(block * kb - blocks // 2 * kb, kb), kb)
            far_ref[far, k_lanes] = (dka_ref[...] * dk_scale).astype(bf16)
            far_ref[far, v_lanes] = dva_ref[...].astype(bf16)

    @pl.loop(0, slots)
    def _(slot):
        out = (dqt_ref[slot] * dq_scale).T
        rows = pl.ds(pl.multiple_of(slot * tok, tok), tok)
        for i in range(repeat):
            dq_ref[rows, i * head_dim:(i + 1) * head_dim] = out[i * tok:(i + 1) * tok]


def turn(values):
    half = values.shape[-1] // 2
    return jnp.concatenate([values[:, half:], values[:, :half]], axis=1)


def rotated_heads(raw, cos_ref, sin_ref, gain_ref, out_ref, head_dim, scale):
    for first in range(0, raw.shape[1], head_dim):
        lanes = slice(first, first + head_dim)
        hat = raw[:, lanes] * rms_scale(raw[:, lanes]) * gain_ref[...]
        out_ref[:, lanes] = ((hat * cos_ref[...] + turn(hat) * sin_ref[...]) * scale).astype(bf16)


def project_kv_kernel(w_ref, cos_ref, sin_ref, gain_ref, norm_ref, *refs, head_dim):
    *slot_refs, x_ref, rows_ref, raw_ref, out_ref = refs
    tok = slot_refs[0].shape[0]
    step = pl.program_id(0)

    @pl.when(step == 0)
    def _():
        for slot, slot_ref in enumerate(slot_refs):
            lines = slice(slot * tok, (slot + 1) * tok)
            values = slot_ref[...].astype(f32)
            scale = rms_scale(values)
            x_ref[lines] = (values * scale * norm_ref[...]).astype(bf16)
            rows_ref[lines] = jnp.broadcast_to(scale, (tok, rows_ref.shape[1]))

    raw = mm(x_ref[...], w_ref[...])

    @pl.when(step == 0)
    def _():
        raw_ref[...] = raw
        rotated_heads(raw, cos_ref, sin_ref, gain_ref, out_ref, head_dim, 1.0)

    @pl.when(step == 1)
    def _():
        out_ref[...] = raw.astype(bf16)


def project_kv(slots, norm, w, cos_table, sin_table, gain, first, tile):
    tok, width = slots[0].shape
    tokens, head_dim = tok * len(slots), gain.shape[1]

    def whole(rows, cols):
        return pl.BlockSpec((rows, cols), lambda j: (0, 0))

    w_spec = pl.BlockSpec((width, tile), lambda j: (0, j + first))
    return pl.pallas_call(
        functools.partial(project_kv_kernel, head_dim=head_dim),
        grid=(2,),
        in_specs=[w_spec, whole(tokens, head_dim), whole(tokens, head_dim), whole(1, head_dim), whole(1, width)]
        + [whole(tok, width)] * len(slots),
        out_specs=[whole(tokens, width), whole(tokens, head_dim), whole(tokens, tile), pl.BlockSpec((tokens, tile), lambda j: (0, j))],
        out_shape=[
            jax.ShapeDtypeStruct((tokens, width), bf16),
            jax.ShapeDtypeStruct((tokens, head_dim), f32),
            jax.ShapeDtypeStruct((tokens, tile), f32),
            jax.ShapeDtypeStruct((tokens, 2 * tile), bf16),
        ],
        cost_estimate=light_cost,
        name="project_kv",
    )(w, cos_table, sin_table, gain, norm, *slots)


def project_q_kernel(x_ref, w_ref, cos_ref, sin_ref, gain_ref, raw_ref, out_ref, *, head_dim, scale):
    raw = mm(x_ref[...], w_ref[...])
    raw_ref[...] = raw
    rotated_heads(raw, cos_ref, sin_ref, gain_ref, out_ref, head_dim, scale)


def project_q(x, w, cos_table, sin_table, gain, cols, tile, scale):
    tokens, width = x.shape
    head_dim = gain.shape[1]

    def whole(rows, cols):
        return pl.BlockSpec((rows, cols), lambda j: (0, 0))

    w_spec = pl.BlockSpec((width, tile), lambda j: (0, j))
    out_spec = pl.BlockSpec((tokens, tile), lambda j: (0, j))
    return pl.pallas_call(
        functools.partial(project_q_kernel, head_dim=head_dim, scale=scale),
        grid=(cols // tile,),
        in_specs=[whole(tokens, width), w_spec, whole(tokens, head_dim), whole(tokens, head_dim), whole(1, head_dim)],
        out_specs=[out_spec, out_spec],
        out_shape=[jax.ShapeDtypeStruct((tokens, cols), f32), jax.ShapeDtypeStruct((tokens, cols), bf16)],
        cost_estimate=light_cost,
        name="project_q",
    )(x, w, cos_table, sin_table, gain)


def unproject_kernel(raw_ref, cos_ref, sin_ref, gain_ref, *refs, head_dim, sums):
    grad_refs, (out_ref, part_ref) = refs[:sums], refs[sums:]
    part = jnp.zeros((1, head_dim), f32)
    for first in range(0, out_ref.shape[1], head_dim):
        lanes = slice(first, first + head_dim)
        grad = grad_refs[0][:, lanes].astype(f32)
        for grad_ref in grad_refs[1:]:
            grad = grad + grad_ref[:, lanes].astype(f32)
        if first < raw_ref.shape[1]:
            raw = raw_ref[:, lanes]
            scale = rms_scale(raw)
            hat = raw * scale
            grad = grad * cos_ref[...] - turn(grad) * sin_ref[...]
            part = part + jnp.sum(grad * hat, axis=0, keepdims=True)
            grad = norm_back(grad * gain_ref[...], hat, scale)
        out_ref[:, lanes] = grad.astype(bf16)
    part_ref[...] = part


def unproject(raw, cos_table, sin_table, gain, grads, name):
    tokens, cols = raw.shape[0], grads[0].shape[1]
    head_dim = gain.shape[1]

    def first_rows(width):
        return pl.BlockSpec((tokens, width), lambda j: (0, 0))

    gain_spec = pl.BlockSpec((1, head_dim), lambda j: (0, 0))
    return pl.pallas_call(
        functools.partial(unproject_kernel, head_dim=head_dim, sums=len(grads)),
        grid=(1,),
        in_specs=[first_rows(raw.shape[1]), first_rows(head_dim), first_rows(head_dim), gain_spec]
        + [first_rows(cols)] * len(grads),
        out_specs=[first_rows(cols), gain_spec],
        out_shape=[
            jax.ShapeDtypeStruct((tokens, cols), bf16),
            jax.ShapeDtypeStruct(gain.shape, f32),
        ],
        cost_estimate=light_cost,
        name=name,
    )(raw, cos_table, sin_table, gain, *grads)


def attn_back_kernel(dq_ref, dkv_ref, w_ref, rows_ref, *refs, slots):
    hidden_refs, out_refs, gain_ref = refs[:slots], refs[slots:-1], refs[-1]
    q_cols = dq_ref.shape[1]
    tok = out_refs[0].shape[0]
    total = mm_nt(dq_ref[...], w_ref[:, :q_cols]) + mm_nt(dkv_ref[...], w_ref[:, q_cols:])
    gain = jnp.zeros((1, total.shape[1]), f32)
    for slot in range(slots):
        lines = slice(slot * tok, (slot + 1) * tok)
        part = total[lines]
        gain = gain + jnp.sum(part * (hidden_refs[slot][...].astype(f32) * rows_ref[lines, :1]), axis=0, keepdims=True)
        out_refs[slot][...] = part.astype(bf16)
    gain_ref[...] = jnp.broadcast_to(gain, gain_ref.shape)


def attn_back_product(dq, dkv, w, row_scales, hidden_slots):
    rows, q_cols = dq.shape
    slots = len(hidden_slots)
    tok, width = hidden_slots[0].shape
    tile = min(512, width)
    slot_spec = pl.BlockSpec((tok, tile), lambda t: (0, t))
    return pl.pallas_call(
        functools.partial(attn_back_kernel, slots=slots),
        grid=(width // tile,),
        in_specs=[
            pl.BlockSpec((rows, q_cols), lambda t: (0, 0)),
            pl.BlockSpec((rows, dkv.shape[1]), lambda t: (0, 0)),
            pl.BlockSpec((tile, q_cols + dkv.shape[1]), lambda t: (t, 0)),
            pl.BlockSpec(row_scales.shape, lambda t: (0, 0)),
        ]
        + [slot_spec] * slots,
        out_specs=[slot_spec] * slots + [pl.BlockSpec((8, tile), lambda t: (0, t))],
        out_shape=[jax.ShapeDtypeStruct((tok, width), bf16)] * slots + [jax.ShapeDtypeStruct((8, width), f32)],
        cost_estimate=light_cost,
        name="attn_back",
    )(dq, dkv, w, row_scales, *hidden_slots)


def grad_attended_kernel(w_ref, *refs):
    *slot_refs, mid_ref, out_ref = refs
    tok = slot_refs[0].shape[0]
    for slot, slot_ref in enumerate(slot_refs):
        mid_ref[slot * tok:(slot + 1) * tok] = slot_ref[...]
    out_ref[...] = mm(mid_ref[...], w_ref[...]).astype(bf16)


def grad_attended_product(slots, w, cols):
    tok, width = slots[0].shape
    rows = tok * len(slots)

    def whole(rows, cols):
        return pl.BlockSpec((rows, cols), lambda j: (0, 0))

    return pl.pallas_call(
        grad_attended_kernel,
        grid=(1,),
        in_specs=[pl.BlockSpec((width, cols), lambda j: (0, w.shape[1] // cols - 1))] + [whole(tok, width)] * len(slots),
        out_specs=[whole(rows, width), whole(rows, cols)],
        out_shape=[jax.ShapeDtypeStruct((rows, width), bf16), jax.ShapeDtypeStruct((rows, cols), bf16)],
        cost_estimate=light_cost,
        name="grad_attended",
    )(w, *slots)


def simple_call(kernel, arrays, shapes, name):
    vmem = pl.BlockSpec(memory_space=pltpu.VMEM)
    return pl.pallas_call(
        kernel,
        in_specs=[vmem] * len(arrays),
        out_specs=[vmem] * len(shapes),
        out_shape=[jax.ShapeDtypeStruct(shape, dtype) for shape, dtype in shapes],
        cost_estimate=light_cost,
        name=name,
    )(*arrays)


def add_rounded(left, right):
    return (left.astype(f32) + right.astype(f32)).astype(bf16)


def summed(refs):
    count = len(refs) // 2
    return jnp.concatenate(
        [came[...].astype(f32) + part[...].astype(f32) for came, part in zip(refs[:count], refs[count:])],
        axis=0,
    )


def store_halves(values, refs):
    rows = refs[0].shape[0]
    for i, ref in enumerate(refs):
        ref[...] = values[i * rows:(i + 1) * rows].astype(ref.dtype)


def mix_kernel(*refs, halves):
    sum_refs, (hidden_ref, norm_ref, mixed_ref, *input_refs) = refs[:2 * halves], refs[2 * halves:]
    mixed = hidden_ref[...].astype(f32) + summed(sum_refs)
    mixed_ref[...] = mixed
    store_halves(mixed * rms_scale(mixed) * norm_ref[...], input_refs)


def mid_kernel(*refs, halves):
    sum_refs, (mixed_ref, norm_ref, out_ref, grad_ref, gain_ref, *low_refs) = refs[:2 * halves], refs[2 * halves:]
    mixed = mixed_ref[...]
    scale = rms_scale(mixed)
    normed = mixed * scale
    back = summed(sum_refs)
    gain_ref[...] = jnp.sum(back * normed, axis=0, keepdims=True)
    grad = out_ref[...].astype(f32) + norm_back(back * norm_ref[...], normed, scale)
    grad_ref[...] = grad
    store_halves(grad, low_refs)


def last_kernel(*refs, halves):
    sum_refs, (grad_ref, hidden_ref, norm_ref, out_ref) = refs[:2 * halves], refs[2 * halves:]
    hidden = hidden_ref[...].astype(f32)
    scale = rms_scale(hidden)
    out_ref[...] = grad_ref[...] + norm_back(summed(sum_refs) * norm_ref[...], hidden * scale, scale)


def result_kernel(*refs, halves):
    sum_refs, (mixed_ref, out_ref) = refs[:2 * halves], refs[2 * halves:]
    out_ref[...] = (mixed_ref[...] + summed(sum_refs)).astype(bf16)


def ffn_kernel(gate_ref, up_ref, down_ref, *refs, parts, held):
    x_refs, g_refs, refs = refs[:parts], refs[parts:2 * parts], refs[2 * parts + held:]
    grad_ref, x_ref, go_ref, *back_refs, back_ref = refs
    tile = pl.program_id(0)
    tok, size = x_refs[0].shape[0], gate_ref.shape[1]
    ff = grad_ref.shape[1] // 3

    @pl.when(tile == 0)
    def _():
        for i in range(parts):
            x_ref[i * tok:(i + 1) * tok] = x_refs[i][...]
            go_ref[i * tok:(i + 1) * tok] = g_refs[i][...]
        back_ref[...] = jnp.zeros_like(back_ref)

    x = x_ref[...]
    gate_pre = mm(x, gate_ref[...])
    up_value = mm(x, up_ref[...])
    grad_act = mm(go_ref[...], down_ref[...])
    sigmoid_gate = jax.nn.sigmoid(gate_pre)
    gated = gate_pre * sigmoid_gate
    grad_gate_pre = (
        grad_act * up_value * sigmoid_gate * (1.0 + gate_pre * (1.0 - sigmoid_gate))
    ).astype(bf16)
    grad_up_value = (grad_act * gated).astype(bf16)
    for i, values in enumerate([grad_gate_pre, grad_up_value, (gated * up_value).astype(bf16)]):
        grad_ref[:, pl.ds(pl.multiple_of(i * ff + tile * size, size), size)] = values
    back_ref[...] += mm_nt(grad_gate_pre, gate_ref[...]) + mm_nt(grad_up_value, up_ref[...])

    @pl.when(tile == pl.num_programs(0) - 1)
    def _():
        store_halves(back_ref[...], back_refs)


def feed_forward(inputs, grads, w_ffn, held, chunk, chunks):
    parts = len(inputs)
    tok, width = inputs[0].shape
    ff = w_ffn.shape[1] // 3
    size = next(s for s in (512, 384, 256, 128) if ff % s == 0)
    tiles = ff // size
    part_spec = pl.BlockSpec((tok, width), lambda t: (0, 0))

    def rows_spec(cols):
        return pl.BlockSpec((parts * tok, cols), lambda t: (chunk, 0))

    rows = parts * tok * chunks
    return pl.pallas_call(
        functools.partial(ffn_kernel, parts=parts, held=len(held)),
        grid=(tiles,),
        in_specs=[
            pl.BlockSpec((width, size), lambda t: (0, t)),
            pl.BlockSpec((width, size), lambda t: (0, tiles + t)),
            pl.BlockSpec((width, size), lambda t: (0, 2 * tiles + t)),
        ]
        + [part_spec] * (2 * parts)
        + [pl.BlockSpec(memory_space=pl.ANY)] * len(held),
        out_specs=[rows_spec(3 * ff), rows_spec(width), rows_spec(width)] + [part_spec] * parts,
        out_shape=[
            jax.ShapeDtypeStruct((rows, 3 * ff), bf16),
            jax.ShapeDtypeStruct((rows, width), bf16),
            jax.ShapeDtypeStruct((rows, width), bf16),
        ]
        + [jax.ShapeDtypeStruct((tok, width), bf16)] * parts,
        scratch_shapes=[pltpu.VMEM((parts * tok, width), f32)],
        input_output_aliases={3 + 2 * parts + i: i for i in range(len(held))},
        cost_estimate=light_cost,
        name="feed_forward",
    )(w_ffn, w_ffn, w_ffn, *inputs, *grads, *held)


def weight_grads_kernel(*refs, turns):
    *left_refs, right_ref, out_ref, turned_ref = refs
    tile = pl.program_id(0)
    for left_ref, at in zip(left_refs, turns):
        @pl.when(tile == at)
        def _(left_ref=left_ref):
            turned_ref[...] = left_ref[...].T

    rows = min(256, out_ref.shape[0])
    for first in range(0, out_ref.shape[0], rows):
        lines = slice(first, first + rows)
        out_ref[lines] = mm(turned_ref[lines], right_ref[...]).astype(bf16)


def weight_grads(lefts, right, starts, name):
    tokens, width = lefts[0].shape
    cols = right.shape[1]
    size = next(s for s in (512, 384, 256, 128) if all(at % s == 0 for at in (cols, *starts)))
    whole = pl.BlockSpec((tokens, width), lambda t: (0, 0))
    return pl.pallas_call(
        functools.partial(weight_grads_kernel, turns=[at // size for at in starts]),
        grid=(cols // size,),
        in_specs=[whole] * len(lefts) + [pl.BlockSpec((tokens, size), lambda t: (0, t))],
        out_specs=pl.BlockSpec((width, size), lambda t: (0, t)),
        out_shape=jax.ShapeDtypeStruct((width, cols), bf16),
        scratch_shapes=[pltpu.VMEM((width, tokens), bf16)],
        cost_estimate=light_cost,
        name=name,
    )(*lefts, right)


def slot_product_kernel(x_ref, w_ref, *out_refs):
    tok = out_refs[0].shape[0]
    total = mm_nt(x_ref[...], w_ref[...])
    for slot, out_ref in enumerate(out_refs):
        out_ref[...] = total[slot * tok:(slot + 1) * tok].astype(bf16)


def slot_product(x, x_block, w, w_block, depth, slots, name):
    rows, width = x.shape[0], w.shape[0]
    tile = min(512, width)
    out_spec = pl.BlockSpec((rows // slots, tile), lambda t: (0, t))
    return pl.pallas_call(
        slot_product_kernel,
        grid=(width // tile,),
        in_specs=[
            pl.BlockSpec((rows, depth), lambda t: (0, x_block)),
            pl.BlockSpec((tile, depth), lambda t: (t, w_block)),
        ],
        out_specs=[out_spec] * slots,
        out_shape=[jax.ShapeDtypeStruct((rows // slots, width), bf16)] * slots,
        cost_estimate=light_cost,
        name=name,
    )(x, w)


def fold_kernel(near_ref, got_ref, *out_refs):
    rows = out_refs[0].shape[0]
    for i, out_ref in enumerate(out_refs):
        lines = slice((i + 1) * rows, (i + 2) * rows)
        out_ref[...] = (near_ref[lines].astype(f32) + got_ref[lines].astype(f32)).astype(bf16)


def fold_blocks(near, got, count):
    vmem = pl.BlockSpec(memory_space=pltpu.VMEM)
    shape = jax.ShapeDtypeStruct((near.shape[0] // count, near.shape[1]), bf16)
    return pl.pallas_call(
        fold_kernel,
        in_specs=[vmem, vmem],
        out_specs=[vmem] * (count - 1),
        out_shape=[shape] * (count - 1),
        cost_estimate=light_cost,
        name="fold_blocks",
    )(near, got)


def body(
    hidden_in,
    doc_lengths,
    attn_norm,
    query_weight,
    key_weight,
    value_weight,
    query_gain,
    key_gain,
    output_weight,
    ffn_norm,
    gate_weight,
    up_weight,
    down_weight,
    grad_out,
):
    dp_count = lax.axis_size("dp")
    mp_count = lax.axis_size("mp")
    slots = mp_count
    tok, width = hidden_in.shape
    group_rows = tok * mp_count
    head_dim = query_gain.shape[0]
    half_dim = head_dim // 2
    q_cols = query_weight.shape[1]
    k_cols = key_weight.shape[1]
    kv_local = k_cols // head_dim
    repeat = q_cols // k_cols
    ff = gate_weight.shape[1]
    group = lax.axis_index("dp")
    my_z = lax.axis_index("mp")
    score_scale = head_dim ** (-0.5)
    ring = [(i, (i + 1) % mp_count) for i in range(mp_count)]
    near_masks = list(range(0, dp_count, 2))
    masks = near_masks + [mask + 1 for mask in near_masks]
    far_masks = near_masks[1:]

    def tie(value, *others):
        return lax.optimization_barrier((value,) + others)[0]

    def shift(values):
        return lax.ppermute(values, "mp", ring)

    def swap(values, mask):
        return lax.ppermute(values, "dp", [(i, i ^ mask) for i in range(dp_count)])

    reach = (min(longest, group_rows * dp_count) - 2) // group_rows + 1

    def needs(reader, owner):
        first = reader // 2 * 2
        return owner <= first + 1 and owner >= first - reach

    def swap_forward(values, mask):
        pairs = [(i, i ^ mask) for i in range(dp_count) if needs(i ^ mask, i)]
        return lax.ppermute(values, "dp", pairs)

    def swap_back(values, mask):
        pairs = [(i, i ^ mask) for i in range(dp_count) if needs(i, i ^ mask)]
        return lax.ppermute(values, "dp", pairs)

    half = dp_count // 2
    halves = 2
    part_rows = tok // halves
    ids = jnp.array(masks, jnp.int32)
    mask_blocks = group ^ ids
    attn_norm = attn_norm.reshape(1, width)
    ffn_norm = ffn_norm.reshape(1, width)
    part_shape = ((part_rows, width), bf16)

    def tie_all(values, *others):
        return list(lax.optimization_barrier((*values, *others)))[:len(values)]

    def flat(slot_lists):
        return [part for slot in slot_lists for part in slot]

    def by_slot(parts):
        return [list(parts[i:i + halves]) for i in range(0, len(parts), halves)]

    def shift_all(parts):
        return [shift(part) for part in parts]

    def ring_add(came, own):
        return [shift(add_rounded(one, other)) for one, other in zip(came, own)]

    w_attn_own = jnp.concatenate([query_weight, key_weight, value_weight, output_weight.T], axis=1)
    w_ffn_own = jnp.concatenate([gate_weight, up_weight, down_weight.T], axis=1)
    w_attn = lax.all_gather(w_attn_own, "dp", axis=0, tiled=True)
    w_ffn = tie(lax.all_gather(w_ffn_own, "dp", axis=0, tiled=True), w_attn)

    doc_ends = jnp.cumsum(doc_lengths)
    slot_offset = ((my_z - jnp.arange(slots, dtype=jnp.int32)) % mp_count) * tok
    places = (
        group * group_rows
        + slot_offset[:, None]
        + jnp.arange(tok, dtype=jnp.int32)[None, :]
    )
    before = doc_ends[None, None, :] <= places[:, :, None]
    starts = jnp.sum(jnp.where(before, doc_lengths[None, None, :], 0), axis=-1)
    position = (places - starts).reshape(group_rows)
    inverse = rope_base ** (-(2.0 * jnp.arange(half_dim, dtype=f32)) / head_dim)
    angles = position.astype(f32)[:, None] * inverse[None, :]
    cos_table, sin_table = jnp.cos(angles), jnp.sin(angles)
    cos_table = jnp.concatenate([cos_table, cos_table], axis=1)
    sin_table = jnp.concatenate([-sin_table, sin_table], axis=1)

    sub = min(4, slots)
    key_base = mask_blocks[:, None] * group_rows + slot_offset[None, :]
    blocks = dp_count * slots // sub
    key_base = key_base.reshape(blocks, sub)
    q_first, q_last = places[:, 0], places[:, -1]
    s_first, s_last = starts[:, 0], starts[:, -1]
    piece_lo, piece_hi = key_base[None], key_base[None] + tok - 1
    some = (piece_lo <= q_last[:, None, None]) & (s_first[:, None, None] <= piece_hi)
    every = (piece_hi <= q_first[:, None, None]) & (s_last[:, None, None] <= piece_lo)
    flags = jnp.where(jnp.all(every, -1), 2, jnp.any(some, -1).astype(jnp.int32)).astype(jnp.int32)
    by_pair = flags.reshape(slots // 2, 2, blocks)
    flags = jnp.where(jnp.all(by_pair == 2, axis=1), 2, jnp.any(by_pair > 0, axis=1).astype(jnp.int32))
    key_base = key_base.reshape(-1)
    lane_places = jnp.tile(jnp.stack([starts, places], axis=1), (1, 1, repeat))

    hidden_slots = [[hidden_in[i * part_rows:(i + 1) * part_rows] for i in range(halves)]]
    for slot in range(1, slots):
        came = shift_all(hidden_slots[-1])
        if slot == 1:
            came = tie_all(came, cos_table, sin_table, lane_places, w_ffn_own)
        hidden_slots.append(came)
    q_gain, k_gain = query_gain.reshape(1, head_dim), key_gain.reshape(1, head_dim)
    attn_input, row_scales, key_raw, kv_own = project_kv(
        flat(hidden_slots), attn_norm, w_attn, cos_table, sin_table, k_gain, repeat, k_cols
    )
    kv_came = [swap_forward(kv_own, mask) for mask in far_masks]
    grad_slots = [tie_all([grad_out[i * part_rows:(i + 1) * part_rows] for i in range(halves)], *hidden_slots[-1])]
    grad_slots.append(tie_all(shift_all(grad_slots[-1]), kv_own))
    query_raw, query_rot = project_q(
        tie(attn_input, kv_own, *grad_slots[-1]), w_attn, cos_table, sin_table, q_gain, q_cols, k_cols,
        score_scale * log2_e,
    )
    for slot in range(2, slots):
        came = shift_all(grad_slots[-1])
        if slot == 2:
            came = tie_all(came, query_rot)
            kv_came = tie_all(kv_came, *came)
        grad_slots.append(came)
    kv_near = [kv_own] + tie_all(kv_came, query_rot)
    kv_pieces = kv_near + [swap(piece, 1) for piece in kv_near]

    keys_total = dp_count * group_rows
    head_rows = repeat * tok
    smem = pl.BlockSpec(memory_space=pltpu.SMEM)
    any_spec = pl.BlockSpec(memory_space=pl.ANY)
    whole_places = pl.BlockSpec((slots, 2, head_rows), lambda h: (0, 0, 0))
    q_spec = pl.BlockSpec((group_rows, repeat * head_dim), lambda h: (0, h))
    lse_spec = pl.BlockSpec((None, slots, 1, head_rows), lambda h: (h, 0, 0, 0))
    dims = dict(
        tok=tok, sub=sub, slots=slots, blocks=blocks, pieces=dp_count, repeat=repeat, head_dim=head_dim
    )
    kv_scratch = pltpu.VMEM((keys_total, 2 * k_cols), bf16)
    attended_low, lse = pl.pallas_call(
        functools.partial(attn_fwd_kernel, **dims),
        grid=(kv_local,),
        in_specs=[smem, smem, whole_places, q_spec] + [any_spec] * dp_count,
        out_specs=[q_spec, lse_spec],
        out_shape=[
            jax.ShapeDtypeStruct((group_rows, q_cols), bf16),
            jax.ShapeDtypeStruct((kv_local, slots, 1, head_rows), f32),
        ],
        scratch_shapes=[
            kv_scratch,
            pltpu.VMEM((slots, head_dim, head_rows), f32),
            pltpu.VMEM((slots, 1, head_rows), f32),
            pltpu.SemaphoreType.DMA((dp_count,)),
        ],
        cost_estimate=light_cost,
        name="attn_fwd",
    )(flags, key_base, lane_places, query_rot, *kv_pieces)

    grad_slots[slots - 1] = tie_all(grad_slots[slots - 1], attended_low)
    parts = by_slot(slot_product(attended_low, 0, w_attn, 2 * k_cols // q_cols + 1, q_cols, slots * halves, "attn_out"))
    came = shift_all(tie_all(parts[1], *grad_slots[-1]))
    for slot in range(2, slots):
        came = ring_add(came, parts[slot])
    mixed_rows, *ffn_input = simple_call(
        functools.partial(mix_kernel, halves=halves),
        [*came, *parts[0], hidden_in, ffn_norm],
        [((tok, width), f32)] + [part_shape] * halves,
        "mix",
    )

    ffn_slots = [ffn_input, shift_all(ffn_input)]
    held, parts = [], []
    for first in range(0, slots, 2):
        *held, = feed_forward(
            flat(ffn_slots[first:first + 2]), flat(grad_slots[first:first + 2]), w_ffn, held, first // 2, slots // 2
        )
        held, back = held[:3], held[3:]
        parts += by_slot(back)
        if first + 2 < slots:
            ffn_slots.append(tie_all(shift_all(ffn_slots[-1]), *back))
            ffn_slots.append(shift_all(ffn_slots[-1]))
    ffn_right, ffn_all, grad_all = held

    came = shift_all(tie_all(parts[1], *ffn_slots[-1]))
    ffn_part = weight_grads([ffn_all, grad_all], tie(ffn_right, *came), [0, 2 * ff], "ffn_grads")
    for slot in range(2, slots):
        came = ring_add(came, parts[slot])
        if slot == 2:
            came = tie_all(came, ffn_part)
    grad_ffn = lax.psum_scatter(ffn_part, "dp", scatter_dimension=0, tiled=True)
    grad_mixed, grad_ffn_norm, *mid_first = simple_call(
        functools.partial(mid_kernel, halves=halves),
        [*came, *parts[0], mixed_rows, ffn_norm, grad_out],
        [((tok, width), f32), ((1, width), f32)] + [part_shape] * halves,
        "mid",
    )
    mid_slots = [mid_first]
    result_parts = by_slot(slot_product(tie(ffn_right, *mid_first), 2, w_ffn, 2, ff, slots * halves, "ffn_out"))
    for slot in range(1, slots):
        came = shift_all(mid_slots[-1])
        if slot == 1:
            came = tie_all(came, *flat(result_parts))
        mid_slots.append(came)

    grad_mid, grad_attended = grad_attended_product(flat(mid_slots), w_attn, q_cols)
    result_first = tie_all(result_parts[1], *mid_slots[-1])
    result_came = shift_all(result_first)
    near_spec = pl.BlockSpec((keys_total // 2, 2 * k_cols), lambda h: (0, 0))
    near_shape = jax.ShapeDtypeStruct((keys_total // 2, 2 * k_cols), bf16)
    dq_rot, dkv_near, dkv_far = pl.pallas_call(
        functools.partial(
            attn_bwd_kernel, **dims, dq_scale=score_scale, dk_scale=1.0 / log2_e
        ),
        grid=(kv_local,),
        in_specs=[smem, smem, whole_places, q_spec, lse_spec, q_spec, q_spec] + [any_spec] * dp_count,
        out_specs=[q_spec, near_spec, near_spec],
        out_shape=[jax.ShapeDtypeStruct((group_rows, q_cols), f32), near_shape, near_shape],
        scratch_shapes=[
            kv_scratch,
            pltpu.VMEM((slots, head_dim, head_rows), f32),
            pltpu.VMEM((slots, 1, head_rows), f32),
            pltpu.VMEM((tok * sub, head_dim), f32),
            pltpu.VMEM((tok * sub, head_dim), f32),
            pltpu.SemaphoreType.DMA((dp_count,)),
        ],
        cost_estimate=light_cost,
        name="attn_bwd",
    )(flags, key_base, lane_places, query_rot, lse, attended_low, tie(grad_attended, *result_first), *kv_pieces)

    dkv_got = swap(tie(dkv_far, *result_came), 1)
    result_came = ring_add(result_came, result_parts[2])
    dkv_sent = fold_blocks(dkv_near, dkv_got, half)
    dkv_came = [swap_back(sent, mask) for sent, mask in zip(dkv_sent, far_masks)]
    dq_raw, query_gain_part = unproject(
        query_raw, cos_table, sin_table, q_gain, [tie(dq_rot, *dkv_sent)], "unproject_q"
    )
    out_part = weight_grads([tie(grad_mid, dq_raw)], attended_low, [0], "out_grads")
    grad_out_weight = lax.psum_scatter(out_part, "dp", scatter_dimension=0, tiled=True)
    result_came = tie_all(result_came, dq_raw)
    dkv_came[-1] = tie(dkv_came[-1], out_part)
    dkv_came[0] = tie(dkv_came[0], *result_came)
    for slot in range(3, slots):
        result_came = ring_add(result_came, result_parts[slot])
    dkv_came[1:] = tie_all(dkv_came[1:], *result_came)
    dkv_raw, key_gain_part = unproject(
        key_raw, cos_table, sin_table, k_gain, [dkv_near, dkv_got] + dkv_came, "unproject_kv"
    )

    *parts, attn_gain_part = attn_back_product(dq_raw, dkv_raw, w_attn, row_scales, flat(hidden_slots))
    parts = by_slot(parts)
    first = parts[1]
    dqkv = jnp.concatenate([dq_raw, dkv_raw], axis=1)
    qkv_part = weight_grads([attn_input], tie(dqkv, *first), [0], "qkv_grads")
    grad_qkv = lax.psum_scatter(qkv_part, "dp", scatter_dimension=0, tiled=True)
    small = jnp.concatenate(
        [attn_gain_part[0], grad_ffn_norm[0], query_gain_part[0], key_gain_part[0]]
    ).reshape(-1, head_dim)
    small = small + swap(small, 1)
    came = tie_all(shift_all(first), small, qkv_part)
    (result,) = simple_call(
        functools.partial(result_kernel, halves=halves), [*tie_all(result_came, *came), *result_parts[0], mixed_rows],
        [((tok, width), bf16)], "result",
    )
    small = small + sum(swap(small, mask) for mask in far_masks)
    for slot in range(2, slots):
        came = ring_add(came, parts[slot])
        if slot == 2:
            came = tie_all(came, small, result)
            turns = [[(i, (i + by) % mp_count) for i in range(mp_count)] for by in range(1, mp_count)]
            small = small + sum(lax.ppermute(small, "mp", turn) for turn in turns)
            grad_ffn = tie(grad_ffn, *came)
            grad_gate, grad_up = grad_ffn[:, :ff].astype(f32), grad_ffn[:, ff:2 * ff].astype(f32)
            grad_down = grad_ffn[:, 2 * ff:].T.astype(f32)
    came = tie_all(came, small, grad_gate, grad_up, grad_down)
    (grad_hidden,) = simple_call(
        functools.partial(last_kernel, halves=halves),
        [*came, *parts[0], grad_mixed, hidden_in, attn_norm],
        [((tok, width), f32)],
        "last",
    )
    grad_out_weight = tie(grad_out_weight, grad_hidden, grad_gate, grad_up, grad_down).T.astype(f32)
    grad_qkv = tie(grad_qkv, grad_out_weight).astype(f32)

    small = small.reshape(-1)
    return (
        result,
        grad_hidden,
        small[:width],
        grad_qkv[:, :q_cols],
        grad_qkv[:, q_cols:q_cols + k_cols],
        grad_qkv[:, q_cols + k_cols:],
        small[2 * width:2 * width + head_dim],
        small[2 * width + head_dim:],
        grad_out_weight,
        small[width:2 * width],
        grad_gate,
        grad_up,
        grad_down,
    )


def solution(mesh):
    rows = P(("dp", "mp"), None)
    placed = (
        rows,
        P(),
        P(),
        P("dp", "mp"),
        P("dp", "mp"),
        P("dp", "mp"),
        P(),
        P(),
        P("mp", "dp"),
        P(),
        P("dp", "mp"),
        P("dp", "mp"),
        P("mp", "dp"),
        rows,
    )
    return jax.shard_map(
        body,
        mesh=mesh,
        in_specs=placed,
        out_specs=(
            rows,
            rows,
            P(),
            P("dp", "mp"),
            P("dp", "mp"),
            P("dp", "mp"),
            P(),
            P(),
            P("mp", "dp"),
            P(),
            P("dp", "mp"),
            P("dp", "mp"),
            P("mp", "dp"),
        ),
        check_vma=False,
    )
```

```python
import functools

import jax
import jax.numpy as jnp
from jax import lax
from jax.experimental import pallas as pl
from jax.experimental.pallas import tpu as pltpu
from jax.sharding import PartitionSpec as P

eps_norm = 1e-06
rope_base = 1000000.0
log2_e = 1.4426950408889634
bf16 = jnp.bfloat16
f32 = jnp.float32
longest = 2048
light_cost = pl.CostEstimate(flops=1 << 20, bytes_accessed=1 << 16, transcendentals=0)


def rms_scale(values):
    return lax.rsqrt(jnp.mean(values * values, axis=-1, keepdims=True) + eps_norm)


def norm_back(grad_hat, normed, scale_rows):
    return scale_rows * (grad_hat - normed * jnp.mean(grad_hat * normed, axis=-1, keepdims=True))


def mm(left, right):
    return jnp.dot(left, right, preferred_element_type=f32)


def mm_nt(left, right):
    return lax.dot_general(left, right, (((1,), (1,)), ((), ())), preferred_element_type=f32)


def mm_tn(left, right):
    return lax.dot_general(left, right, (((0,), (0,)), ((), ())), preferred_element_type=f32)


def load_pieces(refs, held_ref, sem_ref):
    rows = refs[0].shape[0]
    copies = [
        pltpu.make_async_copy(ref, held_ref.at[pl.ds(i * rows, rows), :], sem_ref.at[i])
        for i, ref in enumerate(refs)
    ]
    for copy in copies:
        copy.start()
    for copy in copies:
        copy.wait()


def gather_rows(src_ref, dst_ref, tok, repeat):
    dim = dst_ref.shape[1]
    for slot in range(src_ref.shape[0] // tok):
        for i in range(repeat):
            at = (slot * repeat + i) * tok
            dst_ref[at:at + tok] = src_ref[slot * tok:(slot + 1) * tok, i * dim:(i + 1) * dim]


def head_lanes(dim):
    head, heads = pl.program_id(0), pl.num_programs(0)
    return pl.ds(pl.multiple_of(head * dim, dim), dim), pl.ds(pl.multiple_of((heads + head) * dim, dim), dim)


def attn_fwd_kernel(flags_ref, base_ref, places_ref, q_ref, *refs, tok, sub, slots, blocks, pieces, repeat, head_dim):
    kv_refs, (o_ref, lse_ref, kv_ref, acc_ref, values_ref, rows_ref, sem_ref) = refs[:pieces], refs[pieces:]
    kb, chunk = tok * sub, tok * repeat
    k_lanes, v_lanes = head_lanes(head_dim)

    @pl.when(pl.program_id(0) == 0)
    def _():
        load_pieces(kv_refs, kv_ref, sem_ref)
        values_ref[:, head_dim:] = jnp.ones((kb, head_dim), bf16)

    gather_rows(q_ref, rows_ref, tok, repeat)
    acc_ref[...] = jnp.zeros_like(acc_ref)

    def run(block, keys, masked):
        values_ref[:, :head_dim] = kv_ref[keys, v_lanes]
        k = kv_ref[keys, k_lanes]
        for slot in range(slots):
            lines = slice(slot * chunk, (slot + 1) * chunk)
            p = jnp.exp2(mm_nt(rows_ref[lines], k))
            if masked:
                start, place = places_ref[lines, 0:1], places_ref[lines, 1:2]
                at = lax.broadcasted_iota(jnp.int32, (chunk, tok), 1)
                bases = [base_ref[block * sub + piece] for piece in range(sub)]
                allowed = jnp.concatenate([(at >= start - base) & (at <= place - base) for base in bases], axis=1)
                p = jnp.where(allowed, p, 0.0)
            acc_ref[lines] += mm(p.astype(bf16), values_ref[...])

    @pl.loop(0, blocks)
    def _(block):
        keys = pl.ds(pl.multiple_of(block * kb, kb), kb)
        pl.when(flags_ref[block] == 1)(lambda: run(block, keys, True))
        pl.when(flags_ref[block] == 2)(lambda: run(block, keys, False))

    for slot in range(slots):
        total = acc_ref[slot * chunk:(slot + 1) * chunk, head_dim:]
        out = acc_ref[slot * chunk:(slot + 1) * chunk, :head_dim] * (1.0 / total)
        for i in range(repeat):
            o_ref[slot * tok:(slot + 1) * tok, i * head_dim:(i + 1) * head_dim] = out[i * tok:(i + 1) * tok].astype(bf16)
        lse_ref[:, slot * chunk:(slot + 1) * chunk] = jnp.log2(total).T[:1]


def attn_bwd_kernel(flags_ref, base_ref, places_ref, q_ref, lse_ref, o_ref, do_ref, *refs, tok, sub, slots, blocks, pieces, repeat, head_dim, dq_scale, dk_scale):
    kv_refs = refs[:pieces]
    dq_ref, near_ref, far_ref, kv_ref, rows_ref, grads_ref, dqt_ref, delta_ref, dka_ref, dva_ref, sem_ref = refs[pieces:]
    kb, chunk = tok * sub, tok * repeat
    k_lanes, v_lanes = head_lanes(head_dim)

    @pl.when(pl.program_id(0) == 0)
    def _():
        load_pieces(kv_refs, kv_ref, sem_ref)

    gather_rows(q_ref, rows_ref, tok, repeat)
    gather_rows(do_ref, grads_ref, tok, repeat)
    dqt_ref[...] = jnp.zeros_like(dqt_ref)
    for slot in range(slots):
        for i in range(repeat):
            lines, lanes = slice(slot * tok, (slot + 1) * tok), slice(i * head_dim, (i + 1) * head_dim)
            prod = do_ref[lines, lanes].astype(f32) * o_ref[lines, lanes].astype(f32)
            at = (slot * repeat + i) * tok
            delta_ref[:, at:at + tok] = jnp.sum(prod.T, axis=0, keepdims=True)

    def run(block, keys, masked):
        k = kv_ref[keys, k_lanes]
        v = kv_ref[keys, v_lanes]
        kt = k.T
        for slot in range(slots):
            lanes = slice(slot * chunk, (slot + 1) * chunk)
            q = rows_ref[lanes]
            do = grads_ref[lanes]
            p = jnp.exp2(mm_nt(k, q) - lse_ref[:, lanes])
            if masked:
                start, place = places_ref[0:1, lanes], places_ref[1:2, lanes]
                at = lax.broadcasted_iota(jnp.int32, (tok, chunk), 0)
                bases = [base_ref[block * sub + piece] for piece in range(sub)]
                allowed = jnp.concatenate([(at >= start - base) & (at <= place - base) for base in bases], axis=0)
                p = jnp.where(allowed, p, 0.0)
            ds = (p * (mm_nt(v, do) - delta_ref[:, lanes])).astype(bf16)
            dva_ref[...] += mm(p.astype(bf16), do)
            dka_ref[...] += mm(ds, q)
            dqt_ref[:, lanes] += mm(kt, ds)

    @pl.loop(0, blocks)
    def _(block):
        keys = pl.ds(pl.multiple_of(block * kb, kb), kb)
        dka_ref[...] = jnp.zeros_like(dka_ref)
        dva_ref[...] = jnp.zeros_like(dva_ref)
        pl.when(flags_ref[block] == 1)(lambda: run(block, keys, True))
        pl.when(flags_ref[block] == 2)(lambda: run(block, keys, False))

        @pl.when(block < blocks // 2)
        def _():
            near_ref[keys, k_lanes] = (dka_ref[...] * dk_scale).astype(bf16)
            near_ref[keys, v_lanes] = dva_ref[...].astype(bf16)

        @pl.when(block >= blocks // 2)
        def _():
            far = pl.ds(pl.multiple_of(block * kb - blocks // 2 * kb, kb), kb)
            far_ref[far, k_lanes] = (dka_ref[...] * dk_scale).astype(bf16)
            far_ref[far, v_lanes] = dva_ref[...].astype(bf16)

    for slot in range(slots):
        out = (dqt_ref[:, slot * chunk:(slot + 1) * chunk] * dq_scale).T
        for i in range(repeat):
            dq_ref[slot * tok:(slot + 1) * tok, i * head_dim:(i + 1) * head_dim] = out[i * tok:(i + 1) * tok]


def turn(values):
    half = values.shape[-1] // 2
    return jnp.concatenate([values[:, half:], values[:, :half]], axis=1)


def ignoring(kernel, at, count):
    def reduced(*refs):
        kernel(*refs[:at], *refs[at + count:])

    return reduced


any_place = pl.BlockSpec(memory_space=pl.ANY)


def rotated_heads(raw, cos_ref, sin_ref, gain_ref, out_ref, head_dim, scale):
    for first in range(0, raw.shape[1], head_dim):
        lanes = slice(first, first + head_dim)
        hat = raw[:, lanes] * rms_scale(raw[:, lanes]) * gain_ref[...]
        out_ref[:, lanes] = ((hat * cos_ref[...] + turn(hat) * sin_ref[...]) * scale).astype(bf16)


def project_kv_kernel(w_ref, cos_ref, sin_ref, gain_ref, norm_ref, *refs, head_dim):
    *slot_refs, x_ref, rows_ref, raw_ref, out_ref = refs
    tok = slot_refs[0].shape[0]
    step = pl.program_id(0)

    @pl.when(step == 0)
    def _():
        for slot, slot_ref in enumerate(slot_refs):
            lines = slice(slot * tok, (slot + 1) * tok)
            values = slot_ref[...].astype(f32)
            scale = rms_scale(values)
            x_ref[lines] = (values * scale * norm_ref[...]).astype(bf16)
            rows_ref[lines] = jnp.broadcast_to(scale, (tok, rows_ref.shape[1]))

    raw = mm(x_ref[...], w_ref[...])

    @pl.when(step == 0)
    def _():
        raw_ref[...] = raw
        rotated_heads(raw, cos_ref, sin_ref, gain_ref, out_ref, head_dim, 1.0)

    @pl.when(step == 1)
    def _():
        out_ref[...] = raw.astype(bf16)


def project_kv(slots, norm, w, cos_table, sin_table, gain, first, tile):
    tok, width = slots[0].shape
    tokens, head_dim = tok * len(slots), gain.shape[1]

    def whole(rows, cols):
        return pl.BlockSpec((rows, cols), lambda j: (0, 0))

    w_spec = pl.BlockSpec((width, tile), lambda j: (0, j + first))
    return pl.pallas_call(
        functools.partial(project_kv_kernel, head_dim=head_dim),
        grid=(2,),
        in_specs=[w_spec, whole(tokens, head_dim), whole(tokens, head_dim), whole(1, head_dim), whole(1, width)]
        + [whole(tok, width)] * len(slots),
        out_specs=[whole(tokens, width), whole(tokens, head_dim), whole(tokens, tile), pl.BlockSpec((tokens, tile), lambda j: (0, j))],
        out_shape=[
            jax.ShapeDtypeStruct((tokens, width), bf16),
            jax.ShapeDtypeStruct((tokens, head_dim), f32),
            jax.ShapeDtypeStruct((tokens, tile), f32),
            jax.ShapeDtypeStruct((tokens, 2 * tile), bf16),
        ],
        cost_estimate=light_cost,
        name="project_kv",
    )(w, cos_table, sin_table, gain, norm, *slots)


def project_q_kernel(x_ref, w_ref, cos_ref, sin_ref, gain_ref, raw_ref, out_ref, *, head_dim, scale):
    raw = mm(x_ref[...], w_ref[...])
    raw_ref[...] = raw
    rotated_heads(raw, cos_ref, sin_ref, gain_ref, out_ref, head_dim, scale)


def project_q(x, w, cos_table, sin_table, gain, cols, tile, scale, after):
    tokens, width = x.shape
    head_dim = gain.shape[1]

    def whole(rows, cols):
        return pl.BlockSpec((rows, cols), lambda j: (0, 0))

    w_spec = pl.BlockSpec((width, tile), lambda j: (0, j))
    out_spec = pl.BlockSpec((tokens, tile), lambda j: (0, j))
    return pl.pallas_call(
        ignoring(functools.partial(project_q_kernel, head_dim=head_dim, scale=scale), 5, len(after)),
        grid=(cols // tile,),
        in_specs=[whole(tokens, width), w_spec, whole(tokens, head_dim), whole(tokens, head_dim), whole(1, head_dim)] + [any_place] * len(after),
        out_specs=[out_spec, out_spec],
        out_shape=[jax.ShapeDtypeStruct((tokens, cols), f32), jax.ShapeDtypeStruct((tokens, cols), bf16)],
        cost_estimate=light_cost,
        name="project_q",
    )(x, w, cos_table, sin_table, gain, *after)


def unproject_kernel(raw_ref, cos_ref, sin_ref, gain_ref, *refs, head_dim, sums):
    grad_refs, (out_ref, part_ref) = refs[:sums], refs[sums:]
    part = jnp.zeros((1, head_dim), f32)
    for first in range(0, out_ref.shape[1], head_dim):
        lanes = slice(first, first + head_dim)
        grad = grad_refs[0][:, lanes].astype(f32)
        for grad_ref in grad_refs[1:]:
            grad = grad + grad_ref[:, lanes].astype(f32)
        if first < raw_ref.shape[1]:
            raw = raw_ref[:, lanes]
            scale = rms_scale(raw)
            hat = raw * scale
            grad = grad * cos_ref[...] - turn(grad) * sin_ref[...]
            part = part + jnp.sum(grad * hat, axis=0, keepdims=True)
            grad = norm_back(grad * gain_ref[...], hat, scale)
        out_ref[:, lanes] = grad.astype(bf16)
    part_ref[...] = part


def unproject(raw, cos_table, sin_table, gain, grads, after, name):
    tokens, cols = raw.shape[0], grads[0].shape[1]
    head_dim = gain.shape[1]

    def first_rows(width):
        return pl.BlockSpec((tokens, width), lambda j: (0, 0))

    gain_spec = pl.BlockSpec((1, head_dim), lambda j: (0, 0))
    return pl.pallas_call(
        ignoring(functools.partial(unproject_kernel, head_dim=head_dim, sums=len(grads)), 4 + len(grads), len(after)),
        grid=(1,),
        in_specs=[first_rows(raw.shape[1]), first_rows(head_dim), first_rows(head_dim), gain_spec]
        + [first_rows(cols)] * len(grads)
        + [any_place] * len(after),
        out_specs=[first_rows(cols), gain_spec],
        out_shape=[
            jax.ShapeDtypeStruct((tokens, cols), bf16),
            jax.ShapeDtypeStruct(gain.shape, f32),
        ],
        cost_estimate=light_cost,
        name=name,
    )(raw, cos_table, sin_table, gain, *grads, *after)


def attn_back_kernel(dq_ref, dkv_ref, w_ref, rows_ref, *refs, slots):
    hidden_refs, out_refs, gain_ref = refs[:slots], refs[slots:-1], refs[-1]
    q_cols = dq_ref.shape[1]
    tok = out_refs[0].shape[0]
    total = mm_nt(dq_ref[...], w_ref[:, :q_cols]) + mm_nt(dkv_ref[...], w_ref[:, q_cols:])
    gain = jnp.zeros((1, total.shape[1]), f32)
    for slot in range(slots):
        lines = slice(slot * tok, (slot + 1) * tok)
        part = total[lines]
        gain = gain + jnp.sum(part * (hidden_refs[slot][...].astype(f32) * rows_ref[lines, :1]), axis=0, keepdims=True)
        out_refs[slot][...] = part.astype(bf16)
    gain_ref[...] = jnp.broadcast_to(gain, gain_ref.shape)


def attn_back_product(dq, dkv, w, row_scales, hidden_slots, after):
    rows, q_cols = dq.shape
    slots = len(hidden_slots)
    tok, width = hidden_slots[0].shape
    tile = min(512, width)
    slot_spec = pl.BlockSpec((tok, tile), lambda t: (0, t))
    return pl.pallas_call(
        ignoring(functools.partial(attn_back_kernel, slots=slots), 4 + slots, len(after)),
        grid=(width // tile,),
        in_specs=[
            pl.BlockSpec((rows, q_cols), lambda t: (0, 0)),
            pl.BlockSpec((rows, dkv.shape[1]), lambda t: (0, 0)),
            pl.BlockSpec((tile, q_cols + dkv.shape[1]), lambda t: (t, 0)),
            pl.BlockSpec(row_scales.shape, lambda t: (0, 0)),
        ]
        + [slot_spec] * slots
        + [any_place] * len(after),
        out_specs=[slot_spec] * slots + [pl.BlockSpec((8, tile), lambda t: (0, t))],
        out_shape=[jax.ShapeDtypeStruct((tok, width), bf16)] * slots + [jax.ShapeDtypeStruct((8, width), f32)],
        cost_estimate=light_cost,
        name="attn_back",
    )(dq, dkv, w, row_scales, *hidden_slots, *after)


def grad_attended_kernel(w_ref, *refs):
    *slot_refs, mid_ref, out_ref = refs
    tok = slot_refs[0].shape[0]
    for slot, slot_ref in enumerate(slot_refs):
        mid_ref[slot * tok:(slot + 1) * tok] = slot_ref[...]
    out_ref[...] = mm(mid_ref[...], w_ref[...]).astype(bf16)


def grad_attended_product(slots, w, cols, after):
    tok, width = slots[0].shape
    rows = tok * len(slots)

    def whole(rows, cols):
        return pl.BlockSpec((rows, cols), lambda j: (0, 0))

    return pl.pallas_call(
        ignoring(grad_attended_kernel, 1 + len(slots), len(after)),
        grid=(1,),
        in_specs=[pl.BlockSpec((width, cols), lambda j: (0, w.shape[1] // cols - 1))] + [whole(tok, width)] * len(slots) + [any_place] * len(after),
        out_specs=[whole(rows, width), whole(rows, cols)],
        out_shape=[jax.ShapeDtypeStruct((rows, width), bf16), jax.ShapeDtypeStruct((rows, cols), bf16)],
        cost_estimate=light_cost,
        name="grad_attended",
    )(w, *slots, *after)


def simple_call(kernel, arrays, shapes, name, after=()):
    vmem = pl.BlockSpec(memory_space=pltpu.VMEM)
    return pl.pallas_call(
        ignoring(kernel, len(arrays), len(after)),
        in_specs=[vmem] * len(arrays) + [any_place] * len(after),
        out_specs=[vmem] * len(shapes),
        out_shape=[jax.ShapeDtypeStruct(shape, dtype) for shape, dtype in shapes],
        cost_estimate=light_cost,
        name=name,
    )(*arrays, *after)


def add_rounded(left, right):
    return (left.astype(f32) + right.astype(f32)).astype(bf16)


def summed(refs):
    count = len(refs) // 2
    return jnp.concatenate(
        [came[...].astype(f32) + part[...].astype(f32) for came, part in zip(refs[:count], refs[count:])],
        axis=0,
    )


def store_halves(values, refs):
    rows = refs[0].shape[0]
    for i, ref in enumerate(refs):
        ref[...] = values[i * rows:(i + 1) * rows].astype(ref.dtype)


def mix_kernel(*refs, halves):
    sum_refs, (hidden_ref, norm_ref, mixed_ref, *input_refs) = refs[:2 * halves], refs[2 * halves:]
    mixed = hidden_ref[...].astype(f32) + summed(sum_refs)
    mixed_ref[...] = mixed
    store_halves(mixed * rms_scale(mixed) * norm_ref[...], input_refs)


def mid_kernel(*refs, halves):
    sum_refs, (mixed_ref, norm_ref, out_ref, grad_ref, gain_ref, *low_refs) = refs[:2 * halves], refs[2 * halves:]
    mixed = mixed_ref[...]
    scale = rms_scale(mixed)
    normed = mixed * scale
    back = summed(sum_refs)
    gain_ref[...] = jnp.sum(back * normed, axis=0, keepdims=True)
    grad = out_ref[...].astype(f32) + norm_back(back * norm_ref[...], normed, scale)
    grad_ref[...] = grad
    store_halves(grad, low_refs)


def last_kernel(*refs, halves):
    sum_refs, (grad_ref, hidden_ref, norm_ref, out_ref) = refs[:2 * halves], refs[2 * halves:]
    hidden = hidden_ref[...].astype(f32)
    scale = rms_scale(hidden)
    out_ref[...] = grad_ref[...] + norm_back(summed(sum_refs) * norm_ref[...], hidden * scale, scale)


def result_kernel(*refs):
    *sum_refs, mixed_ref, out_ref = refs
    total = sum_refs[0][...].astype(f32)
    for sum_ref in sum_refs[1:]:
        total = total + sum_ref[...].astype(f32)
    out_ref[...] = (mixed_ref[...] + total).astype(bf16)


def mark_kernel(out_ref):
    out_ref[...] = jnp.zeros_like(out_ref)


def ffn_kernel(gate_ref, up_ref, down_ref, *refs, parts, held):
    x_refs, g_refs, refs = refs[:parts], refs[parts:2 * parts], refs[2 * parts + held:]
    grad_ref, x_ref, go_ref, *back_refs, back_ref = refs
    tile = pl.program_id(0)
    tok, size = x_refs[0].shape[0], gate_ref.shape[1]
    ff = grad_ref.shape[1] // 3

    @pl.when(tile == 0)
    def _():
        for i in range(parts):
            x_ref[i * tok:(i + 1) * tok] = x_refs[i][...]
            go_ref[i * tok:(i + 1) * tok] = g_refs[i][...]
        back_ref[...] = jnp.zeros_like(back_ref)

    x = x_ref[...]
    gate_pre = mm(x, gate_ref[...])
    up_value = mm(x, up_ref[...])
    grad_act = mm(go_ref[...], down_ref[...])
    sigmoid_gate = jax.nn.sigmoid(gate_pre)
    gated = gate_pre * sigmoid_gate
    grad_gate_pre = (
        grad_act * up_value * sigmoid_gate * (1.0 + gate_pre * (1.0 - sigmoid_gate))
    ).astype(bf16)
    grad_up_value = (grad_act * gated).astype(bf16)
    for i, values in enumerate([grad_gate_pre, grad_up_value, (gated * up_value).astype(bf16)]):
        grad_ref[:, pl.ds(pl.multiple_of(i * ff + tile * size, size), size)] = values
    back_ref[...] += mm_nt(grad_gate_pre, gate_ref[...]) + mm_nt(grad_up_value, up_ref[...])

    @pl.when(tile == pl.num_programs(0) - 1)
    def _():
        store_halves(back_ref[...], back_refs)


def feed_forward(inputs, grads, w_ffn, held, chunk, chunks):
    parts = len(inputs)
    tok, width = inputs[0].shape
    ff = w_ffn.shape[1] // 3
    size = next(s for s in (512, 384, 256, 128) if ff % s == 0)
    tiles = ff // size
    part_spec = pl.BlockSpec((tok, width), lambda t: (0, 0))

    def rows_spec(cols):
        return pl.BlockSpec((parts * tok, cols), lambda t: (chunk, 0))

    rows = parts * tok * chunks
    return pl.pallas_call(
        functools.partial(ffn_kernel, parts=parts, held=len(held)),
        grid=(tiles,),
        in_specs=[
            pl.BlockSpec((width, size), lambda t: (0, t)),
            pl.BlockSpec((width, size), lambda t: (0, tiles + t)),
            pl.BlockSpec((width, size), lambda t: (0, 2 * tiles + t)),
        ]
        + [part_spec] * (2 * parts)
        + [pl.BlockSpec(memory_space=pl.ANY)] * len(held),
        out_specs=[rows_spec(3 * ff), rows_spec(width), rows_spec(width)] + [part_spec] * parts,
        out_shape=[
            jax.ShapeDtypeStruct((rows, 3 * ff), bf16),
            jax.ShapeDtypeStruct((rows, width), bf16),
            jax.ShapeDtypeStruct((rows, width), bf16),
        ]
        + [jax.ShapeDtypeStruct((tok, width), bf16)] * parts,
        scratch_shapes=[pltpu.VMEM((parts * tok, width), f32)],
        input_output_aliases={3 + 2 * parts + i: i for i in range(len(held))},
        cost_estimate=light_cost,
        name="feed_forward",
    )(w_ffn, w_ffn, w_ffn, *inputs, *grads, *held)


def weight_grads_kernel(*refs, turns):
    *left_refs, right_ref, out_ref, turned_ref = refs
    tile = pl.program_id(0)
    for left_ref, at in zip(left_refs, turns):
        @pl.when(tile == at)
        def _(left_ref=left_ref):
            turned_ref[...] = left_ref[...].T

    rows = min(256, out_ref.shape[0])
    for first in range(0, out_ref.shape[0], rows):
        lines = slice(first, first + rows)
        out_ref[lines] = mm(turned_ref[lines], right_ref[...]).astype(bf16)


def weight_grads(lefts, right, starts, after, name):
    tokens, width = lefts[0].shape
    cols = right.shape[1]
    size = next(s for s in (512, 384, 256, 128) if all(at % s == 0 for at in (cols, *starts)))
    whole = pl.BlockSpec((tokens, width), lambda t: (0, 0))
    return pl.pallas_call(
        ignoring(functools.partial(weight_grads_kernel, turns=[at // size for at in starts]), len(lefts) + 1, len(after)),
        grid=(cols // size,),
        in_specs=[whole] * len(lefts) + [pl.BlockSpec((tokens, size), lambda t: (0, t))] + [any_place] * len(after),
        out_specs=pl.BlockSpec((width, size), lambda t: (0, t)),
        out_shape=jax.ShapeDtypeStruct((width, cols), bf16),
        scratch_shapes=[pltpu.VMEM((width, tokens), bf16)],
        cost_estimate=light_cost,
        name=name,
    )(*lefts, right, *after)


def slot_product_kernel(x_ref, w_ref, *out_refs):
    tok = out_refs[0].shape[0]
    total = mm_nt(x_ref[...], w_ref[...])
    for slot, out_ref in enumerate(out_refs):
        out_ref[...] = total[slot * tok:(slot + 1) * tok].astype(bf16)


def slot_product(x, x_block, w, w_block, depth, slots, after, name):
    rows, width = x.shape[0], w.shape[0]
    tile = min(512, width)
    out_spec = pl.BlockSpec((rows // slots, tile), lambda t: (0, t))
    return pl.pallas_call(
        ignoring(slot_product_kernel, 2, len(after)),
        grid=(width // tile,),
        in_specs=[
            pl.BlockSpec((rows, depth), lambda t: (0, x_block)),
            pl.BlockSpec((tile, depth), lambda t: (t, w_block)),
        ]
        + [any_place] * len(after),
        out_specs=[out_spec] * slots,
        out_shape=[jax.ShapeDtypeStruct((rows // slots, width), bf16)] * slots,
        cost_estimate=light_cost,
        name=name,
    )(x, w, *after)


def more_grads_kernel(left_ref, *refs, rights):
    right_refs, out_ref, turned_ref = refs[:rights], refs[-2], refs[-1]
    tile = pl.program_id(0)

    @pl.when(tile == 0)
    def _():
        turned_ref[...] = left_ref[...].T

    def run(right_ref):
        rows = min(256, out_ref.shape[0])
        for first in range(0, out_ref.shape[0], rows):
            lines = slice(first, first + rows)
            out_ref[lines] = mm(turned_ref[lines], right_ref[...]).astype(bf16)

    for i, right_ref in enumerate(right_refs):
        pl.when(tile == i)(functools.partial(run, right_ref))


def more_grads(left, rights, held, at, blocks, after, name):
    tokens, width = left.shape
    size = rights[0].shape[1]
    return pl.pallas_call(
        ignoring(functools.partial(more_grads_kernel, rights=len(rights)), 1 + len(rights), len(held) + len(after)),
        grid=(len(rights),),
        in_specs=[pl.BlockSpec((tokens, width), lambda t: (0, 0))]
        + [pl.BlockSpec((tokens, size), lambda t: (0, 0))] * len(rights)
        + [any_place] * (len(held) + len(after)),
        out_specs=pl.BlockSpec((width, size), lambda t: (0, at + t)),
        out_shape=jax.ShapeDtypeStruct((width, blocks * size), bf16),
        scratch_shapes=[pltpu.VMEM((width, tokens), bf16)],
        input_output_aliases={1 + len(rights) + i: 0 for i in range(len(held))},
        cost_estimate=light_cost,
        name=name,
    )(left, *rights, *held, *after)


def fold_kernel(near_ref, got_ref, *out_refs):
    rows = out_refs[0].shape[0]
    for i, out_ref in enumerate(out_refs):
        lines = slice((i + 1) * rows, (i + 2) * rows)
        out_ref[...] = (near_ref[lines].astype(f32) + got_ref[lines].astype(f32)).astype(bf16)


def fold_blocks(near, got, count, after):
    vmem = pl.BlockSpec(memory_space=pltpu.VMEM)
    shape = jax.ShapeDtypeStruct((near.shape[0] // count, near.shape[1]), bf16)
    return pl.pallas_call(
        ignoring(fold_kernel, 2, len(after)),
        in_specs=[vmem, vmem] + [any_place] * len(after),
        out_specs=[vmem] * (count - 1),
        out_shape=[shape] * (count - 1),
        cost_estimate=light_cost,
        name="fold_blocks",
    )(near, got, *after)


def body(
    hidden_in,
    doc_lengths,
    attn_norm,
    query_weight,
    key_weight,
    value_weight,
    query_gain,
    key_gain,
    output_weight,
    ffn_norm,
    gate_weight,
    up_weight,
    down_weight,
    grad_out,
):
    dp_count = lax.axis_size("dp")
    mp_count = lax.axis_size("mp")
    slots = mp_count
    tok, width = hidden_in.shape
    group_rows = tok * mp_count
    head_dim = query_gain.shape[0]
    half_dim = head_dim // 2
    q_cols = query_weight.shape[1]
    k_cols = key_weight.shape[1]
    kv_local = k_cols // head_dim
    repeat = q_cols // k_cols
    ff = gate_weight.shape[1]
    group = lax.axis_index("dp")
    my_z = lax.axis_index("mp")
    score_scale = head_dim ** (-0.5)
    ring = [(i, (i + 1) % mp_count) for i in range(mp_count)]
    near_masks = list(range(0, dp_count, 2))
    masks = near_masks + [mask + 1 for mask in near_masks]
    far_masks = near_masks[1:]

    def tie(value, *others):
        return lax.optimization_barrier((value,) + others)[0]

    def shift(values):
        return lax.ppermute(values, "mp", ring)

    def swap(values, mask):
        return lax.ppermute(values, "dp", [(i, i ^ mask) for i in range(dp_count)])

    reach = (min(longest, group_rows * dp_count) - 2) // group_rows + 1

    def needs(reader, owner):
        first = reader // 2 * 2
        return owner <= first + 1 and owner >= first - reach

    def swap_forward(values, mask):
        pairs = [(i, i ^ mask) for i in range(dp_count) if needs(i ^ mask, i)]
        return lax.ppermute(values, "dp", pairs)

    def swap_back(values, mask):
        pairs = [(i, i ^ mask) for i in range(dp_count) if needs(i, i ^ mask)]
        return lax.ppermute(values, "dp", pairs)

    half = dp_count // 2
    halves = 2
    part_rows = tok // halves
    ids = jnp.array(masks, jnp.int32)
    mask_blocks = group ^ ids
    attn_norm = attn_norm.reshape(1, width)
    ffn_norm = ffn_norm.reshape(1, width)
    part_shape = ((part_rows, width), bf16)

    def tie_all(values, *others):
        return list(lax.optimization_barrier((*values, *others)))[:len(values)]

    def order(values, others):
        both = lax.optimization_barrier((*values, *others))
        return list(both[:len(values)]), list(both[len(values):])

    def mark(*operands):
        (tiny,) = simple_call(mark_kernel, [], [((8, 128), f32)], "mark", operands)
        return [swap(tiny, 1)]

    def flat(slot_lists):
        return [part for slot in slot_lists for part in slot]

    def by_slot(parts):
        return [list(parts[i:i + halves]) for i in range(0, len(parts), halves)]

    def shift_all(parts):
        return [shift(part) for part in parts]

    def ring_add(came, own):
        return [shift(add_rounded(one, other)) for one, other in zip(came, own)]

    w_attn_own = jnp.concatenate([query_weight, key_weight, value_weight, output_weight.T], axis=1)
    w_ffn_own = jnp.concatenate([gate_weight, up_weight, down_weight.T], axis=1)
    w_attn = lax.all_gather(w_attn_own, "dp", axis=0, tiled=True)
    w_ffn = tie(lax.all_gather(w_ffn_own, "dp", axis=0, tiled=True), w_attn)

    doc_ends = jnp.cumsum(doc_lengths)
    slot_offset = ((my_z - jnp.arange(slots, dtype=jnp.int32)) % mp_count) * tok
    places = (
        group * group_rows
        + slot_offset[:, None]
        + jnp.arange(tok, dtype=jnp.int32)[None, :]
    )
    before = doc_ends[None, None, :] <= places[:, :, None]
    starts = jnp.sum(jnp.where(before, doc_lengths[None, None, :], 0), axis=-1)
    position = (places - starts).reshape(group_rows)
    inverse = rope_base ** (-(2.0 * jnp.arange(half_dim, dtype=f32)) / head_dim)
    angles = position.astype(f32)[:, None] * inverse[None, :]
    cos_table, sin_table = jnp.cos(angles), jnp.sin(angles)
    cos_table = jnp.concatenate([cos_table, cos_table], axis=1)
    sin_table = jnp.concatenate([-sin_table, sin_table], axis=1)

    sub = min(4, slots)
    key_base = mask_blocks[:, None] * group_rows + slot_offset[None, :]
    blocks = dp_count * slots // sub
    key_base = key_base.reshape(blocks, sub)
    q_first, q_last = places[:, 0], places[:, -1]
    s_first, s_last = starts[:, 0], starts[:, -1]
    piece_lo, piece_hi = key_base[None], key_base[None] + tok - 1
    some = (piece_lo <= q_last[:, None, None]) & (s_first[:, None, None] <= piece_hi)
    every = (piece_hi <= q_first[:, None, None]) & (s_last[:, None, None] <= piece_lo)
    flags = jnp.where(jnp.all(every, -1), 2, jnp.any(some, -1).astype(jnp.int32)).astype(jnp.int32)
    flags = jnp.where(jnp.all(flags == 2, axis=0), 2, jnp.any(flags > 0, axis=0).astype(jnp.int32))
    key_base = key_base.reshape(-1)
    lane_places = jnp.tile(jnp.stack([starts, places]), (1, 1, repeat)).reshape(2, -1)
    row_places = lane_places.T

    hidden_slots = [[hidden_in[i * part_rows:(i + 1) * part_rows] for i in range(halves)]]
    for slot in range(1, slots):
        came = shift_all(hidden_slots[-1])
        if slot == 1:
            came = tie_all(came, cos_table, sin_table, lane_places, w_ffn_own)
        hidden_slots.append(came)
    q_gain, k_gain = query_gain.reshape(1, head_dim), key_gain.reshape(1, head_dim)
    attn_input, row_scales, key_raw, kv_own = project_kv(
        flat(hidden_slots), attn_norm, w_attn, cos_table, sin_table, k_gain, repeat, k_cols
    )
    kv_came = [swap_forward(kv_own, mask) for mask in far_masks]
    grad_slots = [tie_all([grad_out[i * part_rows:(i + 1) * part_rows] for i in range(halves)], *hidden_slots[-1])]
    grad_slots.append(tie_all(shift_all(grad_slots[-1]), kv_own))
    query_raw, query_rot = project_q(
        tie(attn_input, kv_own, *grad_slots[-1]), w_attn, cos_table, sin_table, q_gain, q_cols, k_cols,
        score_scale * log2_e, [],
    )
    for slot in range(2, slots):
        came = shift_all(grad_slots[-1])
        if slot == 2:
            came = tie_all(came, query_rot)
            kv_came = tie_all(kv_came, *came)
        grad_slots.append(came)
    kv_near = [kv_own] + tie_all(kv_came, query_rot)
    kv_pieces = kv_near + [swap(piece, 1) for piece in kv_near]

    keys_total = dp_count * group_rows
    head_rows = repeat * tok
    smem = pl.BlockSpec(memory_space=pltpu.SMEM)
    any_spec = pl.BlockSpec(memory_space=pl.ANY)
    all_rows = slots * head_rows
    lane_spec = pl.BlockSpec((2, all_rows), lambda h: (0, 0))
    row_spec = pl.BlockSpec((all_rows, 2), lambda h: (0, 0))
    q_spec = pl.BlockSpec((group_rows, repeat * head_dim), lambda h: (0, h))
    lse_spec = pl.BlockSpec((None, 1, all_rows), lambda h: (h, 0, 0))
    dims = dict(
        tok=tok, sub=sub, slots=slots, blocks=blocks, pieces=dp_count, repeat=repeat, head_dim=head_dim
    )
    kv_scratch = pltpu.VMEM((keys_total, 2 * k_cols), bf16)
    attended_low, lse = pl.pallas_call(
        functools.partial(attn_fwd_kernel, **dims),
        grid=(kv_local,),
        in_specs=[smem, smem, row_spec, q_spec] + [any_spec] * dp_count,
        out_specs=[q_spec, lse_spec],
        out_shape=[
            jax.ShapeDtypeStruct((group_rows, q_cols), bf16),
            jax.ShapeDtypeStruct((kv_local, 1, all_rows), f32),
        ],
        scratch_shapes=[
            kv_scratch,
            pltpu.VMEM((all_rows, 2 * head_dim), f32),
            pltpu.VMEM((tok * sub, 2 * head_dim), bf16),
            pltpu.VMEM((all_rows, head_dim), bf16),
            pltpu.SemaphoreType.DMA((dp_count,)),
        ],
        cost_estimate=light_cost,
        name="attn_fwd",
    )(flags, key_base, row_places, query_rot, *kv_pieces)

    grad_slots[slots - 1] = tie_all(grad_slots[slots - 1], attended_low)
    parts = by_slot(slot_product(attended_low, 0, w_attn, 2 * k_cols // q_cols + 1, q_cols, slots * halves, [], "attn_out"))
    came = shift_all(tie_all(parts[1], *grad_slots[-1]))
    for slot in range(2, slots):
        came = ring_add(came, parts[slot])
    mixed_rows, *ffn_input = simple_call(
        functools.partial(mix_kernel, halves=halves),
        [*came, *parts[0], hidden_in, ffn_norm],
        [((tok, width), f32)] + [part_shape] * halves,
        "mix",
    )

    ffn_slots = [ffn_input, shift_all(ffn_input)]
    held, parts = [], []
    for first in range(0, slots, 2):
        *held, = feed_forward(
            flat(ffn_slots[first:first + 2]), flat(grad_slots[first:first + 2]), w_ffn, held, first // 2, slots // 2
        )
        held, back = held[:3], held[3:]
        parts += by_slot(back)
        if first + 2 < slots:
            ffn_slots.append(tie_all(shift_all(ffn_slots[-1]), *back))
            ffn_slots.append(shift_all(ffn_slots[-1]))
    ffn_right, ffn_all, grad_all = held

    came = shift_all(tie_all(parts[1], *ffn_slots[-1]))
    ffn_part = weight_grads([ffn_all, grad_all], tie(ffn_right, *came), [0, 2 * ff], [], "ffn_grads")
    for slot in range(2, slots):
        came = ring_add(came, parts[slot])
        if slot == 2:
            came = tie_all(came, ffn_part)
    grad_ffn = lax.psum_scatter(ffn_part, "dp", scatter_dimension=0, tiled=True)
    grad_mixed, grad_ffn_norm, *mid_first = simple_call(
        functools.partial(mid_kernel, halves=halves),
        [*came, *parts[0], mixed_rows, ffn_norm, grad_out],
        [((tok, width), f32), ((1, width), f32)] + [part_shape] * halves,
        "mid",
    )
    mid_slots = [mid_first]
    result_parts = slot_product(ffn_right, 2, w_ffn, 2, ff, slots, [], "ffn_out")
    for slot in range(1, slots):
        came = shift_all(mid_slots[-1])
        mid_slots.append(came)

    result_came = [
        lax.ppermute(result_parts[slot], "mp", [(i, (i - slot) % mp_count) for i in range(mp_count)])
        for slot in range(1, slots)
    ]

    grad_mid, grad_attended = grad_attended_product(flat(mid_slots), w_attn, q_cols, [])
    near_spec = pl.BlockSpec((keys_total // 2, 2 * k_cols), lambda h: (0, 0))
    near_shape = jax.ShapeDtypeStruct((keys_total // 2, 2 * k_cols), bf16)
    dq_rot, dkv_near, dkv_far = pl.pallas_call(
        functools.partial(
            attn_bwd_kernel, **dims, dq_scale=score_scale, dk_scale=1.0 / log2_e
        ),
        grid=(kv_local,),
        in_specs=[smem, smem, lane_spec, q_spec, lse_spec, q_spec, q_spec] + [any_spec] * dp_count,
        out_specs=[q_spec, near_spec, near_spec],
        out_shape=[jax.ShapeDtypeStruct((group_rows, q_cols), f32), near_shape, near_shape],
        scratch_shapes=[
            kv_scratch,
            pltpu.VMEM((all_rows, head_dim), bf16),
            pltpu.VMEM((all_rows, head_dim), bf16),
            pltpu.VMEM((head_dim, all_rows), f32),
            pltpu.VMEM((1, all_rows), f32),
            pltpu.VMEM((tok * sub, head_dim), f32),
            pltpu.VMEM((tok * sub, head_dim), f32),
            pltpu.SemaphoreType.DMA((dp_count,)),
        ],
        cost_estimate=light_cost,
        name="attn_bwd",
    )(flags, key_base, lane_places, query_rot, lse, attended_low, grad_attended, *kv_pieces)

    dkv_got = swap(dkv_far, 1)
    dkv_sent = fold_blocks(dkv_near, dkv_got, half, [])
    dkv_came = [swap_back(sent, mask) for sent, mask in zip(dkv_sent, far_masks)]
    marked = mark(*dkv_sent)
    dq_raw, query_gain_part = unproject(query_raw, cos_table, sin_table, q_gain, [dq_rot], marked, "unproject_q")
    attn_part = more_grads(grad_mid, [attended_low], [], 2, 3, marked, "out_grads")
    dkv_raw, key_gain_part = unproject(
        key_raw, cos_table, sin_table, k_gain, [dkv_near, dkv_got] + dkv_came, [attn_part, *result_came], "unproject_kv"
    )

    attn_part = more_grads(attn_input, [dq_raw, dkv_raw], [attn_part], 0, 3, [grad_ffn], "qkv_grads")
    grad_attn = lax.psum_scatter(attn_part, "dp", scatter_dimension=0, tiled=True)
    *parts, attn_gain_part = attn_back_product(
        dq_raw, dkv_raw, w_attn, row_scales, flat(hidden_slots), [attn_part]
    )
    parts = by_slot(parts)
    came = shift_all(parts[1])
    came, (attn_gain_part,) = order(came, [attn_gain_part])
    small = jnp.concatenate(
        [attn_gain_part[0], grad_ffn_norm[0], query_gain_part[0], key_gain_part[0]]
    ).reshape(-1, head_dim)
    small = small + swap(small, 1)
    for slot in range(2, slots):
        came = ring_add(came, parts[slot])
        if slot == 2:
            came, (small,) = order(came, [small])
            small = small + sum(swap(small, mask) for mask in far_masks)
    came, (small,) = order(came, [small])
    turns = [[(i, (i + by) % mp_count) for i in range(mp_count)] for by in range(1, mp_count)]
    small = small + sum(lax.ppermute(small, "mp", turn) for turn in turns)
    (grad_hidden,) = simple_call(
        functools.partial(last_kernel, halves=halves),
        [*came, *parts[0], grad_mixed, hidden_in, attn_norm],
        [((tok, width), f32)],
        "last",
    )
    (result,) = simple_call(
        result_kernel, [result_parts[0], *result_came, mixed_rows], [((tok, width), bf16)], "result"
    )
    grad_gate, grad_up = grad_ffn[:, :ff].astype(f32), grad_ffn[:, ff:2 * ff].astype(f32)
    grad_down = grad_ffn[:, 2 * ff:].T.astype(f32)
    grad_out_weight = grad_attn[:, q_cols + 2 * k_cols:].T.astype(f32)
    grad_qkv = grad_attn[:, :q_cols + 2 * k_cols].astype(f32)

    small = small.reshape(-1)
    return (
        result,
        grad_hidden,
        small[:width],
        grad_qkv[:, :q_cols],
        grad_qkv[:, q_cols:q_cols + k_cols],
        grad_qkv[:, q_cols + k_cols:],
        small[2 * width:2 * width + head_dim],
        small[2 * width + head_dim:],
        grad_out_weight,
        small[width:2 * width],
        grad_gate,
        grad_up,
        grad_down,
    )


def solution(mesh):
    rows = P(("dp", "mp"), None)
    placed = (
        rows,
        P(),
        P(),
        P("dp", "mp"),
        P("dp", "mp"),
        P("dp", "mp"),
        P(),
        P(),
        P("mp", "dp"),
        P(),
        P("dp", "mp"),
        P("dp", "mp"),
        P("mp", "dp"),
        rows,
    )
    return jax.shard_map(
        body,
        mesh=mesh,
        in_specs=placed,
        out_specs=(
            rows,
            rows,
            P(),
            P("dp", "mp"),
            P("dp", "mp"),
            P("dp", "mp"),
            P(),
            P(),
            P("mp", "dp"),
            P(),
            P("dp", "mp"),
            P("dp", "mp"),
            P("mp", "dp"),
        ),
        check_vma=False,
    )
```

```python
import functools

import jax
import jax.numpy as jnp
from jax import lax
from jax.experimental import pallas as pl
from jax.experimental.pallas import tpu as pltpu
from jax.sharding import PartitionSpec as P

eps_norm = 1e-06
rope_base = 1000000.0
log2_e = 1.4426950408889634
bf16 = jnp.bfloat16
f32 = jnp.float32
longest = 2048
light_cost = pl.CostEstimate(flops=1 << 20, bytes_accessed=1 << 16, transcendentals=0)


def rms_scale(values):
    return lax.rsqrt(jnp.mean(values * values, axis=-1, keepdims=True) + eps_norm)


def norm_back(grad_hat, normed, scale_rows):
    return scale_rows * (grad_hat - normed * jnp.mean(grad_hat * normed, axis=-1, keepdims=True))


def mm(left, right):
    return jnp.dot(left, right, preferred_element_type=f32)


def mm_nt(left, right):
    return lax.dot_general(left, right, (((1,), (1,)), ((), ())), preferred_element_type=f32)


def mm_tn(left, right):
    return lax.dot_general(left, right, (((0,), (0,)), ((), ())), preferred_element_type=f32)


def load_pieces(refs, held_ref, sem_ref):
    rows = refs[0].shape[0]
    copies = [
        pltpu.make_async_copy(ref, held_ref.at[pl.ds(i * rows, rows), :], sem_ref.at[i])
        for i, ref in enumerate(refs)
    ]
    for copy in copies:
        copy.start()
    for copy in copies:
        copy.wait()


def gather_rows(src_ref, dst_ref, tok, repeat):
    dim = dst_ref.shape[1]
    for slot in range(src_ref.shape[0] // tok):
        for i in range(repeat):
            at = (slot * repeat + i) * tok
            dst_ref[at:at + tok] = src_ref[slot * tok:(slot + 1) * tok, i * dim:(i + 1) * dim]


def head_lanes(dim):
    head, heads = pl.program_id(0), pl.num_programs(0)
    return pl.ds(pl.multiple_of(head * dim, dim), dim), pl.ds(pl.multiple_of((heads + head) * dim, dim), dim)


def attn_fwd_kernel(flags_ref, base_ref, places_ref, q_ref, *refs, tok, sub, slots, blocks, pieces, repeat, head_dim):
    kv_refs, (o_ref, lse_ref, kv_ref, acc_ref, values_ref, rows_ref, sem_ref) = refs[:pieces], refs[pieces:]
    kb, chunk = tok * sub, tok * repeat
    k_lanes, v_lanes = head_lanes(head_dim)

    @pl.when(pl.program_id(0) == 0)
    def _():
        load_pieces(kv_refs, kv_ref, sem_ref)
        values_ref[:, head_dim:] = jnp.ones((kb, head_dim), bf16)

    gather_rows(q_ref, rows_ref, tok, repeat)
    acc_ref[...] = jnp.zeros_like(acc_ref)

    def run(block, keys, masked):
        values_ref[:, :head_dim] = kv_ref[keys, v_lanes]
        k = kv_ref[keys, k_lanes]
        for slot in range(slots):
            lines = slice(slot * chunk, (slot + 1) * chunk)
            p = jnp.exp2(mm_nt(rows_ref[lines], k))
            if masked:
                start, place = places_ref[lines, 0:1], places_ref[lines, 1:2]
                at = lax.broadcasted_iota(jnp.int32, (chunk, tok), 1)
                bases = [base_ref[block * sub + piece] for piece in range(sub)]
                allowed = jnp.concatenate([(at >= start - base) & (at <= place - base) for base in bases], axis=1)
                p = jnp.where(allowed, p, 0.0)
            acc_ref[lines] += mm(p.astype(bf16), values_ref[...])

    @pl.loop(0, blocks)
    def _(block):
        keys = pl.ds(pl.multiple_of(block * kb, kb), kb)
        pl.when(flags_ref[block] == 1)(lambda: run(block, keys, True))
        pl.when(flags_ref[block] == 2)(lambda: run(block, keys, False))

    for slot in range(slots):
        total = acc_ref[slot * chunk:(slot + 1) * chunk, head_dim:]
        out = acc_ref[slot * chunk:(slot + 1) * chunk, :head_dim] * (1.0 / total)
        for i in range(repeat):
            o_ref[slot * tok:(slot + 1) * tok, i * head_dim:(i + 1) * head_dim] = out[i * tok:(i + 1) * tok].astype(bf16)
        lse_ref[:, slot * chunk:(slot + 1) * chunk] = jnp.log2(total).T[:1]


def attn_bwd_kernel(flags_ref, base_ref, places_ref, q_ref, lse_ref, o_ref, do_ref, *refs, tok, sub, slots, blocks, pieces, repeat, head_dim, dq_scale, dk_scale):
    kv_refs = refs[:pieces]
    dq_ref, near_ref, far_ref, kv_ref, rows_ref, grads_ref, dqt_ref, delta_ref, dka_ref, dva_ref, sem_ref = refs[pieces:]
    kb, chunk = tok * sub, tok * repeat
    k_lanes, v_lanes = head_lanes(head_dim)

    @pl.when(pl.program_id(0) == 0)
    def _():
        load_pieces(kv_refs, kv_ref, sem_ref)

    gather_rows(q_ref, rows_ref, tok, repeat)
    gather_rows(do_ref, grads_ref, tok, repeat)
    dqt_ref[...] = jnp.zeros_like(dqt_ref)
    for slot in range(slots):
        for i in range(repeat):
            lines, lanes = slice(slot * tok, (slot + 1) * tok), slice(i * head_dim, (i + 1) * head_dim)
            prod = do_ref[lines, lanes].astype(f32) * o_ref[lines, lanes].astype(f32)
            at = (slot * repeat + i) * tok
            delta_ref[:, at:at + tok] = jnp.sum(prod.T, axis=0, keepdims=True)

    def run(block, keys, masked):
        k = kv_ref[keys, k_lanes]
        v = kv_ref[keys, v_lanes]
        kt = k.T
        for slot in range(slots):
            lanes = slice(slot * chunk, (slot + 1) * chunk)
            q = rows_ref[lanes]
            do = grads_ref[lanes]
            p = jnp.exp2(mm_nt(k, q) - lse_ref[:, lanes])
            if masked:
                start, place = places_ref[0:1, lanes], places_ref[1:2, lanes]
                at = lax.broadcasted_iota(jnp.int32, (tok, chunk), 0)
                bases = [base_ref[block * sub + piece] for piece in range(sub)]
                allowed = jnp.concatenate([(at >= start - base) & (at <= place - base) for base in bases], axis=0)
                p = jnp.where(allowed, p, 0.0)
            ds = (p * (mm_nt(v, do) - delta_ref[:, lanes])).astype(bf16)
            dva_ref[...] += mm(p.astype(bf16), do)
            dka_ref[...] += mm(ds, q)
            dqt_ref[:, lanes] += mm(kt, ds)

    @pl.loop(0, blocks)
    def _(block):
        keys = pl.ds(pl.multiple_of(block * kb, kb), kb)
        dka_ref[...] = jnp.zeros_like(dka_ref)
        dva_ref[...] = jnp.zeros_like(dva_ref)
        pl.when(flags_ref[block] == 1)(lambda: run(block, keys, True))
        pl.when(flags_ref[block] == 2)(lambda: run(block, keys, False))

        @pl.when(block < blocks // 2)
        def _():
            near_ref[keys, k_lanes] = (dka_ref[...] * dk_scale).astype(bf16)
            near_ref[keys, v_lanes] = dva_ref[...].astype(bf16)

        @pl.when(block >= blocks // 2)
        def _():
            far = pl.ds(pl.multiple_of(block * kb - blocks // 2 * kb, kb), kb)
            far_ref[far, k_lanes] = (dka_ref[...] * dk_scale).astype(bf16)
            far_ref[far, v_lanes] = dva_ref[...].astype(bf16)

    for slot in range(slots):
        out = (dqt_ref[:, slot * chunk:(slot + 1) * chunk] * dq_scale).T
        for i in range(repeat):
            dq_ref[slot * tok:(slot + 1) * tok, i * head_dim:(i + 1) * head_dim] = out[i * tok:(i + 1) * tok]


def turn(values):
    half = values.shape[-1] // 2
    return jnp.concatenate([values[:, half:], values[:, :half]], axis=1)


def ignoring(kernel, at, count):
    def reduced(*refs):
        kernel(*refs[:at], *refs[at + count:])

    return reduced


any_place = pl.BlockSpec(memory_space=pl.ANY)


def rotated_heads(raw, cos_ref, sin_ref, gain_ref, out_ref, head_dim, scale):
    for first in range(0, raw.shape[1], head_dim):
        lanes = slice(first, first + head_dim)
        hat = raw[:, lanes] * rms_scale(raw[:, lanes]) * gain_ref[...]
        out_ref[:, lanes] = ((hat * cos_ref[...] + turn(hat) * sin_ref[...]) * scale).astype(bf16)


def project_kv_kernel(w_ref, cos_ref, sin_ref, gain_ref, norm_ref, *refs, head_dim):
    *slot_refs, x_ref, rows_ref, raw_ref, out_ref = refs
    tok = slot_refs[0].shape[0]
    step = pl.program_id(0)

    @pl.when(step == 0)
    def _():
        for slot, slot_ref in enumerate(slot_refs):
            lines = slice(slot * tok, (slot + 1) * tok)
            values = slot_ref[...].astype(f32)
            scale = rms_scale(values)
            x_ref[lines] = (values * scale * norm_ref[...]).astype(bf16)
            rows_ref[lines] = jnp.broadcast_to(scale, (tok, rows_ref.shape[1]))

    raw = mm(x_ref[...], w_ref[...])

    @pl.when(step == 0)
    def _():
        raw_ref[...] = raw
        rotated_heads(raw, cos_ref, sin_ref, gain_ref, out_ref, head_dim, 1.0)

    @pl.when(step == 1)
    def _():
        out_ref[...] = raw.astype(bf16)


def project_kv(slots, norm, w, cos_table, sin_table, gain, first, tile):
    tok, width = slots[0].shape
    tokens, head_dim = tok * len(slots), gain.shape[1]

    def whole(rows, cols):
        return pl.BlockSpec((rows, cols), lambda j: (0, 0))

    w_spec = pl.BlockSpec((width, tile), lambda j: (0, j + first))
    return pl.pallas_call(
        functools.partial(project_kv_kernel, head_dim=head_dim),
        grid=(2,),
        in_specs=[w_spec, whole(tokens, head_dim), whole(tokens, head_dim), whole(1, head_dim), whole(1, width)]
        + [whole(tok, width)] * len(slots),
        out_specs=[whole(tokens, width), whole(tokens, head_dim), whole(tokens, tile), pl.BlockSpec((tokens, tile), lambda j: (0, j))],
        out_shape=[
            jax.ShapeDtypeStruct((tokens, width), bf16),
            jax.ShapeDtypeStruct((tokens, head_dim), f32),
            jax.ShapeDtypeStruct((tokens, tile), f32),
            jax.ShapeDtypeStruct((tokens, 2 * tile), bf16),
        ],
        cost_estimate=light_cost,
        name="project_kv",
    )(w, cos_table, sin_table, gain, norm, *slots)


def project_q_kernel(x_ref, w_ref, cos_ref, sin_ref, gain_ref, raw_ref, out_ref, *, head_dim, scale):
    raw = mm(x_ref[...], w_ref[...])
    raw_ref[...] = raw
    rotated_heads(raw, cos_ref, sin_ref, gain_ref, out_ref, head_dim, scale)


def project_q(x, w, cos_table, sin_table, gain, cols, tile, scale, after):
    tokens, width = x.shape
    head_dim = gain.shape[1]

    def whole(rows, cols):
        return pl.BlockSpec((rows, cols), lambda j: (0, 0))

    w_spec = pl.BlockSpec((width, tile), lambda j: (0, j))
    out_spec = pl.BlockSpec((tokens, tile), lambda j: (0, j))
    return pl.pallas_call(
        ignoring(functools.partial(project_q_kernel, head_dim=head_dim, scale=scale), 5, len(after)),
        grid=(cols // tile,),
        in_specs=[whole(tokens, width), w_spec, whole(tokens, head_dim), whole(tokens, head_dim), whole(1, head_dim)] + [any_place] * len(after),
        out_specs=[out_spec, out_spec],
        out_shape=[jax.ShapeDtypeStruct((tokens, cols), f32), jax.ShapeDtypeStruct((tokens, cols), bf16)],
        cost_estimate=light_cost,
        name="project_q",
    )(x, w, cos_table, sin_table, gain, *after)


def unproject_kernel(raw_ref, cos_ref, sin_ref, gain_ref, *refs, head_dim, sums):
    grad_refs, (out_ref, part_ref) = refs[:sums], refs[sums:]
    part = jnp.zeros((1, head_dim), f32)
    for first in range(0, out_ref.shape[1], head_dim):
        lanes = slice(first, first + head_dim)
        grad = grad_refs[0][:, lanes].astype(f32)
        for grad_ref in grad_refs[1:]:
            grad = grad + grad_ref[:, lanes].astype(f32)
        if first < raw_ref.shape[1]:
            raw = raw_ref[:, lanes]
            scale = rms_scale(raw)
            hat = raw * scale
            grad = grad * cos_ref[...] - turn(grad) * sin_ref[...]
            part = part + jnp.sum(grad * hat, axis=0, keepdims=True)
            grad = norm_back(grad * gain_ref[...], hat, scale)
        out_ref[:, lanes] = grad.astype(bf16)
    part_ref[...] = part


def unproject(raw, cos_table, sin_table, gain, grads, after, name):
    tokens, cols = raw.shape[0], grads[0].shape[1]
    head_dim = gain.shape[1]

    def first_rows(width):
        return pl.BlockSpec((tokens, width), lambda j: (0, 0))

    gain_spec = pl.BlockSpec((1, head_dim), lambda j: (0, 0))
    return pl.pallas_call(
        ignoring(functools.partial(unproject_kernel, head_dim=head_dim, sums=len(grads)), 4 + len(grads), len(after)),
        grid=(1,),
        in_specs=[first_rows(raw.shape[1]), first_rows(head_dim), first_rows(head_dim), gain_spec]
        + [first_rows(cols)] * len(grads)
        + [any_place] * len(after),
        out_specs=[first_rows(cols), gain_spec],
        out_shape=[
            jax.ShapeDtypeStruct((tokens, cols), bf16),
            jax.ShapeDtypeStruct(gain.shape, f32),
        ],
        cost_estimate=light_cost,
        name=name,
    )(raw, cos_table, sin_table, gain, *grads, *after)


def attn_back_kernel(dq_ref, dkv_ref, w_ref, rows_ref, *refs, slots):
    hidden_refs, out_refs, gain_ref = refs[:slots], refs[slots:-1], refs[-1]
    q_cols = dq_ref.shape[1]
    tok = out_refs[0].shape[0]
    total = mm_nt(dq_ref[...], w_ref[:, :q_cols]) + mm_nt(dkv_ref[...], w_ref[:, q_cols:])
    gain = jnp.zeros((1, total.shape[1]), f32)
    for slot in range(slots):
        lines = slice(slot * tok, (slot + 1) * tok)
        part = total[lines]
        gain = gain + jnp.sum(part * (hidden_refs[slot][...].astype(f32) * rows_ref[lines, :1]), axis=0, keepdims=True)
        out_refs[slot][...] = part.astype(bf16)
    gain_ref[...] = jnp.broadcast_to(gain, gain_ref.shape)


def attn_back_product(dq, dkv, w, row_scales, hidden_slots, after):
    rows, q_cols = dq.shape
    slots = len(hidden_slots)
    tok, width = hidden_slots[0].shape
    tile = min(512, width)
    slot_spec = pl.BlockSpec((tok, tile), lambda t: (0, t))
    return pl.pallas_call(
        ignoring(functools.partial(attn_back_kernel, slots=slots), 4 + slots, len(after)),
        grid=(width // tile,),
        in_specs=[
            pl.BlockSpec((rows, q_cols), lambda t: (0, 0)),
            pl.BlockSpec((rows, dkv.shape[1]), lambda t: (0, 0)),
            pl.BlockSpec((tile, q_cols + dkv.shape[1]), lambda t: (t, 0)),
            pl.BlockSpec(row_scales.shape, lambda t: (0, 0)),
        ]
        + [slot_spec] * slots
        + [any_place] * len(after),
        out_specs=[slot_spec] * slots + [pl.BlockSpec((8, tile), lambda t: (0, t))],
        out_shape=[jax.ShapeDtypeStruct((tok, width), bf16)] * slots + [jax.ShapeDtypeStruct((8, width), f32)],
        cost_estimate=light_cost,
        name="attn_back",
    )(dq, dkv, w, row_scales, *hidden_slots, *after)


def grad_attended_kernel(w_ref, *refs):
    *slot_refs, mid_ref, out_ref = refs
    tok = slot_refs[0].shape[0]
    for slot, slot_ref in enumerate(slot_refs):
        mid_ref[slot * tok:(slot + 1) * tok] = slot_ref[...]
    out_ref[...] = mm(mid_ref[...], w_ref[...]).astype(bf16)


def grad_attended_product(slots, w, cols, after):
    tok, width = slots[0].shape
    rows = tok * len(slots)

    def whole(rows, cols):
        return pl.BlockSpec((rows, cols), lambda j: (0, 0))

    return pl.pallas_call(
        ignoring(grad_attended_kernel, 1 + len(slots), len(after)),
        grid=(1,),
        in_specs=[pl.BlockSpec((width, cols), lambda j: (0, w.shape[1] // cols - 1))] + [whole(tok, width)] * len(slots) + [any_place] * len(after),
        out_specs=[whole(rows, width), whole(rows, cols)],
        out_shape=[jax.ShapeDtypeStruct((rows, width), bf16), jax.ShapeDtypeStruct((rows, cols), bf16)],
        cost_estimate=light_cost,
        name="grad_attended",
    )(w, *slots, *after)


def simple_call(kernel, arrays, shapes, name, after=()):
    vmem = pl.BlockSpec(memory_space=pltpu.VMEM)
    return pl.pallas_call(
        ignoring(kernel, len(arrays), len(after)),
        in_specs=[vmem] * len(arrays) + [any_place] * len(after),
        out_specs=[vmem] * len(shapes),
        out_shape=[jax.ShapeDtypeStruct(shape, dtype) for shape, dtype in shapes],
        cost_estimate=light_cost,
        name=name,
    )(*arrays, *after)


def add_rounded(left, right):
    return (left.astype(f32) + right.astype(f32)).astype(bf16)


def summed(refs):
    count = len(refs) // 2
    return jnp.concatenate(
        [came[...].astype(f32) + part[...].astype(f32) for came, part in zip(refs[:count], refs[count:])],
        axis=0,
    )


def store_halves(values, refs):
    rows = refs[0].shape[0]
    for i, ref in enumerate(refs):
        ref[...] = values[i * rows:(i + 1) * rows].astype(ref.dtype)


def mix_kernel(*refs, halves):
    sum_refs, (hidden_ref, norm_ref, mixed_ref, *input_refs) = refs[:2 * halves], refs[2 * halves:]
    mixed = hidden_ref[...].astype(f32) + summed(sum_refs)
    mixed_ref[...] = mixed
    store_halves(mixed * rms_scale(mixed) * norm_ref[...], input_refs)


def mid_kernel(*refs, halves):
    sum_refs, (mixed_ref, norm_ref, out_ref, grad_ref, gain_ref, *low_refs) = refs[:2 * halves], refs[2 * halves:]
    mixed = mixed_ref[...]
    scale = rms_scale(mixed)
    normed = mixed * scale
    back = summed(sum_refs)
    gain_ref[...] = jnp.sum(back * normed, axis=0, keepdims=True)
    grad = out_ref[...].astype(f32) + norm_back(back * norm_ref[...], normed, scale)
    grad_ref[...] = grad
    store_halves(grad, low_refs)


def last_kernel(*refs, halves):
    sum_refs, (grad_ref, hidden_ref, norm_ref, out_ref) = refs[:2 * halves], refs[2 * halves:]
    hidden = hidden_ref[...].astype(f32)
    scale = rms_scale(hidden)
    out_ref[...] = grad_ref[...] + norm_back(summed(sum_refs) * norm_ref[...], hidden * scale, scale)


def result_kernel(*refs):
    *sum_refs, mixed_ref, out_ref = refs
    total = sum_refs[0][...].astype(f32)
    for sum_ref in sum_refs[1:]:
        total = total + sum_ref[...].astype(f32)
    out_ref[...] = (mixed_ref[...] + total).astype(bf16)


def mark_kernel(out_ref):
    out_ref[...] = jnp.zeros_like(out_ref)


def split_kernel(x_ref, *out_refs):
    at = 0
    for out_ref in out_refs[:-1]:
        out_ref[...] = x_ref[:, at:at + out_ref.shape[1]].astype(f32)
        at += out_ref.shape[1]
    out_refs[-1][...] = x_ref[:, at:].astype(f32).T


def split_columns(x, cols, name):
    rows = x.shape[0]
    shapes = [((rows, c), f32) for c in cols[:-1]] + [((cols[-1], rows), f32)]
    return simple_call(split_kernel, [x], shapes, name)


def ffn_kernel(gate_ref, up_ref, down_ref, *refs, parts, held):
    x_refs, g_refs, refs = refs[:parts], refs[parts:2 * parts], refs[2 * parts + held:]
    grad_ref, x_ref, go_ref, *back_refs, back_ref = refs
    tile = pl.program_id(0)
    tok, size = x_refs[0].shape[0], gate_ref.shape[1]
    ff = grad_ref.shape[1] // 3

    @pl.when(tile == 0)
    def _():
        for i in range(parts):
            x_ref[i * tok:(i + 1) * tok] = x_refs[i][...]
            go_ref[i * tok:(i + 1) * tok] = g_refs[i][...]
        back_ref[...] = jnp.zeros_like(back_ref)

    x = x_ref[...]
    gate_pre = mm(x, gate_ref[...])
    up_value = mm(x, up_ref[...])
    grad_act = mm(go_ref[...], down_ref[...])
    sigmoid_gate = jax.nn.sigmoid(gate_pre)
    gated = gate_pre * sigmoid_gate
    grad_gate_pre = (
        grad_act * up_value * sigmoid_gate * (1.0 + gate_pre * (1.0 - sigmoid_gate))
    ).astype(bf16)
    grad_up_value = (grad_act * gated).astype(bf16)
    for i, values in enumerate([grad_gate_pre, grad_up_value, (gated * up_value).astype(bf16)]):
        grad_ref[:, pl.ds(pl.multiple_of(i * ff + tile * size, size), size)] = values
    back_ref[...] += mm_nt(grad_gate_pre, gate_ref[...]) + mm_nt(grad_up_value, up_ref[...])

    @pl.when(tile == pl.num_programs(0) - 1)
    def _():
        store_halves(back_ref[...], back_refs)


def feed_forward(inputs, grads, w_ffn, held, chunk, chunks):
    parts = len(inputs)
    tok, width = inputs[0].shape
    ff = w_ffn.shape[1] // 3
    size = next(s for s in (512, 384, 256, 128) if ff % s == 0)
    tiles = ff // size
    part_spec = pl.BlockSpec((tok, width), lambda t: (0, 0))

    def rows_spec(cols):
        return pl.BlockSpec((parts * tok, cols), lambda t: (chunk, 0))

    rows = parts * tok * chunks
    return pl.pallas_call(
        functools.partial(ffn_kernel, parts=parts, held=len(held)),
        grid=(tiles,),
        in_specs=[
            pl.BlockSpec((width, size), lambda t: (0, t)),
            pl.BlockSpec((width, size), lambda t: (0, tiles + t)),
            pl.BlockSpec((width, size), lambda t: (0, 2 * tiles + t)),
        ]
        + [part_spec] * (2 * parts)
        + [pl.BlockSpec(memory_space=pl.ANY)] * len(held),
        out_specs=[rows_spec(3 * ff), rows_spec(width), rows_spec(width)] + [part_spec] * parts,
        out_shape=[
            jax.ShapeDtypeStruct((rows, 3 * ff), bf16),
            jax.ShapeDtypeStruct((rows, width), bf16),
            jax.ShapeDtypeStruct((rows, width), bf16),
        ]
        + [jax.ShapeDtypeStruct((tok, width), bf16)] * parts,
        scratch_shapes=[pltpu.VMEM((parts * tok, width), f32)],
        input_output_aliases={3 + 2 * parts + i: i for i in range(len(held))},
        cost_estimate=light_cost,
        name="feed_forward",
    )(w_ffn, w_ffn, w_ffn, *inputs, *grads, *held)


def weight_grads_kernel(*refs, turns):
    *left_refs, right_ref, out_ref, turned_ref = refs
    tile = pl.program_id(0)
    for left_ref, at in zip(left_refs, turns):
        @pl.when(tile == at)
        def _(left_ref=left_ref):
            turned_ref[...] = left_ref[...].T

    rows = min(256, out_ref.shape[0])
    for first in range(0, out_ref.shape[0], rows):
        lines = slice(first, first + rows)
        out_ref[lines] = mm(turned_ref[lines], right_ref[...]).astype(bf16)


def weight_grads(lefts, right, starts, after, name):
    tokens, width = lefts[0].shape
    cols = right.shape[1]
    size = next(s for s in (512, 384, 256, 128) if all(at % s == 0 for at in (cols, *starts)))
    whole = pl.BlockSpec((tokens, width), lambda t: (0, 0))
    return pl.pallas_call(
        ignoring(functools.partial(weight_grads_kernel, turns=[at // size for at in starts]), len(lefts) + 1, len(after)),
        grid=(cols // size,),
        in_specs=[whole] * len(lefts) + [pl.BlockSpec((tokens, size), lambda t: (0, t))] + [any_place] * len(after),
        out_specs=pl.BlockSpec((width, size), lambda t: (0, t)),
        out_shape=jax.ShapeDtypeStruct((width, cols), bf16),
        scratch_shapes=[pltpu.VMEM((width, tokens), bf16)],
        cost_estimate=light_cost,
        name=name,
    )(*lefts, right, *after)


def slot_product_kernel(x_ref, w_ref, *out_refs):
    tok = out_refs[0].shape[0]
    total = mm_nt(x_ref[...], w_ref[...])
    for slot, out_ref in enumerate(out_refs):
        out_ref[...] = total[slot * tok:(slot + 1) * tok].astype(bf16)


def slot_product(x, x_block, w, w_block, depth, slots, after, name):
    rows, width = x.shape[0], w.shape[0]
    tile = min(512, width)
    out_spec = pl.BlockSpec((rows // slots, tile), lambda t: (0, t))
    return pl.pallas_call(
        ignoring(slot_product_kernel, 2, len(after)),
        grid=(width // tile,),
        in_specs=[
            pl.BlockSpec((rows, depth), lambda t: (0, x_block)),
            pl.BlockSpec((tile, depth), lambda t: (t, w_block)),
        ]
        + [any_place] * len(after),
        out_specs=[out_spec] * slots,
        out_shape=[jax.ShapeDtypeStruct((rows // slots, width), bf16)] * slots,
        cost_estimate=light_cost,
        name=name,
    )(x, w, *after)


def more_grads_kernel(left_ref, *refs, rights):
    right_refs, out_ref, turned_ref = refs[:rights], refs[-2], refs[-1]
    tile = pl.program_id(0)

    @pl.when(tile == 0)
    def _():
        turned_ref[...] = left_ref[...].T

    def run(right_ref):
        rows = min(256, out_ref.shape[0])
        for first in range(0, out_ref.shape[0], rows):
            lines = slice(first, first + rows)
            out_ref[lines] = mm(turned_ref[lines], right_ref[...]).astype(bf16)

    for i, right_ref in enumerate(right_refs):
        pl.when(tile == i)(functools.partial(run, right_ref))


def more_grads(left, rights, held, at, blocks, after, name):
    tokens, width = left.shape
    size = rights[0].shape[1]
    return pl.pallas_call(
        ignoring(functools.partial(more_grads_kernel, rights=len(rights)), 1 + len(rights), len(held) + len(after)),
        grid=(len(rights),),
        in_specs=[pl.BlockSpec((tokens, width), lambda t: (0, 0))]
        + [pl.BlockSpec((tokens, size), lambda t: (0, 0))] * len(rights)
        + [any_place] * (len(held) + len(after)),
        out_specs=pl.BlockSpec((width, size), lambda t: (0, at + t)),
        out_shape=jax.ShapeDtypeStruct((width, blocks * size), bf16),
        scratch_shapes=[pltpu.VMEM((width, tokens), bf16)],
        input_output_aliases={1 + len(rights) + i: 0 for i in range(len(held))},
        cost_estimate=light_cost,
        name=name,
    )(left, *rights, *held, *after)


def fold_kernel(near_ref, got_ref, *out_refs):
    rows = out_refs[0].shape[0]
    for i, out_ref in enumerate(out_refs):
        lines = slice((i + 1) * rows, (i + 2) * rows)
        out_ref[...] = (near_ref[lines].astype(f32) + got_ref[lines].astype(f32)).astype(bf16)


def fold_blocks(near, got, count, after):
    vmem = pl.BlockSpec(memory_space=pltpu.VMEM)
    shape = jax.ShapeDtypeStruct((near.shape[0] // count, near.shape[1]), bf16)
    return pl.pallas_call(
        ignoring(fold_kernel, 2, len(after)),
        in_specs=[vmem, vmem] + [any_place] * len(after),
        out_specs=[vmem] * (count - 1),
        out_shape=[shape] * (count - 1),
        cost_estimate=light_cost,
        name="fold_blocks",
    )(near, got, *after)


def body(
    hidden_in,
    doc_lengths,
    attn_norm,
    query_weight,
    key_weight,
    value_weight,
    query_gain,
    key_gain,
    output_weight,
    ffn_norm,
    gate_weight,
    up_weight,
    down_weight,
    grad_out,
):
    dp_count = lax.axis_size("dp")
    mp_count = lax.axis_size("mp")
    slots = mp_count
    tok, width = hidden_in.shape
    group_rows = tok * mp_count
    head_dim = query_gain.shape[0]
    half_dim = head_dim // 2
    q_cols = query_weight.shape[1]
    k_cols = key_weight.shape[1]
    kv_local = k_cols // head_dim
    repeat = q_cols // k_cols
    ff = gate_weight.shape[1]
    group = lax.axis_index("dp")
    my_z = lax.axis_index("mp")
    score_scale = head_dim ** (-0.5)
    ring = [(i, (i + 1) % mp_count) for i in range(mp_count)]
    near_masks = list(range(0, dp_count, 2))
    masks = near_masks + [mask + 1 for mask in near_masks]
    far_masks = near_masks[1:]

    def tie(value, *others):
        return lax.optimization_barrier((value,) + others)[0]

    def shift(values):
        return lax.ppermute(values, "mp", ring)

    def swap(values, mask):
        return lax.ppermute(values, "dp", [(i, i ^ mask) for i in range(dp_count)])

    reach = (min(longest, group_rows * dp_count) - 2) // group_rows + 1

    def needs(reader, owner):
        first = reader // 2 * 2
        return owner <= first + 1 and owner >= first - reach

    def swap_forward(values, mask):
        pairs = [(i, i ^ mask) for i in range(dp_count) if needs(i ^ mask, i)]
        return lax.ppermute(values, "dp", pairs)

    def swap_back(values, mask):
        pairs = [(i, i ^ mask) for i in range(dp_count) if needs(i, i ^ mask)]
        return lax.ppermute(values, "dp", pairs)

    half = dp_count // 2
    halves = 2
    part_rows = tok // halves
    ids = jnp.array(masks, jnp.int32)
    mask_blocks = group ^ ids
    attn_norm = attn_norm.reshape(1, width)
    ffn_norm = ffn_norm.reshape(1, width)
    part_shape = ((part_rows, width), bf16)

    def tie_all(values, *others):
        return list(lax.optimization_barrier((*values, *others)))[:len(values)]

    def order(values, others):
        both = lax.optimization_barrier((*values, *others))
        return list(both[:len(values)]), list(both[len(values):])

    def mark(*operands):
        (tiny,) = simple_call(mark_kernel, [], [((8, 128), f32)], "mark", operands)
        return [swap(tiny, 1)]

    def flat(slot_lists):
        return [part for slot in slot_lists for part in slot]

    def by_slot(parts):
        return [list(parts[i:i + halves]) for i in range(0, len(parts), halves)]

    def shift_all(parts):
        return [shift(part) for part in parts]

    def ring_add(came, own):
        return [shift(add_rounded(one, other)) for one, other in zip(came, own)]

    w_attn_own = jnp.concatenate([query_weight, key_weight, value_weight, output_weight.T], axis=1)
    w_ffn_own = jnp.concatenate([gate_weight, up_weight, down_weight.T], axis=1)
    w_attn = lax.all_gather(w_attn_own, "dp", axis=0, tiled=True)
    w_ffn = tie(lax.all_gather(w_ffn_own, "dp", axis=0, tiled=True), w_attn)

    doc_ends = jnp.cumsum(doc_lengths)
    slot_offset = ((my_z - jnp.arange(slots, dtype=jnp.int32)) % mp_count) * tok
    places = (
        group * group_rows
        + slot_offset[:, None]
        + jnp.arange(tok, dtype=jnp.int32)[None, :]
    )
    before = doc_ends[None, None, :] <= places[:, :, None]
    starts = jnp.sum(jnp.where(before, doc_lengths[None, None, :], 0), axis=-1)
    position = (places - starts).reshape(group_rows)
    inverse = rope_base ** (-(2.0 * jnp.arange(half_dim, dtype=f32)) / head_dim)
    angles = position.astype(f32)[:, None] * inverse[None, :]
    cos_table, sin_table = jnp.cos(angles), jnp.sin(angles)
    cos_table = jnp.concatenate([cos_table, cos_table], axis=1)
    sin_table = jnp.concatenate([-sin_table, sin_table], axis=1)

    sub = min(4, slots)
    key_base = mask_blocks[:, None] * group_rows + slot_offset[None, :]
    blocks = dp_count * slots // sub
    key_base = key_base.reshape(blocks, sub)
    q_first, q_last = places[:, 0], places[:, -1]
    s_first, s_last = starts[:, 0], starts[:, -1]
    piece_lo, piece_hi = key_base[None], key_base[None] + tok - 1
    some = (piece_lo <= q_last[:, None, None]) & (s_first[:, None, None] <= piece_hi)
    every = (piece_hi <= q_first[:, None, None]) & (s_last[:, None, None] <= piece_lo)
    flags = jnp.where(jnp.all(every, -1), 2, jnp.any(some, -1).astype(jnp.int32)).astype(jnp.int32)
    flags = jnp.where(jnp.all(flags == 2, axis=0), 2, jnp.any(flags > 0, axis=0).astype(jnp.int32))
    key_base = key_base.reshape(-1)
    lane_places = jnp.tile(jnp.stack([starts, places]), (1, 1, repeat)).reshape(2, -1)
    row_places = lane_places.T

    hidden_slots = [[hidden_in[i * part_rows:(i + 1) * part_rows] for i in range(halves)]]
    for slot in range(1, slots):
        came = shift_all(hidden_slots[-1])
        if slot == 1:
            came = tie_all(came, cos_table, sin_table, lane_places, w_ffn_own)
        hidden_slots.append(came)
    q_gain, k_gain = query_gain.reshape(1, head_dim), key_gain.reshape(1, head_dim)
    attn_input, row_scales, key_raw, kv_own = project_kv(
        flat(hidden_slots), attn_norm, w_attn, cos_table, sin_table, k_gain, repeat, k_cols
    )
    kv_came = [swap_forward(kv_own, mask) for mask in far_masks]
    grad_slots = [tie_all([grad_out[i * part_rows:(i + 1) * part_rows] for i in range(halves)], *hidden_slots[-1])]
    grad_slots.append(tie_all(shift_all(grad_slots[-1]), kv_own))
    query_raw, query_rot = project_q(
        tie(attn_input, kv_own, *grad_slots[-1]), w_attn, cos_table, sin_table, q_gain, q_cols, k_cols,
        score_scale * log2_e, [],
    )
    for slot in range(2, slots):
        came = shift_all(grad_slots[-1])
        if slot == 2:
            came = tie_all(came, query_rot)
            kv_came = tie_all(kv_came, *came)
        grad_slots.append(came)
    kv_near = [kv_own] + tie_all(kv_came, query_rot)
    kv_pieces = kv_near + [swap(piece, 1) for piece in kv_near]

    keys_total = dp_count * group_rows
    head_rows = repeat * tok
    smem = pl.BlockSpec(memory_space=pltpu.SMEM)
    any_spec = pl.BlockSpec(memory_space=pl.ANY)
    all_rows = slots * head_rows
    lane_spec = pl.BlockSpec((2, all_rows), lambda h: (0, 0))
    row_spec = pl.BlockSpec((all_rows, 2), lambda h: (0, 0))
    q_spec = pl.BlockSpec((group_rows, repeat * head_dim), lambda h: (0, h))
    lse_spec = pl.BlockSpec((None, 1, all_rows), lambda h: (h, 0, 0))
    dims = dict(
        tok=tok, sub=sub, slots=slots, blocks=blocks, pieces=dp_count, repeat=repeat, head_dim=head_dim
    )
    kv_scratch = pltpu.VMEM((keys_total, 2 * k_cols), bf16)
    attended_low, lse = pl.pallas_call(
        functools.partial(attn_fwd_kernel, **dims),
        grid=(kv_local,),
        in_specs=[smem, smem, row_spec, q_spec] + [any_spec] * dp_count,
        out_specs=[q_spec, lse_spec],
        out_shape=[
            jax.ShapeDtypeStruct((group_rows, q_cols), bf16),
            jax.ShapeDtypeStruct((kv_local, 1, all_rows), f32),
        ],
        scratch_shapes=[
            kv_scratch,
            pltpu.VMEM((all_rows, 2 * head_dim), f32),
            pltpu.VMEM((tok * sub, 2 * head_dim), bf16),
            pltpu.VMEM((all_rows, head_dim), bf16),
            pltpu.SemaphoreType.DMA((dp_count,)),
        ],
        cost_estimate=light_cost,
        name="attn_fwd",
    )(flags, key_base, row_places, query_rot, *kv_pieces)

    grad_slots[slots - 1] = tie_all(grad_slots[slots - 1], attended_low)
    parts = by_slot(slot_product(attended_low, 0, w_attn, 2 * k_cols // q_cols + 1, q_cols, slots * halves, [], "attn_out"))
    came = shift_all(tie_all(parts[1], *grad_slots[-1]))
    for slot in range(2, slots):
        came = ring_add(came, parts[slot])
    mixed_rows, *ffn_input = simple_call(
        functools.partial(mix_kernel, halves=halves),
        [*came, *parts[0], hidden_in, ffn_norm],
        [((tok, width), f32)] + [part_shape] * halves,
        "mix",
    )

    ffn_slots = [ffn_input, shift_all(ffn_input)]
    held, parts = [], []
    for first in range(0, slots, 2):
        *held, = feed_forward(
            flat(ffn_slots[first:first + 2]), flat(grad_slots[first:first + 2]), w_ffn, held, first // 2, slots // 2
        )
        held, back = held[:3], held[3:]
        parts += by_slot(back)
        if first + 2 < slots:
            ffn_slots.append(tie_all(shift_all(ffn_slots[-1]), *back))
            ffn_slots.append(shift_all(ffn_slots[-1]))
    ffn_right, ffn_all, grad_all = held

    came = shift_all(tie_all(parts[1], *ffn_slots[-1]))
    ffn_part = weight_grads([ffn_all, grad_all], tie(ffn_right, *came), [0, 2 * ff], [], "ffn_grads")
    for slot in range(2, slots):
        came = ring_add(came, parts[slot])
        if slot == 2:
            came = tie_all(came, ffn_part)
    grad_ffn = lax.psum_scatter(ffn_part, "dp", scatter_dimension=0, tiled=True)
    grad_mixed, grad_ffn_norm, *mid_first = simple_call(
        functools.partial(mid_kernel, halves=halves),
        [*came, *parts[0], mixed_rows, ffn_norm, grad_out],
        [((tok, width), f32), ((1, width), f32)] + [part_shape] * halves,
        "mid",
    )
    mid_slots = [mid_first]
    result_parts = slot_product(ffn_right, 2, w_ffn, 2, ff, slots, [], "ffn_out")
    for slot in range(1, slots):
        came = shift_all(mid_slots[-1])
        mid_slots.append(came)

    result_came = [
        lax.ppermute(result_parts[slot], "mp", [(i, (i - slot) % mp_count) for i in range(mp_count)])
        for slot in range(1, slots)
    ]

    grad_mid, grad_attended = grad_attended_product(flat(mid_slots), w_attn, q_cols, [])
    near_spec = pl.BlockSpec((keys_total // 2, 2 * k_cols), lambda h: (0, 0))
    near_shape = jax.ShapeDtypeStruct((keys_total // 2, 2 * k_cols), bf16)
    dq_rot, dkv_near, dkv_far = pl.pallas_call(
        functools.partial(
            attn_bwd_kernel, **dims, dq_scale=score_scale, dk_scale=1.0 / log2_e
        ),
        grid=(kv_local,),
        in_specs=[smem, smem, lane_spec, q_spec, lse_spec, q_spec, q_spec] + [any_spec] * dp_count,
        out_specs=[q_spec, near_spec, near_spec],
        out_shape=[jax.ShapeDtypeStruct((group_rows, q_cols), f32), near_shape, near_shape],
        scratch_shapes=[
            kv_scratch,
            pltpu.VMEM((all_rows, head_dim), bf16),
            pltpu.VMEM((all_rows, head_dim), bf16),
            pltpu.VMEM((head_dim, all_rows), f32),
            pltpu.VMEM((1, all_rows), f32),
            pltpu.VMEM((tok * sub, head_dim), f32),
            pltpu.VMEM((tok * sub, head_dim), f32),
            pltpu.SemaphoreType.DMA((dp_count,)),
        ],
        cost_estimate=light_cost,
        name="attn_bwd",
    )(flags, key_base, lane_places, query_rot, lse, attended_low, grad_attended, *kv_pieces)

    dkv_got = swap(dkv_far, 1)
    dkv_sent = fold_blocks(dkv_near, dkv_got, half, [])
    dkv_came = [swap_back(sent, mask) for sent, mask in zip(dkv_sent, far_masks)]
    marked = mark(*dkv_sent)
    dq_raw, query_gain_part = unproject(query_raw, cos_table, sin_table, q_gain, [dq_rot], marked, "unproject_q")
    attn_part = more_grads(grad_mid, [attended_low], [], 2, 3, marked, "out_grads")
    attn_part = more_grads(attn_input, [dq_raw], [attn_part], 0, 3, [], "q_grads")
    dkv_raw, key_gain_part = unproject(
        key_raw, cos_table, sin_table, k_gain, [dkv_near, dkv_got] + dkv_came, [attn_part, *result_came], "unproject_kv"
    )

    attn_part = more_grads(attn_input, [dkv_raw], [attn_part], 1, 3, [grad_ffn], "kv_grads")
    grad_attn = lax.psum_scatter(attn_part, "dp", scatter_dimension=0, tiled=True)
    *parts, attn_gain_part = attn_back_product(
        dq_raw, dkv_raw, w_attn, row_scales, flat(hidden_slots), [attn_part]
    )
    parts = by_slot(parts)
    came = shift_all(parts[1])
    came, (attn_gain_part,) = order(came, [attn_gain_part])
    small = jnp.concatenate(
        [attn_gain_part[0], grad_ffn_norm[0], query_gain_part[0], key_gain_part[0]]
    ).reshape(-1, head_dim)
    small = small + swap(small, 1)
    for slot in range(2, slots):
        came = ring_add(came, parts[slot])
        if slot == 2:
            grads = split_columns(grad_ffn, [ff, ff, ff], "split_ffn")
            came, (small, grad_gate, grad_up, grad_down) = order(came, [small, *grads])
            small = small + sum(swap(small, mask) for mask in far_masks)
    came, (small,) = order(came, [small])
    turns = [[(i, (i + by) % mp_count) for i in range(mp_count)] for by in range(1, mp_count)]
    small = small + sum(lax.ppermute(small, "mp", turn) for turn in turns)
    (grad_hidden,) = simple_call(
        functools.partial(last_kernel, halves=halves),
        [*came, *parts[0], grad_mixed, hidden_in, attn_norm],
        [((tok, width), f32)],
        "last",
    )
    (result,) = simple_call(
        result_kernel, [result_parts[0], *result_came, mixed_rows], [((tok, width), bf16)], "result"
    )
    grad_query, grad_key, grad_value, grad_out_weight = split_columns(
        grad_attn, [q_cols, k_cols, k_cols, q_cols], "split_attn"
    )

    small = small.reshape(-1)
    return (
        result,
        grad_hidden,
        small[:width],
        grad_query,
        grad_key,
        grad_value,
        small[2 * width:2 * width + head_dim],
        small[2 * width + head_dim:],
        grad_out_weight,
        small[width:2 * width],
        grad_gate,
        grad_up,
        grad_down,
    )


def solution(mesh):
    rows = P(("dp", "mp"), None)
    placed = (
        rows,
        P(),
        P(),
        P("dp", "mp"),
        P("dp", "mp"),
        P("dp", "mp"),
        P(),
        P(),
        P("mp", "dp"),
        P(),
        P("dp", "mp"),
        P("dp", "mp"),
        P("mp", "dp"),
        rows,
    )
    return jax.shard_map(
        body,
        mesh=mesh,
        in_specs=placed,
        out_specs=(
            rows,
            rows,
            P(),
            P("dp", "mp"),
            P("dp", "mp"),
            P("dp", "mp"),
            P(),
            P(),
            P("mp", "dp"),
            P(),
            P("dp", "mp"),
            P("dp", "mp"),
            P("mp", "dp"),
        ),
        check_vma=False,
    )
```

```python
import functools

import jax
import jax.numpy as jnp
from jax import lax
from jax.experimental import pallas as pl
from jax.experimental.pallas import tpu as pltpu
from jax.sharding import PartitionSpec as P

eps_norm = 1e-06
rope_base = 1000000.0
log2_e = 1.4426950408889634
bf16 = jnp.bfloat16
f32 = jnp.float32
longest = 2048
light_cost = pl.CostEstimate(flops=1 << 20, bytes_accessed=1 << 16, transcendentals=0)


def rms_scale(values):
    return lax.rsqrt(jnp.mean(values * values, axis=-1, keepdims=True) + eps_norm)


def norm_back(grad_hat, normed, scale_rows):
    return scale_rows * (grad_hat - normed * jnp.mean(grad_hat * normed, axis=-1, keepdims=True))


def mm(left, right):
    return jnp.dot(left, right, preferred_element_type=f32)


def mm_nt(left, right):
    return lax.dot_general(left, right, (((1,), (1,)), ((), ())), preferred_element_type=f32)


def mm_tn(left, right):
    return lax.dot_general(left, right, (((0,), (0,)), ((), ())), preferred_element_type=f32)


def load_pieces(refs, held_ref, sem_ref):
    rows = refs[0].shape[0]
    copies = [
        pltpu.make_async_copy(ref, held_ref.at[pl.ds(i * rows, rows), :], sem_ref.at[i])
        for i, ref in enumerate(refs)
    ]
    for copy in copies:
        copy.start()
    for copy in copies:
        copy.wait()


def gather_rows(src_ref, dst_ref, tok, repeat):
    dim = dst_ref.shape[1]
    for slot in range(src_ref.shape[0] // tok):
        for i in range(repeat):
            at = (slot * repeat + i) * tok
            dst_ref[at:at + tok] = src_ref[slot * tok:(slot + 1) * tok, i * dim:(i + 1) * dim]


def head_lanes(dim):
    head, heads = pl.program_id(0), pl.num_programs(0)
    return pl.ds(pl.multiple_of(head * dim, dim), dim), pl.ds(pl.multiple_of((heads + head) * dim, dim), dim)


def attn_fwd_kernel(flags_ref, base_ref, places_ref, q_ref, *refs, tok, sub, slots, blocks, pieces, repeat, head_dim):
    kv_refs, (o_ref, lse_ref, kv_ref, acc_ref, values_ref, rows_ref, sem_ref) = refs[:pieces], refs[pieces:]
    kb, chunk = tok * sub, tok * repeat
    k_lanes, v_lanes = head_lanes(head_dim)

    @pl.when(pl.program_id(0) == 0)
    def _():
        load_pieces(kv_refs, kv_ref, sem_ref)
        values_ref[:, head_dim:] = jnp.ones((kb, head_dim), bf16)

    gather_rows(q_ref, rows_ref, tok, repeat)
    acc_ref[...] = jnp.zeros_like(acc_ref)

    def run(block, keys, masked):
        values_ref[:, :head_dim] = kv_ref[keys, v_lanes]
        k = kv_ref[keys, k_lanes]
        for slot in range(slots):
            lines = slice(slot * chunk, (slot + 1) * chunk)
            p = jnp.exp2(mm_nt(rows_ref[lines], k))
            if masked:
                start, place = places_ref[lines, 0:1], places_ref[lines, 1:2]
                at = lax.broadcasted_iota(jnp.int32, (chunk, tok), 1)
                bases = [base_ref[block * sub + piece] for piece in range(sub)]
                allowed = jnp.concatenate([(at >= start - base) & (at <= place - base) for base in bases], axis=1)
                p = jnp.where(allowed, p, 0.0)
            acc_ref[lines] += mm(p.astype(bf16), values_ref[...])

    @pl.loop(0, blocks)
    def _(block):
        keys = pl.ds(pl.multiple_of(block * kb, kb), kb)
        pl.when(flags_ref[block] == 1)(lambda: run(block, keys, True))
        pl.when(flags_ref[block] == 2)(lambda: run(block, keys, False))

    for slot in range(slots):
        total = acc_ref[slot * chunk:(slot + 1) * chunk, head_dim:]
        out = acc_ref[slot * chunk:(slot + 1) * chunk, :head_dim] * (1.0 / total)
        for i in range(repeat):
            o_ref[slot * tok:(slot + 1) * tok, i * head_dim:(i + 1) * head_dim] = out[i * tok:(i + 1) * tok].astype(bf16)
        lse_ref[:, slot * chunk:(slot + 1) * chunk] = jnp.log2(total).T[:1]


def attn_bwd_kernel(flags_ref, base_ref, places_ref, q_ref, lse_ref, o_ref, do_ref, *refs, tok, sub, slots, blocks, pieces, repeat, head_dim, dq_scale, dk_scale):
    kv_refs = refs[:pieces]
    dq_ref, near_ref, far_ref, kv_ref, rows_ref, grads_ref, dqt_ref, delta_ref, dka_ref, dva_ref, sem_ref = refs[pieces:]
    kb, chunk = tok * sub, tok * repeat
    k_lanes, v_lanes = head_lanes(head_dim)

    @pl.when(pl.program_id(0) == 0)
    def _():
        load_pieces(kv_refs, kv_ref, sem_ref)

    gather_rows(q_ref, rows_ref, tok, repeat)
    gather_rows(do_ref, grads_ref, tok, repeat)
    dqt_ref[...] = jnp.zeros_like(dqt_ref)
    for slot in range(slots):
        for i in range(repeat):
            lines, lanes = slice(slot * tok, (slot + 1) * tok), slice(i * head_dim, (i + 1) * head_dim)
            prod = do_ref[lines, lanes].astype(f32) * o_ref[lines, lanes].astype(f32)
            at = (slot * repeat + i) * tok
            delta_ref[:, at:at + tok] = jnp.sum(prod.T, axis=0, keepdims=True)

    def run(block, keys, masked):
        k = kv_ref[keys, k_lanes]
        v = kv_ref[keys, v_lanes]
        kt = k.T
        for slot in range(slots):
            lanes = slice(slot * chunk, (slot + 1) * chunk)
            q = rows_ref[lanes]
            do = grads_ref[lanes]
            p = jnp.exp2(mm_nt(k, q) - lse_ref[:, lanes])
            if masked:
                start, place = places_ref[0:1, lanes], places_ref[1:2, lanes]
                at = lax.broadcasted_iota(jnp.int32, (tok, chunk), 0)
                bases = [base_ref[block * sub + piece] for piece in range(sub)]
                allowed = jnp.concatenate([(at >= start - base) & (at <= place - base) for base in bases], axis=0)
                p = jnp.where(allowed, p, 0.0)
            ds = (p * (mm_nt(v, do) - delta_ref[:, lanes])).astype(bf16)
            dva_ref[...] += mm(p.astype(bf16), do)
            dka_ref[...] += mm(ds, q)
            dqt_ref[:, lanes] += mm(kt, ds)

    @pl.loop(0, blocks)
    def _(block):
        keys = pl.ds(pl.multiple_of(block * kb, kb), kb)
        dka_ref[...] = jnp.zeros_like(dka_ref)
        dva_ref[...] = jnp.zeros_like(dva_ref)
        pl.when(flags_ref[block] == 1)(lambda: run(block, keys, True))
        pl.when(flags_ref[block] == 2)(lambda: run(block, keys, False))

        @pl.when(block < blocks // 2)
        def _():
            near_ref[keys, k_lanes] = (dka_ref[...] * dk_scale).astype(bf16)
            near_ref[keys, v_lanes] = dva_ref[...].astype(bf16)

        @pl.when(block >= blocks // 2)
        def _():
            far = pl.ds(pl.multiple_of(block * kb - blocks // 2 * kb, kb), kb)
            far_ref[far, k_lanes] = (dka_ref[...] * dk_scale).astype(bf16)
            far_ref[far, v_lanes] = dva_ref[...].astype(bf16)

    for slot in range(slots):
        out = (dqt_ref[:, slot * chunk:(slot + 1) * chunk] * dq_scale).T
        for i in range(repeat):
            dq_ref[slot * tok:(slot + 1) * tok, i * head_dim:(i + 1) * head_dim] = out[i * tok:(i + 1) * tok]


def turn(values):
    half = values.shape[-1] // 2
    return jnp.concatenate([values[:, half:], values[:, :half]], axis=1)


def ignoring(kernel, at, count):
    def reduced(*refs):
        kernel(*refs[:at], *refs[at + count:])

    return reduced


any_place = pl.BlockSpec(memory_space=pl.ANY)


def rotated_heads(raw, cos_ref, sin_ref, gain_ref, out_ref, head_dim, scale):
    for first in range(0, raw.shape[1], head_dim):
        lanes = slice(first, first + head_dim)
        hat = raw[:, lanes] * rms_scale(raw[:, lanes]) * gain_ref[...]
        out_ref[:, lanes] = ((hat * cos_ref[...] + turn(hat) * sin_ref[...]) * scale).astype(bf16)


def project_kv_kernel(w_ref, cos_ref, sin_ref, gain_ref, norm_ref, *refs, head_dim):
    *slot_refs, x_ref, rows_ref, raw_ref, out_ref = refs
    tok = slot_refs[0].shape[0]
    step = pl.program_id(0)

    @pl.when(step == 0)
    def _():
        for slot, slot_ref in enumerate(slot_refs):
            lines = slice(slot * tok, (slot + 1) * tok)
            values = slot_ref[...].astype(f32)
            scale = rms_scale(values)
            x_ref[lines] = (values * scale * norm_ref[...]).astype(bf16)
            rows_ref[lines] = jnp.broadcast_to(scale, (tok, rows_ref.shape[1]))

    raw = mm(x_ref[...], w_ref[...])

    @pl.when(step == 0)
    def _():
        raw_ref[...] = raw
        rotated_heads(raw, cos_ref, sin_ref, gain_ref, out_ref, head_dim, 1.0)

    @pl.when(step == 1)
    def _():
        out_ref[...] = raw.astype(bf16)


def project_kv(slots, norm, w, cos_table, sin_table, gain, first, tile):
    tok, width = slots[0].shape
    tokens, head_dim = tok * len(slots), gain.shape[1]

    def whole(rows, cols):
        return pl.BlockSpec((rows, cols), lambda j: (0, 0))

    w_spec = pl.BlockSpec((width, tile), lambda j: (0, j + first))
    return pl.pallas_call(
        functools.partial(project_kv_kernel, head_dim=head_dim),
        grid=(2,),
        in_specs=[w_spec, whole(tokens, head_dim), whole(tokens, head_dim), whole(1, head_dim), whole(1, width)]
        + [whole(tok, width)] * len(slots),
        out_specs=[whole(tokens, width), whole(tokens, head_dim), whole(tokens, tile), pl.BlockSpec((tokens, tile), lambda j: (0, j))],
        out_shape=[
            jax.ShapeDtypeStruct((tokens, width), bf16),
            jax.ShapeDtypeStruct((tokens, head_dim), f32),
            jax.ShapeDtypeStruct((tokens, tile), f32),
            jax.ShapeDtypeStruct((tokens, 2 * tile), bf16),
        ],
        cost_estimate=light_cost,
        name="project_kv",
    )(w, cos_table, sin_table, gain, norm, *slots)


def project_q_kernel(x_ref, w_ref, cos_ref, sin_ref, gain_ref, raw_ref, out_ref, *, head_dim, scale):
    raw = mm(x_ref[...], w_ref[...])
    raw_ref[...] = raw
    rotated_heads(raw, cos_ref, sin_ref, gain_ref, out_ref, head_dim, scale)


def project_q(x, w, cos_table, sin_table, gain, cols, tile, scale, after):
    tokens, width = x.shape
    head_dim = gain.shape[1]

    def whole(rows, cols):
        return pl.BlockSpec((rows, cols), lambda j: (0, 0))

    w_spec = pl.BlockSpec((width, tile), lambda j: (0, j))
    out_spec = pl.BlockSpec((tokens, tile), lambda j: (0, j))
    return pl.pallas_call(
        ignoring(functools.partial(project_q_kernel, head_dim=head_dim, scale=scale), 5, len(after)),
        grid=(cols // tile,),
        in_specs=[whole(tokens, width), w_spec, whole(tokens, head_dim), whole(tokens, head_dim), whole(1, head_dim)] + [any_place] * len(after),
        out_specs=[out_spec, out_spec],
        out_shape=[jax.ShapeDtypeStruct((tokens, cols), f32), jax.ShapeDtypeStruct((tokens, cols), bf16)],
        cost_estimate=light_cost,
        name="project_q",
    )(x, w, cos_table, sin_table, gain, *after)


def unproject_kernel(raw_ref, cos_ref, sin_ref, gain_ref, *refs, head_dim, sums):
    grad_refs, (out_ref, part_ref) = refs[:sums], refs[sums:]
    part = jnp.zeros((1, head_dim), f32)
    for first in range(0, out_ref.shape[1], head_dim):
        lanes = slice(first, first + head_dim)
        grad = grad_refs[0][:, lanes].astype(f32)
        for grad_ref in grad_refs[1:]:
            grad = grad + grad_ref[:, lanes].astype(f32)
        if first < raw_ref.shape[1]:
            raw = raw_ref[:, lanes]
            scale = rms_scale(raw)
            hat = raw * scale
            grad = grad * cos_ref[...] - turn(grad) * sin_ref[...]
            part = part + jnp.sum(grad * hat, axis=0, keepdims=True)
            grad = norm_back(grad * gain_ref[...], hat, scale)
        out_ref[:, lanes] = grad.astype(bf16)
    part_ref[...] = part


def unproject(raw, cos_table, sin_table, gain, grads, after, name):
    tokens, cols = raw.shape[0], grads[0].shape[1]
    head_dim = gain.shape[1]

    def first_rows(width):
        return pl.BlockSpec((tokens, width), lambda j: (0, 0))

    gain_spec = pl.BlockSpec((1, head_dim), lambda j: (0, 0))
    return pl.pallas_call(
        ignoring(functools.partial(unproject_kernel, head_dim=head_dim, sums=len(grads)), 4 + len(grads), len(after)),
        grid=(1,),
        in_specs=[first_rows(raw.shape[1]), first_rows(head_dim), first_rows(head_dim), gain_spec]
        + [first_rows(cols)] * len(grads)
        + [any_place] * len(after),
        out_specs=[first_rows(cols), gain_spec],
        out_shape=[
            jax.ShapeDtypeStruct((tokens, cols), bf16),
            jax.ShapeDtypeStruct(gain.shape, f32),
        ],
        cost_estimate=light_cost,
        name=name,
    )(raw, cos_table, sin_table, gain, *grads, *after)


def attn_back_kernel(dq_ref, dkv_ref, w_ref, rows_ref, *refs, slots):
    hidden_refs, out_refs, gain_ref = refs[:slots], refs[slots:-1], refs[-1]
    q_cols = dq_ref.shape[1]
    tok = out_refs[0].shape[0]
    total = mm_nt(dq_ref[...], w_ref[:, :q_cols]) + mm_nt(dkv_ref[...], w_ref[:, q_cols:])
    gain = jnp.zeros((1, total.shape[1]), f32)
    for slot in range(slots):
        lines = slice(slot * tok, (slot + 1) * tok)
        part = total[lines]
        gain = gain + jnp.sum(part * (hidden_refs[slot][...].astype(f32) * rows_ref[lines, :1]), axis=0, keepdims=True)
        out_refs[slot][...] = part.astype(bf16)
    gain_ref[...] = jnp.broadcast_to(gain, gain_ref.shape)


def attn_back_product(dq, dkv, w, row_scales, hidden_slots, after):
    rows, q_cols = dq.shape
    slots = len(hidden_slots)
    tok, width = hidden_slots[0].shape
    tile = min(512, width)
    slot_spec = pl.BlockSpec((tok, tile), lambda t: (0, t))
    return pl.pallas_call(
        ignoring(functools.partial(attn_back_kernel, slots=slots), 4 + slots, len(after)),
        grid=(width // tile,),
        in_specs=[
            pl.BlockSpec((rows, q_cols), lambda t: (0, 0)),
            pl.BlockSpec((rows, dkv.shape[1]), lambda t: (0, 0)),
            pl.BlockSpec((tile, q_cols + dkv.shape[1]), lambda t: (t, 0)),
            pl.BlockSpec(row_scales.shape, lambda t: (0, 0)),
        ]
        + [slot_spec] * slots
        + [any_place] * len(after),
        out_specs=[slot_spec] * slots + [pl.BlockSpec((8, tile), lambda t: (0, t))],
        out_shape=[jax.ShapeDtypeStruct((tok, width), bf16)] * slots + [jax.ShapeDtypeStruct((8, width), f32)],
        cost_estimate=light_cost,
        name="attn_back",
    )(dq, dkv, w, row_scales, *hidden_slots, *after)


def grad_attended_kernel(w_ref, *refs):
    *slot_refs, mid_ref, out_ref = refs
    tok = slot_refs[0].shape[0]
    for slot, slot_ref in enumerate(slot_refs):
        mid_ref[slot * tok:(slot + 1) * tok] = slot_ref[...]
    out_ref[...] = mm(mid_ref[...], w_ref[...]).astype(bf16)


def grad_attended_product(slots, w, cols, after):
    tok, width = slots[0].shape
    rows = tok * len(slots)

    def whole(rows, cols):
        return pl.BlockSpec((rows, cols), lambda j: (0, 0))

    return pl.pallas_call(
        ignoring(grad_attended_kernel, 1 + len(slots), len(after)),
        grid=(1,),
        in_specs=[pl.BlockSpec((width, cols), lambda j: (0, w.shape[1] // cols - 1))] + [whole(tok, width)] * len(slots) + [any_place] * len(after),
        out_specs=[whole(rows, width), whole(rows, cols)],
        out_shape=[jax.ShapeDtypeStruct((rows, width), bf16), jax.ShapeDtypeStruct((rows, cols), bf16)],
        cost_estimate=light_cost,
        name="grad_attended",
    )(w, *slots, *after)


def simple_call(kernel, arrays, shapes, name, after=()):
    vmem = pl.BlockSpec(memory_space=pltpu.VMEM)
    return pl.pallas_call(
        ignoring(kernel, len(arrays), len(after)),
        in_specs=[vmem] * len(arrays) + [any_place] * len(after),
        out_specs=[vmem] * len(shapes),
        out_shape=[jax.ShapeDtypeStruct(shape, dtype) for shape, dtype in shapes],
        cost_estimate=light_cost,
        name=name,
    )(*arrays, *after)


def add_rounded(left, right):
    return (left.astype(f32) + right.astype(f32)).astype(bf16)


def summed(refs):
    count = len(refs) // 2
    return jnp.concatenate(
        [came[...].astype(f32) + part[...].astype(f32) for came, part in zip(refs[:count], refs[count:])],
        axis=0,
    )


def store_halves(values, refs):
    rows = refs[0].shape[0]
    for i, ref in enumerate(refs):
        ref[...] = values[i * rows:(i + 1) * rows].astype(ref.dtype)


def mix_kernel(*refs, halves):
    sum_refs, (hidden_ref, norm_ref, mixed_ref, *input_refs) = refs[:2 * halves], refs[2 * halves:]
    mixed = hidden_ref[...].astype(f32) + summed(sum_refs)
    mixed_ref[...] = mixed
    store_halves(mixed * rms_scale(mixed) * norm_ref[...], input_refs)


def mid_kernel(*refs, halves):
    sum_refs, (mixed_ref, norm_ref, out_ref, grad_ref, gain_ref, *low_refs) = refs[:2 * halves], refs[2 * halves:]
    mixed = mixed_ref[...]
    scale = rms_scale(mixed)
    normed = mixed * scale
    back = summed(sum_refs)
    gain_ref[...] = jnp.sum(back * normed, axis=0, keepdims=True)
    grad = out_ref[...].astype(f32) + norm_back(back * norm_ref[...], normed, scale)
    grad_ref[...] = grad
    store_halves(grad, low_refs)


def last_kernel(*refs, halves):
    sum_refs, (grad_ref, hidden_ref, norm_ref, out_ref) = refs[:2 * halves], refs[2 * halves:]
    hidden = hidden_ref[...].astype(f32)
    scale = rms_scale(hidden)
    out_ref[...] = grad_ref[...] + norm_back(summed(sum_refs) * norm_ref[...], hidden * scale, scale)


def result_kernel(*refs):
    *sum_refs, mixed_ref, out_ref = refs
    total = sum_refs[0][...].astype(f32)
    for sum_ref in sum_refs[1:]:
        total = total + sum_ref[...].astype(f32)
    out_ref[...] = (mixed_ref[...] + total).astype(bf16)


def mark_kernel(out_ref):
    out_ref[...] = jnp.zeros_like(out_ref)


def split_kernel(x_ref, *out_refs):
    at = 0
    for out_ref in out_refs[:-1]:
        out_ref[...] = x_ref[:, at:at + out_ref.shape[1]].astype(f32)
        at += out_ref.shape[1]
    out_refs[-1][...] = x_ref[:, at:].astype(f32).T


def split_columns(x, cols, name):
    rows = x.shape[0]
    shapes = [((rows, c), f32) for c in cols[:-1]] + [((cols[-1], rows), f32)]
    return simple_call(split_kernel, [x], shapes, name)


def ffn_kernel(gate_ref, up_ref, down_ref, *refs, parts, held):
    x_refs, g_refs, refs = refs[:parts], refs[parts:2 * parts], refs[2 * parts + held:]
    grad_ref, x_ref, go_ref, *back_refs, back_ref = refs
    tile = pl.program_id(0)
    tok, size = x_refs[0].shape[0], gate_ref.shape[1]
    ff = grad_ref.shape[1] // 3

    @pl.when(tile == 0)
    def _():
        for i in range(parts):
            x_ref[i * tok:(i + 1) * tok] = x_refs[i][...]
            go_ref[i * tok:(i + 1) * tok] = g_refs[i][...]
        back_ref[...] = jnp.zeros_like(back_ref)

    x = x_ref[...]
    gate_pre = mm(x, gate_ref[...])
    up_value = mm(x, up_ref[...])
    grad_act = mm(go_ref[...], down_ref[...])
    sigmoid_gate = jax.nn.sigmoid(gate_pre)
    gated = gate_pre * sigmoid_gate
    grad_gate_pre = (
        grad_act * up_value * sigmoid_gate * (1.0 + gate_pre * (1.0 - sigmoid_gate))
    ).astype(bf16)
    grad_up_value = (grad_act * gated).astype(bf16)
    for i, values in enumerate([grad_gate_pre, grad_up_value, (gated * up_value).astype(bf16)]):
        grad_ref[:, pl.ds(pl.multiple_of(i * ff + tile * size, size), size)] = values
    back_ref[...] += mm_nt(grad_gate_pre, gate_ref[...]) + mm_nt(grad_up_value, up_ref[...])

    @pl.when(tile == pl.num_programs(0) - 1)
    def _():
        store_halves(back_ref[...], back_refs)


def feed_forward(inputs, grads, w_ffn, held, chunk, chunks):
    parts = len(inputs)
    tok, width = inputs[0].shape
    ff = w_ffn.shape[1] // 3
    size = next(s for s in (512, 384, 256, 128) if ff % s == 0)
    tiles = ff // size
    part_spec = pl.BlockSpec((tok, width), lambda t: (0, 0))

    def rows_spec(cols):
        return pl.BlockSpec((parts * tok, cols), lambda t: (chunk, 0))

    rows = parts * tok * chunks
    return pl.pallas_call(
        functools.partial(ffn_kernel, parts=parts, held=len(held)),
        grid=(tiles,),
        in_specs=[
            pl.BlockSpec((width, size), lambda t: (0, t)),
            pl.BlockSpec((width, size), lambda t: (0, tiles + t)),
            pl.BlockSpec((width, size), lambda t: (0, 2 * tiles + t)),
        ]
        + [part_spec] * (2 * parts)
        + [pl.BlockSpec(memory_space=pl.ANY)] * len(held),
        out_specs=[rows_spec(3 * ff), rows_spec(width), rows_spec(width)] + [part_spec] * parts,
        out_shape=[
            jax.ShapeDtypeStruct((rows, 3 * ff), bf16),
            jax.ShapeDtypeStruct((rows, width), bf16),
            jax.ShapeDtypeStruct((rows, width), bf16),
        ]
        + [jax.ShapeDtypeStruct((tok, width), bf16)] * parts,
        scratch_shapes=[pltpu.VMEM((parts * tok, width), f32)],
        input_output_aliases={3 + 2 * parts + i: i for i in range(len(held))},
        cost_estimate=light_cost,
        name="feed_forward",
    )(w_ffn, w_ffn, w_ffn, *inputs, *grads, *held)


def weight_grads_kernel(*refs, turns):
    *left_refs, right_ref, out_ref, turned_ref = refs
    tile = pl.program_id(0)
    for left_ref, at in zip(left_refs, turns):
        @pl.when(tile == at)
        def _(left_ref=left_ref):
            turned_ref[...] = left_ref[...].T

    rows = min(256, out_ref.shape[0])
    for first in range(0, out_ref.shape[0], rows):
        lines = slice(first, first + rows)
        out_ref[lines] = mm(turned_ref[lines], right_ref[...]).astype(bf16)


def weight_grads(lefts, right, starts, after, name):
    tokens, width = lefts[0].shape
    cols = right.shape[1]
    size = next(s for s in (512, 384, 256, 128) if all(at % s == 0 for at in (cols, *starts)))
    whole = pl.BlockSpec((tokens, width), lambda t: (0, 0))
    return pl.pallas_call(
        ignoring(functools.partial(weight_grads_kernel, turns=[at // size for at in starts]), len(lefts) + 1, len(after)),
        grid=(cols // size,),
        in_specs=[whole] * len(lefts) + [pl.BlockSpec((tokens, size), lambda t: (0, t))] + [any_place] * len(after),
        out_specs=pl.BlockSpec((width, size), lambda t: (0, t)),
        out_shape=jax.ShapeDtypeStruct((width, cols), bf16),
        scratch_shapes=[pltpu.VMEM((width, tokens), bf16)],
        cost_estimate=light_cost,
        name=name,
    )(*lefts, right, *after)


def slot_product_kernel(x_ref, w_ref, *out_refs):
    tok = out_refs[0].shape[0]
    total = mm_nt(x_ref[...], w_ref[...])
    for slot, out_ref in enumerate(out_refs):
        out_ref[...] = total[slot * tok:(slot + 1) * tok].astype(bf16)


def slot_product(x, x_block, w, w_block, depth, slots, after, name):
    rows, width = x.shape[0], w.shape[0]
    tile = min(512, width)
    out_spec = pl.BlockSpec((rows // slots, tile), lambda t: (0, t))
    return pl.pallas_call(
        ignoring(slot_product_kernel, 2, len(after)),
        grid=(width // tile,),
        in_specs=[
            pl.BlockSpec((rows, depth), lambda t: (0, x_block)),
            pl.BlockSpec((tile, depth), lambda t: (t, w_block)),
        ]
        + [any_place] * len(after),
        out_specs=[out_spec] * slots,
        out_shape=[jax.ShapeDtypeStruct((rows // slots, width), bf16)] * slots,
        cost_estimate=light_cost,
        name=name,
    )(x, w, *after)


def more_grads_kernel(left_ref, *refs, rights):
    right_refs, out_ref, turned_ref = refs[:rights], refs[-2], refs[-1]
    tile = pl.program_id(0)

    @pl.when(tile == 0)
    def _():
        turned_ref[...] = left_ref[...].T

    def run(right_ref):
        rows = min(256, out_ref.shape[0])
        for first in range(0, out_ref.shape[0], rows):
            lines = slice(first, first + rows)
            out_ref[lines] = mm(turned_ref[lines], right_ref[...]).astype(bf16)

    for i, right_ref in enumerate(right_refs):
        pl.when(tile == i)(functools.partial(run, right_ref))


def more_grads(left, rights, held, at, blocks, after, name):
    tokens, width = left.shape
    size = rights[0].shape[1]
    return pl.pallas_call(
        ignoring(functools.partial(more_grads_kernel, rights=len(rights)), 1 + len(rights), len(held) + len(after)),
        grid=(len(rights),),
        in_specs=[pl.BlockSpec((tokens, width), lambda t: (0, 0))]
        + [pl.BlockSpec((tokens, size), lambda t: (0, 0))] * len(rights)
        + [any_place] * (len(held) + len(after)),
        out_specs=pl.BlockSpec((width, size), lambda t: (0, at + t)),
        out_shape=jax.ShapeDtypeStruct((width, blocks * size), bf16),
        scratch_shapes=[pltpu.VMEM((width, tokens), bf16)],
        input_output_aliases={1 + len(rights) + i: 0 for i in range(len(held))},
        cost_estimate=light_cost,
        name=name,
    )(left, *rights, *held, *after)


def fold_kernel(near_ref, got_ref, *out_refs):
    rows = out_refs[0].shape[0]
    for i, out_ref in enumerate(out_refs):
        lines = slice((i + 1) * rows, (i + 2) * rows)
        out_ref[...] = (near_ref[lines].astype(f32) + got_ref[lines].astype(f32)).astype(bf16)


def fold_blocks(near, got, count, after):
    vmem = pl.BlockSpec(memory_space=pltpu.VMEM)
    shape = jax.ShapeDtypeStruct((near.shape[0] // count, near.shape[1]), bf16)
    return pl.pallas_call(
        ignoring(fold_kernel, 2, len(after)),
        in_specs=[vmem, vmem] + [any_place] * len(after),
        out_specs=[vmem] * (count - 1),
        out_shape=[shape] * (count - 1),
        cost_estimate=light_cost,
        name="fold_blocks",
    )(near, got, *after)


def body(
    hidden_in,
    doc_lengths,
    attn_norm,
    query_weight,
    key_weight,
    value_weight,
    query_gain,
    key_gain,
    output_weight,
    ffn_norm,
    gate_weight,
    up_weight,
    down_weight,
    grad_out,
):
    dp_count = lax.axis_size("dp")
    mp_count = lax.axis_size("mp")
    slots = mp_count
    tok, width = hidden_in.shape
    group_rows = tok * mp_count
    head_dim = query_gain.shape[0]
    half_dim = head_dim // 2
    q_cols = query_weight.shape[1]
    k_cols = key_weight.shape[1]
    kv_local = k_cols // head_dim
    repeat = q_cols // k_cols
    ff = gate_weight.shape[1]
    group = lax.axis_index("dp")
    my_z = lax.axis_index("mp")
    score_scale = head_dim ** (-0.5)
    ring = [(i, (i + 1) % mp_count) for i in range(mp_count)]
    near_masks = list(range(0, dp_count, 2))
    masks = near_masks + [mask + 1 for mask in near_masks]
    far_masks = near_masks[1:]

    def tie(value, *others):
        return lax.optimization_barrier((value,) + others)[0]

    def shift(values):
        return lax.ppermute(values, "mp", ring)

    def swap(values, mask):
        return lax.ppermute(values, "dp", [(i, i ^ mask) for i in range(dp_count)])

    reach = (min(longest, group_rows * dp_count) - 2) // group_rows + 1

    def needs(reader, owner):
        first = reader // 2 * 2
        return owner <= first + 1 and owner >= first - reach

    def swap_forward(values, mask):
        pairs = [(i, i ^ mask) for i in range(dp_count) if needs(i ^ mask, i)]
        return lax.ppermute(values, "dp", pairs)

    def swap_back(values, mask):
        pairs = [(i, i ^ mask) for i in range(dp_count) if needs(i, i ^ mask)]
        return lax.ppermute(values, "dp", pairs)

    half = dp_count // 2
    halves = 2
    part_rows = tok // halves
    ids = jnp.array(masks, jnp.int32)
    mask_blocks = group ^ ids
    attn_norm = attn_norm.reshape(1, width)
    ffn_norm = ffn_norm.reshape(1, width)
    part_shape = ((part_rows, width), bf16)

    def tie_all(values, *others):
        return list(lax.optimization_barrier((*values, *others)))[:len(values)]

    def order(values, others):
        both = lax.optimization_barrier((*values, *others))
        return list(both[:len(values)]), list(both[len(values):])

    def mark(*operands):
        (tiny,) = simple_call(mark_kernel, [], [((8, 128), f32)], "mark", operands)
        return [swap(tiny, 1)]

    def flat(slot_lists):
        return [part for slot in slot_lists for part in slot]

    def by_slot(parts):
        return [list(parts[i:i + halves]) for i in range(0, len(parts), halves)]

    def shift_all(parts):
        return [shift(part) for part in parts]

    def ring_add(came, own):
        return [shift(add_rounded(one, other)) for one, other in zip(came, own)]

    w_attn_own = jnp.concatenate([query_weight, key_weight, value_weight, output_weight.T], axis=1)
    w_ffn_own = jnp.concatenate([gate_weight, up_weight, down_weight.T], axis=1)
    w_attn = lax.all_gather(w_attn_own, "dp", axis=0, tiled=True)
    w_ffn = tie(lax.all_gather(w_ffn_own, "dp", axis=0, tiled=True), w_attn)

    doc_ends = jnp.cumsum(doc_lengths)
    slot_offset = ((my_z - jnp.arange(slots, dtype=jnp.int32)) % mp_count) * tok
    places = (
        group * group_rows
        + slot_offset[:, None]
        + jnp.arange(tok, dtype=jnp.int32)[None, :]
    )
    before = doc_ends[None, None, :] <= places[:, :, None]
    starts = jnp.sum(jnp.where(before, doc_lengths[None, None, :], 0), axis=-1)
    position = (places - starts).reshape(group_rows)
    inverse = rope_base ** (-(2.0 * jnp.arange(half_dim, dtype=f32)) / head_dim)
    angles = position.astype(f32)[:, None] * inverse[None, :]
    cos_table, sin_table = jnp.cos(angles), jnp.sin(angles)
    cos_table = jnp.concatenate([cos_table, cos_table], axis=1)
    sin_table = jnp.concatenate([-sin_table, sin_table], axis=1)

    sub = min(4, slots)
    key_base = mask_blocks[:, None] * group_rows + slot_offset[None, :]
    blocks = dp_count * slots // sub
    key_base = key_base.reshape(blocks, sub)
    q_first, q_last = places[:, 0], places[:, -1]
    s_first, s_last = starts[:, 0], starts[:, -1]
    piece_lo, piece_hi = key_base[None], key_base[None] + tok - 1
    some = (piece_lo <= q_last[:, None, None]) & (s_first[:, None, None] <= piece_hi)
    every = (piece_hi <= q_first[:, None, None]) & (s_last[:, None, None] <= piece_lo)
    flags = jnp.where(jnp.all(every, -1), 2, jnp.any(some, -1).astype(jnp.int32)).astype(jnp.int32)
    flags = jnp.where(jnp.all(flags == 2, axis=0), 2, jnp.any(flags > 0, axis=0).astype(jnp.int32))
    key_base = key_base.reshape(-1)
    lane_places = jnp.tile(jnp.stack([starts, places]), (1, 1, repeat)).reshape(2, -1)
    row_places = lane_places.T

    hidden_slots = [[hidden_in[i * part_rows:(i + 1) * part_rows] for i in range(halves)]]
    for slot in range(1, slots):
        came = shift_all(hidden_slots[-1])
        if slot == 1:
            came = tie_all(came, cos_table, sin_table, lane_places, w_ffn_own)
        hidden_slots.append(came)
    q_gain, k_gain = query_gain.reshape(1, head_dim), key_gain.reshape(1, head_dim)
    attn_input, row_scales, key_raw, kv_own = project_kv(
        flat(hidden_slots), attn_norm, w_attn, cos_table, sin_table, k_gain, repeat, k_cols
    )
    kv_came = [swap_forward(kv_own, mask) for mask in far_masks]
    grad_slots = [tie_all([grad_out[i * part_rows:(i + 1) * part_rows] for i in range(halves)], *hidden_slots[-1])]
    grad_slots.append(tie_all(shift_all(grad_slots[-1]), kv_own))
    query_raw, query_rot = project_q(
        tie(attn_input, kv_own, *grad_slots[-1]), w_attn, cos_table, sin_table, q_gain, q_cols, k_cols,
        score_scale * log2_e, [flags, key_base, row_places],
    )
    (query_rot,), grad_slots[-1] = order([query_rot], grad_slots[-1])
    for slot in range(2, slots):
        came = shift_all(grad_slots[-1])
        if slot == 2:
            came = tie_all(came, query_rot)
            kv_came = tie_all(kv_came, *came)
        grad_slots.append(came)
    kv_near = [kv_own] + tie_all(kv_came, query_rot)
    kv_pieces = kv_near + [swap(piece, 1) for piece in kv_near]

    keys_total = dp_count * group_rows
    head_rows = repeat * tok
    smem = pl.BlockSpec(memory_space=pltpu.SMEM)
    any_spec = pl.BlockSpec(memory_space=pl.ANY)
    all_rows = slots * head_rows
    lane_spec = pl.BlockSpec((2, all_rows), lambda h: (0, 0))
    row_spec = pl.BlockSpec((all_rows, 2), lambda h: (0, 0))
    q_spec = pl.BlockSpec((group_rows, repeat * head_dim), lambda h: (0, h))
    lse_spec = pl.BlockSpec((None, 1, all_rows), lambda h: (h, 0, 0))
    dims = dict(
        tok=tok, sub=sub, slots=slots, blocks=blocks, pieces=dp_count, repeat=repeat, head_dim=head_dim
    )
    kv_scratch = pltpu.VMEM((keys_total, 2 * k_cols), bf16)
    attended_low, lse = pl.pallas_call(
        functools.partial(attn_fwd_kernel, **dims),
        grid=(kv_local,),
        in_specs=[smem, smem, row_spec, q_spec] + [any_spec] * dp_count,
        out_specs=[q_spec, lse_spec],
        out_shape=[
            jax.ShapeDtypeStruct((group_rows, q_cols), bf16),
            jax.ShapeDtypeStruct((kv_local, 1, all_rows), f32),
        ],
        scratch_shapes=[
            kv_scratch,
            pltpu.VMEM((all_rows, 2 * head_dim), f32),
            pltpu.VMEM((tok * sub, 2 * head_dim), bf16),
            pltpu.VMEM((all_rows, head_dim), bf16),
            pltpu.SemaphoreType.DMA((dp_count,)),
        ],
        cost_estimate=light_cost,
        name="attn_fwd",
    )(flags, key_base, row_places, query_rot, *kv_pieces)

    grad_slots[slots - 1] = tie_all(grad_slots[slots - 1], attended_low)
    parts = by_slot(slot_product(attended_low, 0, w_attn, 2 * k_cols // q_cols + 1, q_cols, slots * halves, [], "attn_out"))
    came = shift_all(tie_all(parts[1], *grad_slots[-1]))
    for slot in range(2, slots):
        came = ring_add(came, parts[slot])
    mixed_rows, *ffn_input = simple_call(
        functools.partial(mix_kernel, halves=halves),
        [*came, *parts[0], hidden_in, ffn_norm],
        [((tok, width), f32)] + [part_shape] * halves,
        "mix",
    )

    ffn_slots = [ffn_input, shift_all(ffn_input)]
    held, parts = [], []
    for first in range(0, slots, 2):
        *held, = feed_forward(
            flat(ffn_slots[first:first + 2]), flat(grad_slots[first:first + 2]), w_ffn, held, first // 2, slots // 2
        )
        held, back = held[:3], held[3:]
        parts += by_slot(back)
        if first + 2 < slots:
            ffn_slots.append(tie_all(shift_all(ffn_slots[-1]), *back))
            ffn_slots.append(shift_all(ffn_slots[-1]))
    ffn_right, ffn_all, grad_all = held

    came = shift_all(tie_all(parts[1], *ffn_slots[-1]))
    ffn_part = weight_grads([ffn_all, grad_all], tie(ffn_right, *came), [0, 2 * ff], [], "ffn_grads")
    for slot in range(2, slots):
        came = ring_add(came, parts[slot])
        if slot == 2:
            came = tie_all(came, ffn_part)
    grad_ffn = lax.psum_scatter(ffn_part, "dp", scatter_dimension=0, tiled=True)
    grad_mixed, grad_ffn_norm, *mid_first = simple_call(
        functools.partial(mid_kernel, halves=halves),
        [*came, *parts[0], mixed_rows, ffn_norm, grad_out],
        [((tok, width), f32), ((1, width), f32)] + [part_shape] * halves,
        "mid",
    )
    mid_slots = [mid_first]
    result_parts = slot_product(ffn_right, 2, w_ffn, 2, ff, slots, [], "ffn_out")
    for slot in range(1, slots):
        came = shift_all(mid_slots[-1])
        if slot == 1:
            came[1:], result_parts = order(came[1:], result_parts)
        mid_slots.append(came)

    result_came = [
        lax.ppermute(result_parts[slot], "mp", [(i, (i - slot) % mp_count) for i in range(mp_count)])
        for slot in range(1, slots)
    ]

    grad_mid, grad_attended = grad_attended_product(flat(mid_slots), w_attn, q_cols, [])
    near_spec = pl.BlockSpec((keys_total // 2, 2 * k_cols), lambda h: (0, 0))
    near_shape = jax.ShapeDtypeStruct((keys_total // 2, 2 * k_cols), bf16)
    dq_rot, dkv_near, dkv_far = pl.pallas_call(
        functools.partial(
            attn_bwd_kernel, **dims, dq_scale=score_scale, dk_scale=1.0 / log2_e
        ),
        grid=(kv_local,),
        in_specs=[smem, smem, lane_spec, q_spec, lse_spec, q_spec, q_spec] + [any_spec] * dp_count,
        out_specs=[q_spec, near_spec, near_spec],
        out_shape=[jax.ShapeDtypeStruct((group_rows, q_cols), f32), near_shape, near_shape],
        scratch_shapes=[
            kv_scratch,
            pltpu.VMEM((all_rows, head_dim), bf16),
            pltpu.VMEM((all_rows, head_dim), bf16),
            pltpu.VMEM((head_dim, all_rows), f32),
            pltpu.VMEM((1, all_rows), f32),
            pltpu.VMEM((tok * sub, head_dim), f32),
            pltpu.VMEM((tok * sub, head_dim), f32),
            pltpu.SemaphoreType.DMA((dp_count,)),
        ],
        cost_estimate=light_cost,
        name="attn_bwd",
    )(flags, key_base, lane_places, query_rot, lse, attended_low, grad_attended, *kv_pieces)

    dkv_got = swap(dkv_far, 1)
    dkv_sent = fold_blocks(dkv_near, dkv_got, half, [])
    dkv_came = [swap_back(sent, mask) for sent, mask in zip(dkv_sent, far_masks)]
    marked = mark(*dkv_sent)
    dq_raw, query_gain_part = unproject(query_raw, cos_table, sin_table, q_gain, [dq_rot], marked, "unproject_q")
    attn_part = more_grads(grad_mid, [attended_low], [], 2, 3, marked, "out_grads")
    attn_part = more_grads(attn_input, [dq_raw], [attn_part], 0, 3, [], "q_grads")
    dkv_raw, key_gain_part = unproject(
        key_raw, cos_table, sin_table, k_gain, [dkv_near, dkv_got] + dkv_came, [attn_part, *result_came], "unproject_kv"
    )

    attn_part = more_grads(attn_input, [dkv_raw], [attn_part], 1, 3, [grad_ffn], "kv_grads")
    grad_attn = lax.psum_scatter(attn_part, "dp", scatter_dimension=0, tiled=True)
    *parts, attn_gain_part = attn_back_product(
        dq_raw, dkv_raw, w_attn, row_scales, flat(hidden_slots), [attn_part]
    )
    parts = by_slot(parts)
    came = shift_all(parts[1])
    came, (attn_gain_part,) = order(came, [attn_gain_part])
    small = jnp.concatenate(
        [attn_gain_part[0], grad_ffn_norm[0], query_gain_part[0], key_gain_part[0]]
    ).reshape(-1, head_dim)
    small = small + swap(small, 1)
    for slot in range(2, slots):
        came = ring_add(came, parts[slot])
        if slot == 2:
            grads = split_columns(grad_ffn, [ff, ff, ff], "split_ffn")
            came, (small, grad_gate, grad_up, grad_down) = order(came, [small, *grads])
            small = small + sum(swap(small, mask) for mask in far_masks)
    came, (small,) = order(came, [small])
    turns = [[(i, (i + by) % mp_count) for i in range(mp_count)] for by in range(1, mp_count)]
    small = small + sum(lax.ppermute(small, "mp", turn) for turn in turns)
    (grad_hidden,) = simple_call(
        functools.partial(last_kernel, halves=halves),
        [*came, *parts[0], grad_mixed, hidden_in, attn_norm],
        [((tok, width), f32)],
        "last",
    )
    (result,) = simple_call(
        result_kernel, [result_parts[0], *result_came, mixed_rows], [((tok, width), bf16)], "result"
    )
    grad_query, grad_key, grad_value, grad_out_weight = split_columns(
        grad_attn, [q_cols, k_cols, k_cols, q_cols], "split_attn"
    )

    small = small.reshape(-1)
    return (
        result,
        grad_hidden,
        small[:width],
        grad_query,
        grad_key,
        grad_value,
        small[2 * width:2 * width + head_dim],
        small[2 * width + head_dim:],
        grad_out_weight,
        small[width:2 * width],
        grad_gate,
        grad_up,
        grad_down,
    )


def solution(mesh):
    rows = P(("dp", "mp"), None)
    placed = (
        rows,
        P(),
        P(),
        P("dp", "mp"),
        P("dp", "mp"),
        P("dp", "mp"),
        P(),
        P(),
        P("mp", "dp"),
        P(),
        P("dp", "mp"),
        P("dp", "mp"),
        P("mp", "dp"),
        rows,
    )
    return jax.shard_map(
        body,
        mesh=mesh,
        in_specs=placed,
        out_specs=(
            rows,
            rows,
            P(),
            P("dp", "mp"),
            P("dp", "mp"),
            P("dp", "mp"),
            P(),
            P(),
            P("mp", "dp"),
            P(),
            P("dp", "mp"),
            P("dp", "mp"),
            P("mp", "dp"),
        ),
        check_vma=False,
    )
```

```python
import functools

import jax
import jax.numpy as jnp
from jax import lax
from jax.experimental import pallas as pl
from jax.experimental.pallas import tpu as pltpu
from jax.sharding import PartitionSpec as P

eps_norm = 1e-06
rope_base = 1000000.0
log2_e = 1.4426950408889634
bf16 = jnp.bfloat16
f32 = jnp.float32
longest = 2048
light_cost = pl.CostEstimate(flops=1 << 20, bytes_accessed=1 << 16, transcendentals=0)


def rms_scale(values):
    return lax.rsqrt(jnp.mean(values * values, axis=-1, keepdims=True) + eps_norm)


def norm_back(grad_hat, normed, scale_rows):
    return scale_rows * (grad_hat - normed * jnp.mean(grad_hat * normed, axis=-1, keepdims=True))


def mm(left, right):
    return jnp.dot(left, right, preferred_element_type=f32)


def mm_nt(left, right):
    return lax.dot_general(left, right, (((1,), (1,)), ((), ())), preferred_element_type=f32)


def mm_tn(left, right):
    return lax.dot_general(left, right, (((0,), (0,)), ((), ())), preferred_element_type=f32)


def load_pieces(refs, held_ref, sem_ref):
    rows = refs[0].shape[0]
    copies = [
        pltpu.make_async_copy(ref, held_ref.at[pl.ds(i * rows, rows), :], sem_ref.at[i])
        for i, ref in enumerate(refs)
    ]
    for copy in copies:
        copy.start()
    for copy in copies:
        copy.wait()


def gather_rows(src_ref, dst_ref, tok, repeat):
    dim = dst_ref.shape[1]
    for slot in range(src_ref.shape[0] // tok):
        for i in range(repeat):
            at = (slot * repeat + i) * tok
            dst_ref[at:at + tok] = src_ref[slot * tok:(slot + 1) * tok, i * dim:(i + 1) * dim]


def head_lanes(dim):
    head, heads = pl.program_id(0), pl.num_programs(0)
    return pl.ds(pl.multiple_of(head * dim, dim), dim), pl.ds(pl.multiple_of((heads + head) * dim, dim), dim)


def attn_fwd_kernel(flags_ref, base_ref, places_ref, q_ref, *refs, tok, sub, slots, blocks, pieces, repeat, head_dim):
    kv_refs, (o_ref, lse_ref, kv_ref, acc_ref, values_ref, rows_ref, sem_ref) = refs[:pieces], refs[pieces:]
    kb, chunk = tok * sub, tok * repeat
    k_lanes, v_lanes = head_lanes(head_dim)

    @pl.when(pl.program_id(0) == 0)
    def _():
        load_pieces(kv_refs, kv_ref, sem_ref)
        values_ref[:, head_dim:] = jnp.ones((kb, head_dim), bf16)

    gather_rows(q_ref, rows_ref, tok, repeat)
    acc_ref[...] = jnp.zeros_like(acc_ref)

    def run(block, keys, masked):
        values_ref[:, :head_dim] = kv_ref[keys, v_lanes]
        k = kv_ref[keys, k_lanes]
        for slot in range(slots):
            lines = slice(slot * chunk, (slot + 1) * chunk)
            p = jnp.exp2(mm_nt(rows_ref[lines], k))
            if masked:
                start, place = places_ref[lines, 0:1], places_ref[lines, 1:2]
                at = lax.broadcasted_iota(jnp.int32, (chunk, tok), 1)
                bases = [base_ref[block * sub + piece] for piece in range(sub)]
                allowed = jnp.concatenate([(at >= start - base) & (at <= place - base) for base in bases], axis=1)
                p = jnp.where(allowed, p, 0.0)
            acc_ref[lines] += mm(p.astype(bf16), values_ref[...])

    @pl.loop(0, blocks)
    def _(block):
        keys = pl.ds(pl.multiple_of(block * kb, kb), kb)
        pl.when(flags_ref[block] == 1)(lambda: run(block, keys, True))
        pl.when(flags_ref[block] == 2)(lambda: run(block, keys, False))

    for slot in range(slots):
        total = acc_ref[slot * chunk:(slot + 1) * chunk, head_dim:]
        out = acc_ref[slot * chunk:(slot + 1) * chunk, :head_dim] * (1.0 / total)
        for i in range(repeat):
            o_ref[slot * tok:(slot + 1) * tok, i * head_dim:(i + 1) * head_dim] = out[i * tok:(i + 1) * tok].astype(bf16)
        lse_ref[:, slot * chunk:(slot + 1) * chunk] = jnp.log2(total).T[:1]


def attn_bwd_kernel(flags_ref, base_ref, places_ref, q_ref, lse_ref, o_ref, do_ref, *refs, tok, sub, slots, blocks, pieces, repeat, head_dim, dq_scale, dk_scale):
    kv_refs = refs[:pieces]
    dq_ref, near_ref, far_ref, kv_ref, rows_ref, grads_ref, dqt_ref, delta_ref, dka_ref, dva_ref, sem_ref = refs[pieces:]
    kb, chunk = tok * sub, tok * repeat
    k_lanes, v_lanes = head_lanes(head_dim)

    @pl.when(pl.program_id(0) == 0)
    def _():
        load_pieces(kv_refs, kv_ref, sem_ref)

    gather_rows(q_ref, rows_ref, tok, repeat)
    gather_rows(do_ref, grads_ref, tok, repeat)
    dqt_ref[...] = jnp.zeros_like(dqt_ref)
    for slot in range(slots):
        for i in range(repeat):
            lines, lanes = slice(slot * tok, (slot + 1) * tok), slice(i * head_dim, (i + 1) * head_dim)
            prod = do_ref[lines, lanes].astype(f32) * o_ref[lines, lanes].astype(f32)
            at = (slot * repeat + i) * tok
            delta_ref[:, at:at + tok] = jnp.sum(prod.T, axis=0, keepdims=True)

    def run(block, keys, masked):
        k = kv_ref[keys, k_lanes]
        v = kv_ref[keys, v_lanes]
        kt = k.T
        for slot in range(slots):
            lanes = slice(slot * chunk, (slot + 1) * chunk)
            q = rows_ref[lanes]
            do = grads_ref[lanes]
            p = jnp.exp2(mm_nt(k, q) - lse_ref[:, lanes])
            if masked:
                start, place = places_ref[0:1, lanes], places_ref[1:2, lanes]
                at = lax.broadcasted_iota(jnp.int32, (tok, chunk), 0)
                bases = [base_ref[block * sub + piece] for piece in range(sub)]
                allowed = jnp.concatenate([(at >= start - base) & (at <= place - base) for base in bases], axis=0)
                p = jnp.where(allowed, p, 0.0)
            ds = (p * (mm_nt(v, do) - delta_ref[:, lanes])).astype(bf16)
            dva_ref[...] += mm(p.astype(bf16), do)
            dka_ref[...] += mm(ds, q)
            dqt_ref[:, lanes] += mm(kt, ds)

    @pl.loop(0, blocks)
    def _(block):
        keys = pl.ds(pl.multiple_of(block * kb, kb), kb)
        dka_ref[...] = jnp.zeros_like(dka_ref)
        dva_ref[...] = jnp.zeros_like(dva_ref)
        pl.when(flags_ref[block] == 1)(lambda: run(block, keys, True))
        pl.when(flags_ref[block] == 2)(lambda: run(block, keys, False))

        @pl.when(block < blocks // 2)
        def _():
            near_ref[keys, k_lanes] = (dka_ref[...] * dk_scale).astype(bf16)
            near_ref[keys, v_lanes] = dva_ref[...].astype(bf16)

        @pl.when(block >= blocks // 2)
        def _():
            far = pl.ds(pl.multiple_of(block * kb - blocks // 2 * kb, kb), kb)
            far_ref[far, k_lanes] = (dka_ref[...] * dk_scale).astype(bf16)
            far_ref[far, v_lanes] = dva_ref[...].astype(bf16)

    for slot in range(slots):
        out = (dqt_ref[:, slot * chunk:(slot + 1) * chunk] * dq_scale).T
        for i in range(repeat):
            dq_ref[slot * tok:(slot + 1) * tok, i * head_dim:(i + 1) * head_dim] = out[i * tok:(i + 1) * tok]


def turn(values):
    half = values.shape[-1] // 2
    return jnp.concatenate([values[:, half:], values[:, :half]], axis=1)


def ignoring(kernel, at, count):
    def reduced(*refs):
        kernel(*refs[:at], *refs[at + count:])

    return reduced


any_place = pl.BlockSpec(memory_space=pl.ANY)


def rotated_heads(raw, cos_ref, sin_ref, gain_ref, out_ref, head_dim, scale):
    for first in range(0, raw.shape[1], head_dim):
        lanes = slice(first, first + head_dim)
        hat = raw[:, lanes] * rms_scale(raw[:, lanes]) * gain_ref[...]
        out_ref[:, lanes] = ((hat * cos_ref[...] + turn(hat) * sin_ref[...]) * scale).astype(bf16)


def project_kv_kernel(w_ref, cos_ref, sin_ref, gain_ref, norm_ref, *refs, head_dim):
    *slot_refs, x_ref, rows_ref, raw_ref, out_ref = refs
    tok = slot_refs[0].shape[0]
    step = pl.program_id(0)

    @pl.when(step == 0)
    def _():
        for slot, slot_ref in enumerate(slot_refs):
            lines = slice(slot * tok, (slot + 1) * tok)
            values = slot_ref[...].astype(f32)
            scale = rms_scale(values)
            x_ref[lines] = (values * scale * norm_ref[...]).astype(bf16)
            rows_ref[lines] = jnp.broadcast_to(scale, (tok, rows_ref.shape[1]))

    raw = mm(x_ref[...], w_ref[...])

    @pl.when(step == 0)
    def _():
        raw_ref[...] = raw
        rotated_heads(raw, cos_ref, sin_ref, gain_ref, out_ref, head_dim, 1.0)

    @pl.when(step == 1)
    def _():
        out_ref[...] = raw.astype(bf16)


def project_kv(slots, norm, w, cos_table, sin_table, gain, first, tile):
    tok, width = slots[0].shape
    tokens, head_dim = tok * len(slots), gain.shape[1]

    def whole(rows, cols):
        return pl.BlockSpec((rows, cols), lambda j: (0, 0))

    w_spec = pl.BlockSpec((width, tile), lambda j: (0, j + first))
    return pl.pallas_call(
        functools.partial(project_kv_kernel, head_dim=head_dim),
        grid=(2,),
        in_specs=[w_spec, whole(tokens, head_dim), whole(tokens, head_dim), whole(1, head_dim), whole(1, width)]
        + [whole(tok, width)] * len(slots),
        out_specs=[whole(tokens, width), whole(tokens, head_dim), whole(tokens, tile), pl.BlockSpec((tokens, tile), lambda j: (0, j))],
        out_shape=[
            jax.ShapeDtypeStruct((tokens, width), bf16),
            jax.ShapeDtypeStruct((tokens, head_dim), f32),
            jax.ShapeDtypeStruct((tokens, tile), f32),
            jax.ShapeDtypeStruct((tokens, 2 * tile), bf16),
        ],
        cost_estimate=light_cost,
        name="project_kv",
    )(w, cos_table, sin_table, gain, norm, *slots)


def project_q_kernel(x_ref, w_ref, cos_ref, sin_ref, gain_ref, raw_ref, out_ref, *, head_dim, scale):
    raw = mm(x_ref[...], w_ref[...])
    raw_ref[...] = raw
    rotated_heads(raw, cos_ref, sin_ref, gain_ref, out_ref, head_dim, scale)


def project_q(x, w, cos_table, sin_table, gain, cols, tile, scale, after):
    tokens, width = x.shape
    head_dim = gain.shape[1]

    def whole(rows, cols):
        return pl.BlockSpec((rows, cols), lambda j: (0, 0))

    w_spec = pl.BlockSpec((width, tile), lambda j: (0, j))
    out_spec = pl.BlockSpec((tokens, tile), lambda j: (0, j))
    return pl.pallas_call(
        ignoring(functools.partial(project_q_kernel, head_dim=head_dim, scale=scale), 5, len(after)),
        grid=(cols // tile,),
        in_specs=[whole(tokens, width), w_spec, whole(tokens, head_dim), whole(tokens, head_dim), whole(1, head_dim)] + [any_place] * len(after),
        out_specs=[out_spec, out_spec],
        out_shape=[jax.ShapeDtypeStruct((tokens, cols), f32), jax.ShapeDtypeStruct((tokens, cols), bf16)],
        cost_estimate=light_cost,
        name="project_q",
    )(x, w, cos_table, sin_table, gain, *after)


def unproject_kernel(raw_ref, cos_ref, sin_ref, gain_ref, *refs, head_dim, sums):
    grad_refs, (out_ref, part_ref) = refs[:sums], refs[sums:]
    part = jnp.zeros((1, head_dim), f32)
    for first in range(0, out_ref.shape[1], head_dim):
        lanes = slice(first, first + head_dim)
        grad = grad_refs[0][:, lanes].astype(f32)
        for grad_ref in grad_refs[1:]:
            grad = grad + grad_ref[:, lanes].astype(f32)
        if first < raw_ref.shape[1]:
            raw = raw_ref[:, lanes]
            scale = rms_scale(raw)
            hat = raw * scale
            grad = grad * cos_ref[...] - turn(grad) * sin_ref[...]
            part = part + jnp.sum(grad * hat, axis=0, keepdims=True)
            grad = norm_back(grad * gain_ref[...], hat, scale)
        out_ref[:, lanes] = grad.astype(bf16)
    part_ref[...] = part


def unproject(raw, cos_table, sin_table, gain, grads, after, name):
    tokens, cols = raw.shape[0], grads[0].shape[1]
    head_dim = gain.shape[1]

    def first_rows(width):
        return pl.BlockSpec((tokens, width), lambda j: (0, 0))

    gain_spec = pl.BlockSpec((1, head_dim), lambda j: (0, 0))
    return pl.pallas_call(
        ignoring(functools.partial(unproject_kernel, head_dim=head_dim, sums=len(grads)), 4 + len(grads), len(after)),
        grid=(1,),
        in_specs=[first_rows(raw.shape[1]), first_rows(head_dim), first_rows(head_dim), gain_spec]
        + [first_rows(cols)] * len(grads)
        + [any_place] * len(after),
        out_specs=[first_rows(cols), gain_spec],
        out_shape=[
            jax.ShapeDtypeStruct((tokens, cols), bf16),
            jax.ShapeDtypeStruct(gain.shape, f32),
        ],
        cost_estimate=light_cost,
        name=name,
    )(raw, cos_table, sin_table, gain, *grads, *after)


def attn_back_kernel(dq_ref, dkv_ref, w_ref, rows_ref, *refs, slots):
    hidden_refs, out_refs, gain_ref = refs[:slots], refs[slots:-1], refs[-1]
    q_cols = dq_ref.shape[1]
    tok = out_refs[0].shape[0]
    total = mm_nt(dq_ref[...], w_ref[:, :q_cols]) + mm_nt(dkv_ref[...], w_ref[:, q_cols:])
    gain = jnp.zeros((1, total.shape[1]), f32)
    for slot in range(slots):
        lines = slice(slot * tok, (slot + 1) * tok)
        part = total[lines]
        gain = gain + jnp.sum(part * (hidden_refs[slot][...].astype(f32) * rows_ref[lines, :1]), axis=0, keepdims=True)
        out_refs[slot][...] = part.astype(bf16)
    gain_ref[...] = jnp.broadcast_to(gain, gain_ref.shape)


def attn_back_product(dq, dkv, w, row_scales, hidden_slots, after):
    rows, q_cols = dq.shape
    slots = len(hidden_slots)
    tok, width = hidden_slots[0].shape
    tile = min(1024, width)
    slot_spec = pl.BlockSpec((tok, tile), lambda t: (0, t))
    return pl.pallas_call(
        ignoring(functools.partial(attn_back_kernel, slots=slots), 4 + slots, len(after)),
        grid=(width // tile,),
        in_specs=[
            pl.BlockSpec((rows, q_cols), lambda t: (0, 0)),
            pl.BlockSpec((rows, dkv.shape[1]), lambda t: (0, 0)),
            pl.BlockSpec((tile, q_cols + dkv.shape[1]), lambda t: (t, 0)),
            pl.BlockSpec(row_scales.shape, lambda t: (0, 0)),
        ]
        + [slot_spec] * slots
        + [any_place] * len(after),
        out_specs=[slot_spec] * slots + [pl.BlockSpec((8, tile), lambda t: (0, t))],
        out_shape=[jax.ShapeDtypeStruct((tok, width), bf16)] * slots + [jax.ShapeDtypeStruct((8, width), f32)],
        cost_estimate=light_cost,
        name="attn_back",
    )(dq, dkv, w, row_scales, *hidden_slots, *after)


def grad_attended_kernel(w_ref, *refs):
    *slot_refs, mid_ref, out_ref = refs
    tok = slot_refs[0].shape[0]
    for slot, slot_ref in enumerate(slot_refs):
        mid_ref[slot * tok:(slot + 1) * tok] = slot_ref[...]
    out_ref[...] = mm(mid_ref[...], w_ref[...]).astype(bf16)


def grad_attended_product(slots, w, cols, after):
    tok, width = slots[0].shape
    rows = tok * len(slots)

    def whole(rows, cols):
        return pl.BlockSpec((rows, cols), lambda j: (0, 0))

    return pl.pallas_call(
        ignoring(grad_attended_kernel, 1 + len(slots), len(after)),
        grid=(1,),
        in_specs=[pl.BlockSpec((width, cols), lambda j: (0, w.shape[1] // cols - 1))] + [whole(tok, width)] * len(slots) + [any_place] * len(after),
        out_specs=[whole(rows, width), whole(rows, cols)],
        out_shape=[jax.ShapeDtypeStruct((rows, width), bf16), jax.ShapeDtypeStruct((rows, cols), bf16)],
        cost_estimate=light_cost,
        name="grad_attended",
    )(w, *slots, *after)


def simple_call(kernel, arrays, shapes, name, after=()):
    vmem = pl.BlockSpec(memory_space=pltpu.VMEM)
    return pl.pallas_call(
        ignoring(kernel, len(arrays), len(after)),
        in_specs=[vmem] * len(arrays) + [any_place] * len(after),
        out_specs=[vmem] * len(shapes),
        out_shape=[jax.ShapeDtypeStruct(shape, dtype) for shape, dtype in shapes],
        cost_estimate=light_cost,
        name=name,
    )(*arrays, *after)


def add_rounded(left, right):
    return (left.astype(f32) + right.astype(f32)).astype(bf16)


def summed(refs):
    count = len(refs) // 2
    return jnp.concatenate(
        [came[...].astype(f32) + part[...].astype(f32) for came, part in zip(refs[:count], refs[count:])],
        axis=0,
    )


def store_halves(values, refs):
    rows = refs[0].shape[0]
    for i, ref in enumerate(refs):
        ref[...] = values[i * rows:(i + 1) * rows].astype(ref.dtype)


def mix_kernel(*refs, halves):
    sum_refs, (hidden_ref, norm_ref, mixed_ref, *input_refs) = refs[:2 * halves], refs[2 * halves:]
    mixed = hidden_ref[...].astype(f32) + summed(sum_refs)
    mixed_ref[...] = mixed
    store_halves(mixed * rms_scale(mixed) * norm_ref[...], input_refs)


def mid_kernel(*refs, halves):
    sum_refs, (mixed_ref, norm_ref, out_ref, grad_ref, gain_ref, *low_refs) = refs[:2 * halves], refs[2 * halves:]
    mixed = mixed_ref[...]
    scale = rms_scale(mixed)
    normed = mixed * scale
    back = summed(sum_refs)
    gain_ref[...] = jnp.sum(back * normed, axis=0, keepdims=True)
    grad = out_ref[...].astype(f32) + norm_back(back * norm_ref[...], normed, scale)
    grad_ref[...] = grad
    store_halves(grad, low_refs)


def last_kernel(*refs, halves):
    sum_refs, (grad_ref, hidden_ref, norm_ref, out_ref) = refs[:2 * halves], refs[2 * halves:]
    hidden = hidden_ref[...].astype(f32)
    scale = rms_scale(hidden)
    out_ref[...] = grad_ref[...] + norm_back(summed(sum_refs) * norm_ref[...], hidden * scale, scale)


def result_kernel(*refs):
    *sum_refs, mixed_ref, out_ref = refs
    total = sum_refs[0][...].astype(f32)
    for sum_ref in sum_refs[1:]:
        total = total + sum_ref[...].astype(f32)
    out_ref[...] = (mixed_ref[...] + total).astype(bf16)


def mark_kernel(out_ref):
    out_ref[...] = jnp.zeros_like(out_ref)


def split_kernel(x_ref, *out_refs):
    at = 0
    for out_ref in out_refs[:-1]:
        out_ref[...] = x_ref[:, at:at + out_ref.shape[1]].astype(f32)
        at += out_ref.shape[1]
    out_refs[-1][...] = x_ref[:, at:].astype(f32).T


def split_columns(x, cols, name):
    rows = x.shape[0]
    shapes = [((rows, c), f32) for c in cols[:-1]] + [((cols[-1], rows), f32)]
    return simple_call(split_kernel, [x], shapes, name)


def ffn_kernel(gate_ref, up_ref, down_ref, *refs, parts, held):
    x_refs, g_refs, refs = refs[:parts], refs[parts:2 * parts], refs[2 * parts + held:]
    grad_ref, x_ref, go_ref, *back_refs, back_ref = refs
    tile = pl.program_id(0)
    tok, size = x_refs[0].shape[0], gate_ref.shape[1]
    ff = grad_ref.shape[1] // 3

    @pl.when(tile == 0)
    def _():
        for i in range(parts):
            x_ref[i * tok:(i + 1) * tok] = x_refs[i][...]
            go_ref[i * tok:(i + 1) * tok] = g_refs[i][...]
        back_ref[...] = jnp.zeros_like(back_ref)

    x = x_ref[...]
    gate_pre = mm(x, gate_ref[...])
    up_value = mm(x, up_ref[...])
    grad_act = mm(go_ref[...], down_ref[...])
    sigmoid_gate = jax.nn.sigmoid(gate_pre)
    gated = gate_pre * sigmoid_gate
    grad_gate_pre = (
        grad_act * up_value * sigmoid_gate * (1.0 + gate_pre * (1.0 - sigmoid_gate))
    ).astype(bf16)
    grad_up_value = (grad_act * gated).astype(bf16)
    for i, values in enumerate([grad_gate_pre, grad_up_value, (gated * up_value).astype(bf16)]):
        grad_ref[:, pl.ds(pl.multiple_of(i * ff + tile * size, size), size)] = values
    back_ref[...] += mm_nt(grad_gate_pre, gate_ref[...]) + mm_nt(grad_up_value, up_ref[...])

    @pl.when(tile == pl.num_programs(0) - 1)
    def _():
        store_halves(back_ref[...], back_refs)


def feed_forward(inputs, grads, w_ffn, held, chunk, chunks):
    parts = len(inputs)
    tok, width = inputs[0].shape
    ff = w_ffn.shape[1] // 3
    size = next(s for s in (512, 384, 256, 128) if ff % s == 0)
    tiles = ff // size
    part_spec = pl.BlockSpec((tok, width), lambda t: (0, 0))

    def rows_spec(cols):
        return pl.BlockSpec((parts * tok, cols), lambda t: (chunk, 0))

    rows = parts * tok * chunks
    return pl.pallas_call(
        functools.partial(ffn_kernel, parts=parts, held=len(held)),
        grid=(tiles,),
        in_specs=[
            pl.BlockSpec((width, size), lambda t: (0, t)),
            pl.BlockSpec((width, size), lambda t: (0, tiles + t)),
            pl.BlockSpec((width, size), lambda t: (0, 2 * tiles + t)),
        ]
        + [part_spec] * (2 * parts)
        + [pl.BlockSpec(memory_space=pl.ANY)] * len(held),
        out_specs=[rows_spec(3 * ff), rows_spec(width), rows_spec(width)] + [part_spec] * parts,
        out_shape=[
            jax.ShapeDtypeStruct((rows, 3 * ff), bf16),
            jax.ShapeDtypeStruct((rows, width), bf16),
            jax.ShapeDtypeStruct((rows, width), bf16),
        ]
        + [jax.ShapeDtypeStruct((tok, width), bf16)] * parts,
        scratch_shapes=[pltpu.VMEM((parts * tok, width), f32)],
        input_output_aliases={3 + 2 * parts + i: i for i in range(len(held))},
        cost_estimate=light_cost,
        name="feed_forward",
    )(w_ffn, w_ffn, w_ffn, *inputs, *grads, *held)


def weight_grads_kernel(*refs, turns):
    *left_refs, right_ref, out_ref, turned_ref = refs
    tile = pl.program_id(0)
    for left_ref, at in zip(left_refs, turns):
        @pl.when(tile == at)
        def _(left_ref=left_ref):
            turned_ref[...] = left_ref[...].T

    rows = min(256, out_ref.shape[0])
    for first in range(0, out_ref.shape[0], rows):
        lines = slice(first, first + rows)
        out_ref[lines] = mm(turned_ref[lines], right_ref[...]).astype(bf16)


def weight_grads(lefts, right, starts, after, name):
    tokens, width = lefts[0].shape
    cols = right.shape[1]
    size = next(s for s in (512, 384, 256, 128) if all(at % s == 0 for at in (cols, *starts)))
    whole = pl.BlockSpec((tokens, width), lambda t: (0, 0))
    return pl.pallas_call(
        ignoring(functools.partial(weight_grads_kernel, turns=[at // size for at in starts]), len(lefts) + 1, len(after)),
        grid=(cols // size,),
        in_specs=[whole] * len(lefts) + [pl.BlockSpec((tokens, size), lambda t: (0, t))] + [any_place] * len(after),
        out_specs=pl.BlockSpec((width, size), lambda t: (0, t)),
        out_shape=jax.ShapeDtypeStruct((width, cols), bf16),
        scratch_shapes=[pltpu.VMEM((width, tokens), bf16)],
        cost_estimate=light_cost,
        name=name,
    )(*lefts, right, *after)


def slot_product_kernel(x_ref, w_ref, *out_refs):
    tok = out_refs[0].shape[0]
    total = mm_nt(x_ref[...], w_ref[...])
    for slot, out_ref in enumerate(out_refs):
        out_ref[...] = total[slot * tok:(slot + 1) * tok].astype(bf16)


def slot_product(x, x_block, w, w_block, depth, slots, after, name):
    rows, width = x.shape[0], w.shape[0]
    tile = min(1024, width)
    out_spec = pl.BlockSpec((rows // slots, tile), lambda t: (0, t))
    return pl.pallas_call(
        ignoring(slot_product_kernel, 2, len(after)),
        grid=(width // tile,),
        in_specs=[
            pl.BlockSpec((rows, depth), lambda t: (0, x_block)),
            pl.BlockSpec((tile, depth), lambda t: (t, w_block)),
        ]
        + [any_place] * len(after),
        out_specs=[out_spec] * slots,
        out_shape=[jax.ShapeDtypeStruct((rows // slots, width), bf16)] * slots,
        cost_estimate=light_cost,
        name=name,
    )(x, w, *after)


def more_grads_kernel(left_ref, *refs, rights):
    right_refs, out_ref, turned_ref = refs[:rights], refs[-2], refs[-1]
    tile = pl.program_id(0)

    @pl.when(tile == 0)
    def _():
        turned_ref[...] = left_ref[...].T

    def run(right_ref):
        rows = min(256, out_ref.shape[0])
        for first in range(0, out_ref.shape[0], rows):
            lines = slice(first, first + rows)
            out_ref[lines] = mm(turned_ref[lines], right_ref[...]).astype(bf16)

    for i, right_ref in enumerate(right_refs):
        pl.when(tile == i)(functools.partial(run, right_ref))


def more_grads(left, rights, held, at, blocks, after, name):
    tokens, width = left.shape
    size = rights[0].shape[1]
    return pl.pallas_call(
        ignoring(functools.partial(more_grads_kernel, rights=len(rights)), 1 + len(rights), len(held) + len(after)),
        grid=(len(rights),),
        in_specs=[pl.BlockSpec((tokens, width), lambda t: (0, 0))]
        + [pl.BlockSpec((tokens, size), lambda t: (0, 0))] * len(rights)
        + [any_place] * (len(held) + len(after)),
        out_specs=pl.BlockSpec((width, size), lambda t: (0, at + t)),
        out_shape=jax.ShapeDtypeStruct((width, blocks * size), bf16),
        scratch_shapes=[pltpu.VMEM((width, tokens), bf16)],
        input_output_aliases={1 + len(rights) + i: 0 for i in range(len(held))},
        cost_estimate=light_cost,
        name=name,
    )(left, *rights, *held, *after)


def fold_kernel(near_ref, got_ref, *out_refs):
    rows = out_refs[0].shape[0]
    for i, out_ref in enumerate(out_refs):
        lines = slice((i + 1) * rows, (i + 2) * rows)
        out_ref[...] = (near_ref[lines].astype(f32) + got_ref[lines].astype(f32)).astype(bf16)


def fold_blocks(near, got, count, after):
    vmem = pl.BlockSpec(memory_space=pltpu.VMEM)
    shape = jax.ShapeDtypeStruct((near.shape[0] // count, near.shape[1]), bf16)
    return pl.pallas_call(
        ignoring(fold_kernel, 2, len(after)),
        in_specs=[vmem, vmem] + [any_place] * len(after),
        out_specs=[vmem] * (count - 1),
        out_shape=[shape] * (count - 1),
        cost_estimate=light_cost,
        name="fold_blocks",
    )(near, got, *after)


def body(
    hidden_in,
    doc_lengths,
    attn_norm,
    query_weight,
    key_weight,
    value_weight,
    query_gain,
    key_gain,
    output_weight,
    ffn_norm,
    gate_weight,
    up_weight,
    down_weight,
    grad_out,
):
    dp_count = lax.axis_size("dp")
    mp_count = lax.axis_size("mp")
    slots = mp_count
    tok, width = hidden_in.shape
    group_rows = tok * mp_count
    head_dim = query_gain.shape[0]
    half_dim = head_dim // 2
    q_cols = query_weight.shape[1]
    k_cols = key_weight.shape[1]
    kv_local = k_cols // head_dim
    repeat = q_cols // k_cols
    ff = gate_weight.shape[1]
    group = lax.axis_index("dp")
    my_z = lax.axis_index("mp")
    score_scale = head_dim ** (-0.5)
    ring = [(i, (i + 1) % mp_count) for i in range(mp_count)]
    near_masks = list(range(0, dp_count, 2))
    masks = near_masks + [mask + 1 for mask in near_masks]
    far_masks = near_masks[1:]

    def tie(value, *others):
        return lax.optimization_barrier((value,) + others)[0]

    def shift(values):
        return lax.ppermute(values, "mp", ring)

    def swap(values, mask):
        return lax.ppermute(values, "dp", [(i, i ^ mask) for i in range(dp_count)])

    reach = (min(longest, group_rows * dp_count) - 2) // group_rows + 1

    def needs(reader, owner):
        first = reader // 2 * 2
        return owner <= first + 1 and owner >= first - reach

    def swap_forward(values, mask):
        pairs = [(i, i ^ mask) for i in range(dp_count) if needs(i ^ mask, i)]
        return lax.ppermute(values, "dp", pairs)

    def swap_back(values, mask):
        pairs = [(i, i ^ mask) for i in range(dp_count) if needs(i, i ^ mask)]
        return lax.ppermute(values, "dp", pairs)

    half = dp_count // 2
    halves = 2
    part_rows = tok // halves
    ids = jnp.array(masks, jnp.int32)
    mask_blocks = group ^ ids
    attn_norm = attn_norm.reshape(1, width)
    ffn_norm = ffn_norm.reshape(1, width)
    part_shape = ((part_rows, width), bf16)

    def tie_all(values, *others):
        return list(lax.optimization_barrier((*values, *others)))[:len(values)]

    def order(values, others):
        both = lax.optimization_barrier((*values, *others))
        return list(both[:len(values)]), list(both[len(values):])

    def mark(*operands):
        (tiny,) = simple_call(mark_kernel, [], [((8, 128), f32)], "mark", operands)
        return [swap(tiny, 1)]

    def flat(slot_lists):
        return [part for slot in slot_lists for part in slot]

    def by_slot(parts):
        return [list(parts[i:i + halves]) for i in range(0, len(parts), halves)]

    def shift_all(parts):
        return [shift(part) for part in parts]

    def ring_add(came, own):
        return [shift(add_rounded(one, other)) for one, other in zip(came, own)]

    w_attn_own = jnp.concatenate([query_weight, key_weight, value_weight, output_weight.T], axis=1)
    w_ffn_own = jnp.concatenate([gate_weight, up_weight, down_weight.T], axis=1)
    w_attn = lax.all_gather(w_attn_own, "dp", axis=0, tiled=True)
    w_ffn = tie(lax.all_gather(w_ffn_own, "dp", axis=0, tiled=True), w_attn)

    doc_ends = jnp.cumsum(doc_lengths)
    slot_offset = ((my_z - jnp.arange(slots, dtype=jnp.int32)) % mp_count) * tok
    places = (
        group * group_rows
        + slot_offset[:, None]
        + jnp.arange(tok, dtype=jnp.int32)[None, :]
    )
    before = doc_ends[None, None, :] <= places[:, :, None]
    starts = jnp.sum(jnp.where(before, doc_lengths[None, None, :], 0), axis=-1)
    position = (places - starts).reshape(group_rows)
    inverse = rope_base ** (-(2.0 * jnp.arange(half_dim, dtype=f32)) / head_dim)
    angles = position.astype(f32)[:, None] * inverse[None, :]
    cos_table, sin_table = jnp.cos(angles), jnp.sin(angles)
    cos_table = jnp.concatenate([cos_table, cos_table], axis=1)
    sin_table = jnp.concatenate([-sin_table, sin_table], axis=1)

    sub = min(4, slots)
    key_base = mask_blocks[:, None] * group_rows + slot_offset[None, :]
    blocks = dp_count * slots // sub
    key_base = key_base.reshape(blocks, sub)
    q_first, q_last = places[:, 0], places[:, -1]
    s_first, s_last = starts[:, 0], starts[:, -1]
    piece_lo, piece_hi = key_base[None], key_base[None] + tok - 1
    some = (piece_lo <= q_last[:, None, None]) & (s_first[:, None, None] <= piece_hi)
    every = (piece_hi <= q_first[:, None, None]) & (s_last[:, None, None] <= piece_lo)
    flags = jnp.where(jnp.all(every, -1), 2, jnp.any(some, -1).astype(jnp.int32)).astype(jnp.int32)
    flags = jnp.where(jnp.all(flags == 2, axis=0), 2, jnp.any(flags > 0, axis=0).astype(jnp.int32))
    key_base = key_base.reshape(-1)
    lane_places = jnp.tile(jnp.stack([starts, places]), (1, 1, repeat)).reshape(2, -1)
    row_places = lane_places.T

    hidden_slots = [[hidden_in[i * part_rows:(i + 1) * part_rows] for i in range(halves)]]
    for slot in range(1, slots):
        came = shift_all(hidden_slots[-1])
        if slot == 1:
            came = tie_all(came, cos_table, sin_table, lane_places, w_ffn_own)
        hidden_slots.append(came)
    q_gain, k_gain = query_gain.reshape(1, head_dim), key_gain.reshape(1, head_dim)
    attn_input, row_scales, key_raw, kv_own = project_kv(
        flat(hidden_slots), attn_norm, w_attn, cos_table, sin_table, k_gain, repeat, k_cols
    )
    kv_came = [swap_forward(kv_own, mask) for mask in far_masks]
    grad_slots = [tie_all([grad_out[i * part_rows:(i + 1) * part_rows] for i in range(halves)], *hidden_slots[-1])]
    grad_slots.append(tie_all(shift_all(grad_slots[-1]), kv_own))
    query_raw, query_rot = project_q(
        tie(attn_input, kv_own, *grad_slots[-1]), w_attn, cos_table, sin_table, q_gain, q_cols, k_cols,
        score_scale * log2_e, [flags, key_base, row_places],
    )
    (query_rot,), grad_slots[-1] = order([query_rot], grad_slots[-1])
    for slot in range(2, slots):
        came = shift_all(grad_slots[-1])
        if slot == 2:
            came = tie_all(came, query_rot)
            kv_came = tie_all(kv_came, *came)
        grad_slots.append(came)
    kv_near = [kv_own] + tie_all(kv_came, query_rot)
    kv_pieces = kv_near + [swap(piece, 1) for piece in kv_near]

    keys_total = dp_count * group_rows
    head_rows = repeat * tok
    smem = pl.BlockSpec(memory_space=pltpu.SMEM)
    any_spec = pl.BlockSpec(memory_space=pl.ANY)
    all_rows = slots * head_rows
    lane_spec = pl.BlockSpec((2, all_rows), lambda h: (0, 0))
    row_spec = pl.BlockSpec((all_rows, 2), lambda h: (0, 0))
    q_spec = pl.BlockSpec((group_rows, repeat * head_dim), lambda h: (0, h))
    lse_spec = pl.BlockSpec((None, 1, all_rows), lambda h: (h, 0, 0))
    dims = dict(
        tok=tok, sub=sub, slots=slots, blocks=blocks, pieces=dp_count, repeat=repeat, head_dim=head_dim
    )
    kv_scratch = pltpu.VMEM((keys_total, 2 * k_cols), bf16)
    attended_low, lse = pl.pallas_call(
        functools.partial(attn_fwd_kernel, **dims),
        grid=(kv_local,),
        in_specs=[smem, smem, row_spec, q_spec] + [any_spec] * dp_count,
        out_specs=[q_spec, lse_spec],
        out_shape=[
            jax.ShapeDtypeStruct((group_rows, q_cols), bf16),
            jax.ShapeDtypeStruct((kv_local, 1, all_rows), f32),
        ],
        scratch_shapes=[
            kv_scratch,
            pltpu.VMEM((all_rows, 2 * head_dim), f32),
            pltpu.VMEM((tok * sub, 2 * head_dim), bf16),
            pltpu.VMEM((all_rows, head_dim), bf16),
            pltpu.SemaphoreType.DMA((dp_count,)),
        ],
        cost_estimate=light_cost,
        name="attn_fwd",
    )(flags, key_base, row_places, query_rot, *kv_pieces)

    grad_slots[slots - 1] = tie_all(grad_slots[slots - 1], attended_low)
    parts = by_slot(slot_product(attended_low, 0, w_attn, 2 * k_cols // q_cols + 1, q_cols, slots * halves, [], "attn_out"))
    came = shift_all(tie_all(parts[1], *grad_slots[-1]))
    for slot in range(2, slots):
        came = ring_add(came, parts[slot])
    mixed_rows, *ffn_input = simple_call(
        functools.partial(mix_kernel, halves=halves),
        [*came, *parts[0], hidden_in, ffn_norm],
        [((tok, width), f32)] + [part_shape] * halves,
        "mix",
    )

    ffn_slots = [ffn_input, shift_all(ffn_input)]
    held, parts = [], []
    for first in range(0, slots, 2):
        *held, = feed_forward(
            flat(ffn_slots[first:first + 2]), flat(grad_slots[first:first + 2]), w_ffn, held, first // 2, slots // 2
        )
        held, back = held[:3], held[3:]
        parts += by_slot(back)
        if first + 2 < slots:
            ffn_slots.append(tie_all(shift_all(ffn_slots[-1]), *back))
            ffn_slots.append(shift_all(ffn_slots[-1]))
    ffn_right, ffn_all, grad_all = held

    came = shift_all(tie_all(parts[1], *ffn_slots[-1]))
    ffn_part = weight_grads([ffn_all, grad_all], tie(ffn_right, *came), [0, 2 * ff], [], "ffn_grads")
    for slot in range(2, slots):
        came = ring_add(came, parts[slot])
        if slot == 2:
            came = tie_all(came, ffn_part)
    grad_ffn = lax.psum_scatter(ffn_part, "dp", scatter_dimension=0, tiled=True)
    grad_mixed, grad_ffn_norm, *mid_first = simple_call(
        functools.partial(mid_kernel, halves=halves),
        [*came, *parts[0], mixed_rows, ffn_norm, grad_out],
        [((tok, width), f32), ((1, width), f32)] + [part_shape] * halves,
        "mid",
    )
    mid_slots = [mid_first]
    result_parts = slot_product(ffn_right, 2, w_ffn, 2, ff, slots, [], "ffn_out")
    for slot in range(1, slots):
        came = shift_all(mid_slots[-1])
        if slot == 1:
            came[1:], result_parts = order(came[1:], result_parts)
        mid_slots.append(came)

    result_came = [
        lax.ppermute(result_parts[slot], "mp", [(i, (i - slot) % mp_count) for i in range(mp_count)])
        for slot in range(1, slots)
    ]

    grad_mid, grad_attended = grad_attended_product(flat(mid_slots), w_attn, q_cols, [])
    near_spec = pl.BlockSpec((keys_total // 2, 2 * k_cols), lambda h: (0, 0))
    near_shape = jax.ShapeDtypeStruct((keys_total // 2, 2 * k_cols), bf16)
    dq_rot, dkv_near, dkv_far = pl.pallas_call(
        functools.partial(
            attn_bwd_kernel, **dims, dq_scale=score_scale, dk_scale=1.0 / log2_e
        ),
        grid=(kv_local,),
        in_specs=[smem, smem, lane_spec, q_spec, lse_spec, q_spec, q_spec] + [any_spec] * dp_count,
        out_specs=[q_spec, near_spec, near_spec],
        out_shape=[jax.ShapeDtypeStruct((group_rows, q_cols), f32), near_shape, near_shape],
        scratch_shapes=[
            kv_scratch,
            pltpu.VMEM((all_rows, head_dim), bf16),
            pltpu.VMEM((all_rows, head_dim), bf16),
            pltpu.VMEM((head_dim, all_rows), f32),
            pltpu.VMEM((1, all_rows), f32),
            pltpu.VMEM((tok * sub, head_dim), f32),
            pltpu.VMEM((tok * sub, head_dim), f32),
            pltpu.SemaphoreType.DMA((dp_count,)),
        ],
        cost_estimate=light_cost,
        name="attn_bwd",
    )(flags, key_base, lane_places, query_rot, lse, attended_low, grad_attended, *kv_pieces)

    dkv_got = swap(dkv_far, 1)
    dkv_sent = fold_blocks(dkv_near, dkv_got, half, [])
    dkv_came = [swap_back(sent, mask) for sent, mask in zip(dkv_sent, far_masks)]
    marked = mark(*dkv_sent)
    dq_raw, query_gain_part = unproject(query_raw, cos_table, sin_table, q_gain, [dq_rot], marked, "unproject_q")
    attn_part = more_grads(grad_mid, [attended_low], [], 2, 3, marked, "out_grads")
    attn_part = more_grads(attn_input, [dq_raw], [attn_part], 0, 3, [], "q_grads")
    dkv_raw, key_gain_part = unproject(
        key_raw, cos_table, sin_table, k_gain, [dkv_near, dkv_got] + dkv_came, [attn_part, *result_came], "unproject_kv"
    )

    attn_part = more_grads(attn_input, [dkv_raw], [attn_part], 1, 3, [grad_ffn], "kv_grads")
    grad_attn = lax.psum_scatter(attn_part, "dp", scatter_dimension=0, tiled=True)
    *parts, attn_gain_part = attn_back_product(
        dq_raw, dkv_raw, w_attn, row_scales, flat(hidden_slots), [attn_part]
    )
    parts = by_slot(parts)
    came = shift_all(parts[1])
    came, (attn_gain_part,) = order(came, [attn_gain_part])
    small = jnp.concatenate(
        [attn_gain_part[0], grad_ffn_norm[0], query_gain_part[0], key_gain_part[0]]
    ).reshape(-1, head_dim)
    small = small + swap(small, 1)
    for slot in range(2, slots):
        came = ring_add(came, parts[slot])
        if slot == 2:
            grads = split_columns(grad_ffn, [ff, ff, ff], "split_ffn")
            came, (small, grad_gate, grad_up, grad_down) = order(came, [small, *grads])
            small = small + sum(swap(small, mask) for mask in far_masks)
    came, (small,) = order(came, [small])
    turns = [[(i, (i + by) % mp_count) for i in range(mp_count)] for by in range(1, mp_count)]
    small = small + sum(lax.ppermute(small, "mp", turn) for turn in turns)
    (grad_hidden,) = simple_call(
        functools.partial(last_kernel, halves=halves),
        [*came, *parts[0], grad_mixed, hidden_in, attn_norm],
        [((tok, width), f32)],
        "last",
    )
    (result,) = simple_call(
        result_kernel, [result_parts[0], *result_came, mixed_rows], [((tok, width), bf16)], "result"
    )
    grad_query, grad_key, grad_value, grad_out_weight = split_columns(
        grad_attn, [q_cols, k_cols, k_cols, q_cols], "split_attn"
    )

    small = small.reshape(-1)
    return (
        result,
        grad_hidden,
        small[:width],
        grad_query,
        grad_key,
        grad_value,
        small[2 * width:2 * width + head_dim],
        small[2 * width + head_dim:],
        grad_out_weight,
        small[width:2 * width],
        grad_gate,
        grad_up,
        grad_down,
    )


def solution(mesh):
    rows = P(("dp", "mp"), None)
    placed = (
        rows,
        P(),
        P(),
        P("dp", "mp"),
        P("dp", "mp"),
        P("dp", "mp"),
        P(),
        P(),
        P("mp", "dp"),
        P(),
        P("dp", "mp"),
        P("dp", "mp"),
        P("mp", "dp"),
        rows,
    )
    return jax.shard_map(
        body,
        mesh=mesh,
        in_specs=placed,
        out_specs=(
            rows,
            rows,
            P(),
            P("dp", "mp"),
            P("dp", "mp"),
            P("dp", "mp"),
            P(),
            P(),
            P("mp", "dp"),
            P(),
            P("dp", "mp"),
            P("dp", "mp"),
            P("mp", "dp"),
        ),
        check_vma=False,
    )
```
